32 devices in a mesh: fsdp: 8 (over z, y), ctx: 4 (over x, core).
Axes of the slice: x: 2, y: 2, z: 4, core: 2. Of those that a mesh axis runs over, the one named last changes fastest.
Arguments:
- hidden: bfloat16 [8, 1024, 8192], P('fsdp', 'ctx'), may hold values from -400 to 400
- norm_gain: bfloat16 [8192], replicated, may hold values from 0.099609375 to 1.8984375
- w_query: bfloat16 [8192, 1024], P('fsdp'), may hold values from -0.109375 to 0.109375
- w_key: bfloat16 [8192, 128], P('fsdp'), may hold values from -0.109375 to 0.109375
- w_value: bfloat16 [8192, 128], P('fsdp'), may hold values from -0.0625 to 0.0625
- bias_query: bfloat16 [1024], replicated, may hold values from -24 to 24
- bias_key: bfloat16 [128], replicated, may hold values from -9 to 9
- bias_value: bfloat16 [128], replicated, may hold values from -3 to 3
Outputs:
- attended: bfloat16 [8, 1024, 1024], P('fsdp', 'ctx')
The draws below stay inside these ranges and needn't reach their ends.
All inputs are finite; a program needn't handle non-finite values.
Results may differ from the reference program's by a relative error of at most 0.012.
Values may be sent and summed in bfloat16 or wider, within the bound.
No kernel may reach another device: no remote copies, remote signals or barrier semaphores. Data moves between devices by JAX's collectives and lax.ppermute only.
A program may use at most 128 MiB of HBM per device.

```python
import math
import jax
import jax.numpy as jnp
from jax import lax

D = 8192
HD = 128
HQ = 8
QW = 1024
SEQ = 1024
PROMPTS = 8


def draw_hidden(key, part):
    entry_key, row_key, column_key = jax.random.split(key, 3)
    entries = jnp.clip(jax.random.normal(entry_key, (PROMPTS, SEQ, D), jnp.float32), -4.0, 4.0)
    row_scale = jnp.exp(jax.random.uniform(row_key, (PROMPTS, SEQ, 1), jnp.float32, 0.0, math.log(10.0)))
    column_scale = jnp.exp(jax.random.uniform(column_key, (1, 1, D), jnp.float32, 0.0, math.log(10.0)))
    return (entries * row_scale * column_scale).astype(jnp.bfloat16)


def bias_parts(key):
    shared_key = jax.random.fold_in(key, 7)
    vector_key, head_key, noise_key = jax.random.split(shared_key, 3)
    shared_vector = jnp.clip(jax.random.normal(vector_key, (HD,), jnp.float32), -3.0, 3.0)
    noise = jnp.clip(jax.random.normal(noise_key, (HQ, HD), jnp.float32), -3.0, 3.0)
    head_scale = jax.random.uniform(head_key, (HQ, 1), jnp.float32, 0.3, 0.7)
    key_scale = 0.5
    return (shared_vector, head_scale, noise, key_scale)


def draw_bias_query(key, part):
    shared_vector, head_scale, noise, key_scale = bias_parts(key)
    return (head_scale * shared_vector[None, :] + 0.5 * noise).reshape(HQ * HD).astype(jnp.bfloat16)


def draw_bias_key(key, part):
    shared_vector, head_scale, noise, key_scale = bias_parts(key)
    return (key_scale * shared_vector).astype(jnp.bfloat16)


def block_scale(own_key, shape, cuts, low, high):
    def one(axis_at, blocks):
        draws = jax.random.uniform(jax.random.fold_in(jax.random.fold_in(own_key, 6), axis_at), (blocks,), jnp.float32, low / len(cuts), high / len(cuts))
        return jnp.repeat(jnp.exp(draws), shape[axis_at] // blocks).reshape((-1,) + (1,) * (len(shape) - axis_at - 1))

    factor_of = one(*cuts[0])
    for cut in cuts[1:]:
        factor_of = factor_of * one(*cut)
    return factor_of


def centred(key, extent, width, reach, cuts=(), held_as=jnp.bfloat16):
    gain = block_scale(key, extent, cuts, -0.22, 0.18) if cuts else 1.0
    values = jax.random.normal(key, extent, jnp.float32) * width * gain
    return jnp.minimum(jnp.maximum(values, -reach), reach).astype(held_as)


def setup_inputs(seed: int = 0) -> dict:
    key_list = jax.random.split(jax.random.key(seed), 9)
    hidden = draw_hidden(jax.random.fold_in(key_list[8], 71), 0)
    norm_gain = jnp.clip(1.0 + 0.18 * jax.random.normal(key_list[1], (D,), jnp.float32), 0.099609375, 1.8984375).astype(jnp.bfloat16)
    w_query = centred(key_list[2], (D, QW), (2 * D // 5) ** -0.5, 0.109375, ((0, 8),))
    w_key = centred(key_list[3], (D, HD), (2 * D // 5) ** -0.5, 0.109375, ((0, 8),))
    w_value = centred(key_list[4], (D, HD), D ** -0.5, 0.0625, ((0, 8),))
    bias_query = draw_bias_query(jax.random.fold_in(key_list[8], 71), 0)
    bias_key = draw_bias_key(jax.random.fold_in(key_list[8], 71), 0)
    bias_value = centred(key_list[7], (HD,), 0.5, 3.0)
    return {"hidden": hidden, "norm_gain": norm_gain, "w_query": w_query, "w_key": w_key, "w_value": w_value, "bias_query": bias_query, "bias_key": bias_key, "bias_value": bias_value}


epsilon = 1e-06
rotary_base = 1000000.0
masked_score = -1e+30

def rotary_tables(positions, head_width):
    half_width = head_width // 2
    frequency = jnp.exp(-(jnp.arange(half_width, dtype=jnp.float32) * (2.0 / head_width)) * math.log(rotary_base))
    angles = positions.astype(jnp.float32)[:, None] * frequency[None, :]
    return (jnp.cos(angles)[:, None, :], jnp.sin(angles)[:, None, :])

def rotate(tensor, cosine, sine_table):
    half_width = tensor.shape[-1] // 2
    lower_half = tensor[..., :half_width]
    upper_half = tensor[..., half_width:]
    return jnp.concatenate([lower_half * cosine - upper_half * sine_table, upper_half * cosine + lower_half * sine_table], axis=-1)

def normalize(inputs, norm_gain):
    floats = inputs.astype(jnp.float32)
    scaled = floats * lax.rsqrt(lax.optimization_barrier(jnp.mean(floats * floats, axis=-1, keepdims=True)) + epsilon)
    return (scaled * norm_gain.astype(jnp.float32)).astype(jnp.bfloat16)

def reference(hidden, norm_gain, w_query, w_key, w_value, bias_query, bias_key, bias_value):
    score_scale = HD ** (-0.5)
    block_rows = math.gcd(SEQ, 512)
    block_count = SEQ // block_rows
    positions = jnp.arange(SEQ, dtype=jnp.int32)
    cosine, sine_table = rotary_tables(positions, HD)

    def one_prompt(prompt):
        normed = normalize(prompt, norm_gain)
        query_sums = jnp.dot(normed, w_query, preferred_element_type=jnp.float32) + bias_query.astype(jnp.float32)
        key_sums = jnp.dot(normed, w_key, preferred_element_type=jnp.float32) + bias_key.astype(jnp.float32)
        value_sums = jnp.dot(normed, w_value, preferred_element_type=jnp.float32) + bias_value.astype(jnp.float32)
        queries = rotate(query_sums.reshape(SEQ, HQ, HD), cosine, sine_table).astype(jnp.bfloat16)
        keys = rotate(key_sums[:, None, :], cosine, sine_table)[:, 0, :].astype(jnp.bfloat16)
        values = value_sums.astype(jnp.bfloat16)
        keys_wide = keys.astype(jnp.float32)
        values_wide = values.astype(jnp.float32)
        query_blocks = queries.reshape(block_count, block_rows, HQ, HD)

        def one_block(inputs):
            query_block, offset = inputs
            scores = jnp.einsum('qhd,kd->hqk', query_block.astype(jnp.float32), keys_wide) * score_scale
            row_ids = offset + jnp.arange(block_rows, dtype=jnp.int32)
            column_ids = jnp.arange(SEQ, dtype=jnp.int32)
            visible = column_ids[None, :] <= row_ids[:, None]
            scores = jnp.where(visible[None], scores, masked_score)
            row_peak = lax.optimization_barrier(jnp.max(scores, axis=-1, keepdims=True))
            expsum = jnp.exp(scores - row_peak)
            row_total = lax.optimization_barrier(jnp.sum(expsum, axis=-1))
            weights = expsum.astype(jnp.bfloat16)
            mixed = jnp.einsum('hqk,kd->hqd', weights.astype(jnp.float32), values_wide)
            result = mixed / row_total[..., None]
            return result.transpose(1, 0, 2).reshape(block_rows, HQ * HD).astype(jnp.bfloat16)
        offsets = jnp.arange(block_count, dtype=jnp.int32) * block_rows
        outputs = lax.map(one_block, (query_blocks, offsets))
        return outputs.reshape(SEQ, HQ * HD)
    return lax.map(one_prompt, hidden)
```

```python
import math

import jax
import jax.numpy as jnp
from jax import lax
from jax.sharding import Mesh, PartitionSpec as P

epsilon = 1e-06
rotary_base = 1000000.0
masked_score = -1e30


def shifted(value, axis, steps):
    count = lax.axis_size(axis)
    first, last = (max(0, -steps), min(count, count - steps))
    return lax.ppermute(value, axis, [(source, source + steps) for source in range(first, last)])


def rotary_tables(positions, head_width):
    half_width = head_width // 2
    frequency = jnp.exp(
        -(jnp.arange(half_width, dtype=jnp.float32) * (2.0 / head_width)) * math.log(rotary_base)
    )
    angles = positions.astype(jnp.float32)[:, None] * frequency[None, :]
    return (jnp.cos(angles)[:, None, :], jnp.sin(angles)[:, None, :])


def rotate(tensor, cosine, sine_table):
    half_width = tensor.shape[-1] // 2
    lower_half = tensor[..., :half_width]
    upper_half = tensor[..., half_width:]
    return jnp.concatenate(
        [
            lower_half * cosine - upper_half * sine_table,
            upper_half * cosine + lower_half * sine_table,
        ],
        axis=-1,
    )


def attend(work_queries, score_scale, running, key_value, visible):
    row_peak, row_total, weighted = running
    scores = (
        jnp.einsum("qhd,kd->hqk", work_queries, key_value[0], preferred_element_type=jnp.float32)
        * score_scale
    )
    scores = jnp.where(visible, scores, masked_score)
    new_peak = jnp.maximum(row_peak, jnp.max(scores, axis=-1))
    factor = jnp.exp(row_peak - new_peak)
    expsum = jnp.exp(scores - new_peak[..., None])
    row_total = row_total * factor + jnp.sum(expsum, axis=-1)
    weights = expsum.astype(jnp.bfloat16)
    weighted = weighted * factor[..., None] + jnp.einsum(
        "hqk,kd->hqd", weights, key_value[1], preferred_element_type=jnp.float32
    )
    return (new_peak, row_total, weighted)


def row_scale(inputs):
    floats = inputs.astype(jnp.float32)
    return lax.rsqrt(jnp.mean(floats * floats, axis=-1, keepdims=True) + epsilon)


def scaled_rows(inputs, scale, gain):
    return (inputs.astype(jnp.float32) * scale * gain.astype(jnp.float32)).astype(jnp.bfloat16)


def project(hidden, norm_gain, w_query, w_key, w_value):
    local_rows, width = hidden.shape
    lines, slabs = (lax.axis_size("line"), lax.axis_size("ctx"))
    depth = w_query.shape[0]
    side = lax.axis_index("pair")
    swap = [(0, 1), (1, 0)]
    split = hidden.reshape(local_rows, lines, 2, depth)
    half_width = lines * depth

    def half(array, which):
        return lax.dynamic_index_in_dim(array, which, array.ndim - 2, keepdims=False)

    sent = half(split, 1 - side).reshape(local_rows, half_width)
    kept = half(split, side).reshape(local_rows, half_width)
    gain = half(norm_gain.reshape(lines, 2, depth), side).reshape(half_width)
    came = lax.ppermute(sent, "pair", swap)
    scale = row_scale(hidden)
    came_scale = lax.ppermute(scale, "pair", swap)
    piece = depth // slabs
    start = lax.axis_index("ctx") * piece
    packed = jnp.concatenate(
        [lax.dynamic_slice_in_dim(w, start, piece, 0) for w in (w_query, w_key, w_value)], axis=1
    )
    weights = lax.all_gather(packed, ("line", "ctx"), axis=0, tiled=True)
    rows = jnp.concatenate(
        [scaled_rows(kept, scale, gain), scaled_rows(came, came_scale, gain)], axis=0
    )
    sums = jnp.dot(rows, weights, preferred_element_type=jnp.float32)
    back = lax.ppermute(sums[local_rows:].astype(jnp.bfloat16), "pair", swap)
    return sums[:local_rows] + back.astype(jnp.float32)


def shards(hidden, norm_gain, w_query, w_key, w_value, bias_query, bias_key, bias_value):
    local_rows = hidden.shape[1]
    head_width = w_key.shape[1]
    query_width = w_query.shape[1]
    query_heads = query_width // head_width
    sums = project(hidden[0], norm_gain, w_query, w_key, w_value)
    query_sums = sums[:, :query_width]
    key_sums = sums[:, query_width : query_width + head_width]
    value_sums = sums[:, query_width + head_width :]
    slab_index = lax.axis_index("ctx")
    slab_count = lax.axis_size("ctx")
    positions = slab_index * local_rows + jnp.arange(local_rows, dtype=jnp.int32)
    cosine, sine_table = rotary_tables(positions, head_width)
    queries = rotate(
        (query_sums + bias_query.astype(jnp.float32)).reshape(local_rows, query_heads, head_width),
        cosine,
        sine_table,
    ).astype(jnp.bfloat16)
    keys = rotate((key_sums + bias_key.astype(jnp.float32))[:, None, :], cosine, sine_table)[
        :, 0, :
    ].astype(jnp.bfloat16)
    values = (value_sums + bias_value.astype(jnp.float32)).astype(jnp.bfloat16)
    score_scale = head_width ** (-0.5)
    start_state = (
        jnp.full((query_heads, local_rows), masked_score, jnp.float32),
        jnp.zeros((query_heads, local_rows), jnp.float32),
        jnp.zeros((query_heads, local_rows, head_width), jnp.float32),
    )
    key_value = jnp.stack([keys, values])
    column_ids = jnp.arange(local_rows, dtype=jnp.int32)
    causal = column_ids[None, :] <= column_ids[:, None]
    running = attend(queries, score_scale, start_state, key_value, causal[None])

    def forward_step(step_number, state):
        held_running, blocks = state
        blocks = shifted(blocks, "ctx", 1)
        visible = step_number <= slab_index
        held_running = attend(queries, score_scale, held_running, blocks, visible)
        return (held_running, blocks)

    running, key_value = lax.fori_loop(1, slab_count, forward_step, (running, key_value))
    row_peak, row_total, weighted = running
    attended = (
        (weighted / row_total[..., None])
        .transpose(1, 0, 2)
        .reshape(local_rows, query_width)
        .astype(jnp.bfloat16)
    )
    return attended[None]


def solution(mesh):
    groups, slabs = (mesh.shape["fsdp"], mesh.shape["ctx"])
    pairs = Mesh(mesh.devices.reshape(groups // 2, 2, slabs), ("line", "pair", "ctx"))
    both = ("line", "pair")
    in_specs = (
        P(both, "ctx", None),
        P(),
        P(both, None),
        P(both, None),
        P(both, None),
        P(),
        P(),
        P(),
    )
    out_specs = P(both, "ctx", None)
    return jax.shard_map(shards, mesh=pairs, in_specs=in_specs, out_specs=out_specs, check_vma=False)
```

```python
import functools
import math

import jax
import jax.numpy as jnp
from jax import lax
from jax.experimental import pallas as pl
from jax.experimental.pallas import tpu as pltpu
from jax.sharding import Mesh, PartitionSpec as P

epsilon = 1e-06
rotary_base = 1000000.0
masked_score = -1e30


def shifted(value, axis, steps):
    count = lax.axis_size(axis)
    first, last = (max(0, -steps), min(count, count - steps))
    return lax.ppermute(value, axis, [(source, source + steps) for source in range(first, last)])


def rotary_tables(positions, head_width):
    half_width = head_width // 2
    frequency = jnp.exp(
        -(jnp.arange(half_width, dtype=jnp.float32) * (2.0 / head_width)) * math.log(rotary_base)
    )
    angles = positions.astype(jnp.float32)[:, None] * frequency[None, :]
    return (jnp.cos(angles)[:, None, :], jnp.sin(angles)[:, None, :])


def rotate(tensor, cosine, sine_table):
    half_width = tensor.shape[-1] // 2
    lower_half = tensor[..., :half_width]
    upper_half = tensor[..., half_width:]
    return jnp.concatenate(
        [
            lower_half * cosine - upper_half * sine_table,
            upper_half * cosine + lower_half * sine_table,
        ],
        axis=-1,
    )


def attend(work_queries, score_scale, running, key_value, visible):
    row_peak, row_total, weighted = running
    scores = (
        jnp.einsum("qhd,kd->hqk", work_queries, key_value[0], preferred_element_type=jnp.float32)
        * score_scale
    )
    scores = jnp.where(visible, scores, masked_score)
    new_peak = jnp.maximum(row_peak, jnp.max(scores, axis=-1))
    factor = jnp.exp(row_peak - new_peak)
    expsum = jnp.exp(scores - new_peak[..., None])
    row_total = row_total * factor + jnp.sum(expsum, axis=-1)
    weights = expsum.astype(jnp.bfloat16)
    weighted = weighted * factor[..., None] + jnp.einsum(
        "hqk,kd->hqd", weights, key_value[1], preferred_element_type=jnp.float32
    )
    return (new_peak, row_total, weighted)


def row_scale(inputs):
    floats = inputs.astype(jnp.float32)
    return lax.rsqrt(jnp.mean(floats * floats, axis=-1, keepdims=True) + epsilon)


def scaled_rows(inputs, scale, gain):
    return (inputs.astype(jnp.float32) * scale * gain.astype(jnp.float32)).astype(jnp.bfloat16)


def project(hidden, norm_gain, w_query, w_key, w_value):
    local_rows, width = hidden.shape
    lines, slabs = (lax.axis_size("line"), lax.axis_size("ctx"))
    depth = w_query.shape[0]
    side = lax.axis_index("pair")
    swap = [(0, 1), (1, 0)]
    split = hidden.reshape(local_rows, lines, 2, depth)
    half_width = lines * depth

    def half(array, which):
        return lax.dynamic_index_in_dim(array, which, array.ndim - 2, keepdims=False)

    sent = half(split, 1 - side).reshape(local_rows, half_width)
    kept = half(split, side).reshape(local_rows, half_width)
    gain = half(norm_gain.reshape(lines, 2, depth), side).reshape(half_width)
    came = lax.ppermute(sent, "pair", swap)
    scale = row_scale(hidden)
    came_scale = lax.ppermute(scale, "pair", swap)
    piece = depth // slabs
    start = lax.axis_index("ctx") * piece
    packed = jnp.concatenate(
        [lax.dynamic_slice_in_dim(w, start, piece, 0) for w in (w_query, w_key, w_value)], axis=1
    )
    weights = lax.all_gather(packed, ("line", "ctx"), axis=0, tiled=True)
    rows = jnp.concatenate(
        [scaled_rows(kept, scale, gain), scaled_rows(came, came_scale, gain)], axis=0
    )
    sums = jnp.dot(rows, weights, preferred_element_type=jnp.float32)
    back = lax.ppermute(sums[local_rows:].astype(jnp.bfloat16), "pair", swap)
    return sums[:local_rows] + back.astype(jnp.float32)


def normed_rows(block, scale, gain):
    return (block.astype(jnp.float32) * scale * gain).astype(jnp.bfloat16)


def slots_body(local, count, piece, order_ref, hidden, came, scale, came_scale, gain, *refs):
    weights = refs[: (3 if local else 0) + 4 * (count - local)]
    refs = refs[len(weights) :]
    if local:
        sums, held, guest, wide, stacked, sems = refs
    else:
        before, sums, back_kv, back_q, held, guest, wide, stacked, total, sems = refs
    rows, depth = held.shape[1:]
    copies = []
    pending = list(weights)
    slab = order_ref[count]
    for slot in range(count):
        column = pl.multiple_of(order_ref[slot] * depth, depth)
        now = [
            (hidden.at[:, pl.ds(column, depth)], held.at[slot]),
            (came.at[:, pl.ds(slot * depth, depth)], guest.at[slot]),
        ]
        if slot < local:
            at = 0
            for _ in range(3):
                weight = pending.pop(0)
                now.append((weight, wide.at[slot, :, pl.ds(at, weight.shape[1])]))
                at += weight.shape[1]
        else:
            for flip in (0, 2, 1, 3):
                row = pl.multiple_of(jnp.bitwise_xor(slab, flip) * piece, piece)
                now.append((pending.pop(0), wide.at[slot, pl.ds(row, piece), :]))
        copies.append(now)
    flights = []
    number = 0
    for now in copies:
        flight = []
        for source, target in now:
            flight.append(pltpu.make_async_copy(source, target, sems.at[number]))
            number += 1
        flights.append(flight)
    for flight in flights:
        for copy in flight:
            copy.start()
    if not local:
        fetch = pltpu.make_async_copy(before, total, sems.at[number])
        fetch.start()
    else:
        total = sums
    width = total.shape[1]
    step = 256
    tiles = list(range(0, width, step))
    for slot in range(count):
        for copy in flights[slot]:
            copy.wait()
        column = pl.multiple_of(order_ref[slot] * depth, depth)
        row_gain = gain[:, pl.ds(column, depth)].astype(jnp.float32)
        stacked[:rows] = normed_rows(held[slot], scale[...], row_gain)
        stacked[rows:] = normed_rows(guest[slot], came_scale[...], row_gain)
        if slot == 0 and not local:
            fetch.wait()
        for at in reversed(tiles):
            cols = pl.ds(at, step)
            product = jnp.dot(
                stacked[...], wide[slot, :, cols], preferred_element_type=jnp.float32
            )
            if slot > 0 or not local:
                product = product + total[:, cols]
            if local or slot < count - 1:
                total[:, cols] = product
            else:
                sums[:, cols] = product[:rows]
                guests = product[rows:].astype(jnp.bfloat16)
                if at == tiles[-1]:
                    back_kv[...] = guests
                else:
                    back_q[:, cols] = guests


def add_slots(local, order, hidden, came, scale, came_scale, gain, weights, before=None):
    rows = hidden.shape[0]
    count = order.shape[0] - 1
    depth = came.shape[1] // count
    piece = depth // 4
    width = weights[-1].shape[1] if not local else sum(w.shape[1] for w in weights[:3])
    anywhere = pl.BlockSpec(memory_space=pl.ANY)
    inside = pl.BlockSpec(memory_space=pltpu.VMEM)
    scratch = [
        pltpu.VMEM((count, rows, depth), jnp.bfloat16),
        pltpu.VMEM((count, rows, depth), jnp.bfloat16),
        pltpu.VMEM((count, depth, width), jnp.bfloat16),
        pltpu.VMEM((2 * rows, depth), jnp.bfloat16),
    ]
    copies = 2 * count + len(weights) + 1
    args = [order, hidden, came, scale, came_scale, gain, *weights]
    in_specs = [pl.BlockSpec(memory_space=pltpu.SMEM), anywhere, anywhere, inside, inside, inside]
    in_specs += [anywhere] * len(weights)
    if local:
        out_shape = jax.ShapeDtypeStruct((2 * rows, width), jnp.float32)
        out_specs = inside
    else:
        args.append(before)
        in_specs.append(anywhere)
        out_shape = (
            jax.ShapeDtypeStruct((rows, width), jnp.float32),
            jax.ShapeDtypeStruct((rows, 256), jnp.bfloat16),
            jax.ShapeDtypeStruct((rows, width - 256), jnp.bfloat16),
        )
        out_specs = (inside, inside, inside)
        scratch.append(pltpu.VMEM((2 * rows, width), jnp.float32))
    scratch.append(pltpu.SemaphoreType.DMA((copies,)))
    flops = 4 * rows * depth * count * width
    moved = 2 * (depth * width * count + 2 * rows * depth * count) + 8 * rows * width
    return pl.pallas_call(
        functools.partial(slots_body, local, count, piece),
        out_shape=out_shape,
        in_specs=in_specs,
        out_specs=out_specs,
        scratch_shapes=scratch,
        cost_estimate=pl.CostEstimate(flops=flops, bytes_accessed=moved, transcendentals=0),
        compiler_params=pltpu.CompilerParams(vmem_limit_bytes=40 * 2**20),
        name="slots_first" if local else "slots_last",
    )(*args)


def turned(tensor, cosine, sine_table):
    half = tensor.shape[-1] // 2
    return tensor * cosine + pltpu.roll(tensor, half, 1) * sine_table


def key_value_body(sums, back, bias, cosine, sine_table, out):
    head = out.shape[1] // 2
    total = sums[...] + back[...].astype(jnp.float32) + bias[...].astype(jnp.float32)
    out[:, :head] = turned(total[:, :head], cosine[...], sine_table[...]).astype(jnp.bfloat16)
    out[:, head:] = total[:, head:].astype(jnp.bfloat16)


def attention_body(scale, slab_ref, sums, back, bias, cosine, sine_table, *refs):
    blocks, (out, keys, values) = (refs[:4], refs[4:])
    rows, width = out.shape
    head = cosine.shape[1]
    slab = slab_ref[0]
    for flip, block in zip((0, 1, 2, 3), blocks):
        row = pl.multiple_of(jnp.bitwise_xor(slab, flip) * rows, rows)
        keys[pl.ds(row, rows), :] = block[:, :head]
        values[pl.ds(row, rows), :] = block[:, head:]
    total_keys = keys.shape[0]
    row_ids = slab * rows + lax.broadcasted_iota(jnp.int32, (rows, total_keys), 0)
    visible = lax.broadcasted_iota(jnp.int32, (rows, total_keys), 1) <= row_ids
    for at in range(0, width, head):
        cols = pl.ds(at, head)
        query = sums[:, cols] + back[:, cols].astype(jnp.float32) + bias[:, cols].astype(jnp.float32)
        query = turned(query, cosine[...], sine_table[...]).astype(jnp.bfloat16)
        scores = lax.dot_general(
            query, keys[...], (((1,), (1,)), ((), ())), preferred_element_type=jnp.float32
        )
        scores = jnp.where(visible, scores * scale, masked_score)
        exps = jnp.exp(scores - jnp.max(scores, axis=1, keepdims=True))
        length = jnp.sum(exps, axis=1, keepdims=True)
        mixed = jnp.dot(exps.astype(jnp.bfloat16), values[...], preferred_element_type=jnp.float32)
        out[:, cols] = (mixed / length).astype(jnp.bfloat16)


def planned(hidden, norm_gain, w_query, w_key, w_value, bias_query, bias_key, bias_value):
    tokens = hidden[0]
    rows = tokens.shape[0]
    depth, query_width = w_query.shape
    head = w_key.shape[1]
    line, side, slab = (lax.axis_index("line"), lax.axis_index("pair"), lax.axis_index("ctx"))
    inner = (line == 1) | (line == 2)
    swap = [(0, 1), (1, 0)]
    ends = [(0, 1), (1, 0), (2, 3), (3, 2)]
    middle = [(1, 2), (2, 1)]
    outward = [(1, 0), (2, 3)]
    across = [(i, i ^ 2) for i in range(4)]
    beside = [(i, i ^ 1) for i in range(4)]
    third = jnp.where(inner, line ^ 3, line ^ 2)
    fourth = jnp.where(inner, line ^ 2, line ^ 3)
    lines = [line, line ^ 1, third, fourth]

    def column_block(which, parity):
        return lax.dynamic_slice_in_dim(tokens, (2 * which + parity) * depth, depth, 1)

    sent_first = jnp.concatenate([column_block(which, 1 - side) for which in lines[:3]], axis=1)
    sent_last = column_block(lines[3], 1 - side)
    came_first = lax.ppermute(sent_first, "pair", swap)
    came_last = lax.ppermute(sent_last, "pair", swap)
    scale = row_scale(tokens)
    came_scale = lax.ppermute(scale.reshape(rows), "pair", swap).reshape(rows, 1)

    piece = depth // 4
    start = slab * piece
    mine = jnp.concatenate(
        [lax.dynamic_slice_in_dim(w, start, piece, 0) for w in (w_query, w_key, w_value)], axis=1
    )
    second_piece = lax.ppermute(mine, "line", ends)
    third_in = lax.ppermute(mine, "line", middle)
    third_out = lax.ppermute(third_in, "line", outward)
    fourth_in = lax.ppermute(second_piece, "line", middle)
    fourth_out = lax.ppermute(fourth_in, "line", outward)
    third_piece = jnp.where(inner, third_in, third_out)
    fourth_piece = jnp.where(inner, fourth_in, fourth_out)

    def spread(part):
        far = lax.ppermute(part, "ctx", across)
        return [part, far, lax.ppermute(part, "ctx", beside), lax.ppermute(far, "ctx", beside)]

    second, third_all, fourth_all = [spread(p) for p in (second_piece, third_piece, fourth_piece)]
    gain = norm_gain.reshape(1, -1)
    order_first = jnp.stack([2 * which + side for which in lines[:3]] + [slab]).astype(jnp.int32)
    order_last = jnp.stack([2 * lines[3] + side, slab]).astype(jnp.int32)
    before = add_slots(
        1,
        order_first,
        tokens,
        came_first,
        scale,
        came_scale,
        gain,
        [w_query, w_key, w_value, *second, *third_all],
    )
    sums, back_kv, back_q = add_slots(
        0, order_last, tokens, came_last, scale, came_scale, gain, fourth_all, before
    )
    back_kv = lax.ppermute(back_kv, "pair", swap)
    back_q = lax.ppermute(back_q, "pair", swap)

    positions = slab * rows + jnp.arange(rows, dtype=jnp.int32)
    cosine, sine_table = rotary_tables(positions, head)
    cosine = jnp.concatenate([cosine, cosine], axis=-1).reshape(rows, head)
    sine_table = jnp.concatenate([-sine_table, sine_table], axis=-1).reshape(rows, head)
    key_value = pl.pallas_call(
        key_value_body,
        out_shape=jax.ShapeDtypeStruct((rows, 2 * head), jnp.bfloat16),
        grid=(1,),
        in_specs=[
            pl.BlockSpec((rows, 2 * head), lambda i: (0, query_width // (2 * head))),
            pl.BlockSpec((rows, 2 * head), lambda i: (0, 0)),
            pl.BlockSpec((1, 2 * head), lambda i: (0, 0)),
            pl.BlockSpec((rows, head), lambda i: (0, 0)),
            pl.BlockSpec((rows, head), lambda i: (0, 0)),
        ],
        out_specs=pl.BlockSpec((rows, 2 * head), lambda i: (0, 0)),
        name="key_value",
    )(sums, back_kv, jnp.concatenate([bias_key, bias_value]).reshape(1, -1), cosine, sine_table)
    kv_across = lax.ppermute(key_value, "ctx", [(0, 2), (1, 3)])
    kv_beside = lax.ppermute(key_value, "ctx", beside)
    kv_corner = lax.ppermute(kv_across, "ctx", [(2, 3), (3, 2)])
    kv_spec = pl.BlockSpec((rows, 2 * head), lambda i: (0, 0))
    attended = pl.pallas_call(
        functools.partial(attention_body, head ** (-0.5)),
        out_shape=jax.ShapeDtypeStruct((rows, query_width), jnp.bfloat16),
        grid=(1,),
        in_specs=[
            pl.BlockSpec(memory_space=pltpu.SMEM),
            pl.BlockSpec((rows, query_width), lambda i: (0, 0)),
            pl.BlockSpec((rows, query_width), lambda i: (0, 0)),
            pl.BlockSpec((1, query_width), lambda i: (0, 0)),
            pl.BlockSpec((rows, head), lambda i: (0, 0)),
            pl.BlockSpec((rows, head), lambda i: (0, 0)),
            kv_spec,
            kv_spec,
            kv_spec,
            kv_spec,
        ],
        out_specs=pl.BlockSpec((rows, query_width), lambda i: (0, 0)),
        scratch_shapes=[
            pltpu.VMEM((4 * rows, head), jnp.bfloat16),
            pltpu.VMEM((4 * rows, head), jnp.bfloat16),
        ],
        compiler_params=pltpu.CompilerParams(vmem_limit_bytes=40 * 2**20),
        name="attention",
    )(
        slab.reshape(1).astype(jnp.int32),
        sums,
        back_q,
        bias_query.reshape(1, -1),
        cosine,
        sine_table,
        key_value,
        kv_beside,
        kv_across,
        kv_corner,
    )
    return attended[None]


def shards(hidden, norm_gain, w_query, w_key, w_value, bias_query, bias_key, bias_value):
    if lax.axis_size("line") == 4 and lax.axis_size("ctx") == 4:
        return planned(
            hidden, norm_gain, w_query, w_key, w_value, bias_query, bias_key, bias_value
        )
    local_rows = hidden.shape[1]
    head_width = w_key.shape[1]
    query_width = w_query.shape[1]
    query_heads = query_width // head_width
    sums = project(hidden[0], norm_gain, w_query, w_key, w_value)
    query_sums = sums[:, :query_width]
    key_sums = sums[:, query_width : query_width + head_width]
    value_sums = sums[:, query_width + head_width :]
    slab_index = lax.axis_index("ctx")
    slab_count = lax.axis_size("ctx")
    positions = slab_index * local_rows + jnp.arange(local_rows, dtype=jnp.int32)
    cosine, sine_table = rotary_tables(positions, head_width)
    queries = rotate(
        (query_sums + bias_query.astype(jnp.float32)).reshape(local_rows, query_heads, head_width),
        cosine,
        sine_table,
    ).astype(jnp.bfloat16)
    keys = rotate((key_sums + bias_key.astype(jnp.float32))[:, None, :], cosine, sine_table)[
        :, 0, :
    ].astype(jnp.bfloat16)
    values = (value_sums + bias_value.astype(jnp.float32)).astype(jnp.bfloat16)
    score_scale = head_width ** (-0.5)
    start_state = (
        jnp.full((query_heads, local_rows), masked_score, jnp.float32),
        jnp.zeros((query_heads, local_rows), jnp.float32),
        jnp.zeros((query_heads, local_rows, head_width), jnp.float32),
    )
    key_value = jnp.stack([keys, values])
    column_ids = jnp.arange(local_rows, dtype=jnp.int32)
    causal = column_ids[None, :] <= column_ids[:, None]
    running = attend(queries, score_scale, start_state, key_value, causal[None])

    def forward_step(step_number, state):
        held_running, blocks = state
        blocks = shifted(blocks, "ctx", 1)
        visible = step_number <= slab_index
        held_running = attend(queries, score_scale, held_running, blocks, visible)
        return (held_running, blocks)

    running, key_value = lax.fori_loop(1, slab_count, forward_step, (running, key_value))
    row_peak, row_total, weighted = running
    attended = (
        (weighted / row_total[..., None])
        .transpose(1, 0, 2)
        .reshape(local_rows, query_width)
        .astype(jnp.bfloat16)
    )
    return attended[None]


def solution(mesh):
    groups, slabs = (mesh.shape["fsdp"], mesh.shape["ctx"])
    pairs = Mesh(mesh.devices.reshape(groups // 2, 2, slabs), ("line", "pair", "ctx"))
    both = ("line", "pair")
    in_specs = (
        P(both, "ctx", None),
        P(),
        P(both, None),
        P(both, None),
        P(both, None),
        P(),
        P(),
        P(),
    )
    out_specs = P(both, "ctx", None)
    return jax.shard_map(shards, mesh=pairs, in_specs=in_specs, out_specs=out_specs, check_vma=False)
```

```python
import functools
import math

import jax
import jax.numpy as jnp
from jax import lax
from jax.experimental import pallas as pl
from jax.experimental.pallas import tpu as pltpu
from jax.sharding import Mesh, PartitionSpec as P

epsilon = 1e-06
rotary_base = 1000000.0
masked_score = -1e30


def shifted(value, axis, steps):
    count = lax.axis_size(axis)
    first, last = (max(0, -steps), min(count, count - steps))
    return lax.ppermute(value, axis, [(source, source + steps) for source in range(first, last)])


def rotary_tables(positions, head_width):
    half_width = head_width // 2
    frequency = jnp.exp(
        -(jnp.arange(half_width, dtype=jnp.float32) * (2.0 / head_width)) * math.log(rotary_base)
    )
    angles = positions.astype(jnp.float32)[:, None] * frequency[None, :]
    return (jnp.cos(angles)[:, None, :], jnp.sin(angles)[:, None, :])


def rotate(tensor, cosine, sine_table):
    half_width = tensor.shape[-1] // 2
    lower_half = tensor[..., :half_width]
    upper_half = tensor[..., half_width:]
    return jnp.concatenate(
        [
            lower_half * cosine - upper_half * sine_table,
            upper_half * cosine + lower_half * sine_table,
        ],
        axis=-1,
    )


def attend(work_queries, score_scale, running, key_value, visible):
    row_peak, row_total, weighted = running
    scores = (
        jnp.einsum("qhd,kd->hqk", work_queries, key_value[0], preferred_element_type=jnp.float32)
        * score_scale
    )
    scores = jnp.where(visible, scores, masked_score)
    new_peak = jnp.maximum(row_peak, jnp.max(scores, axis=-1))
    factor = jnp.exp(row_peak - new_peak)
    expsum = jnp.exp(scores - new_peak[..., None])
    row_total = row_total * factor + jnp.sum(expsum, axis=-1)
    weights = expsum.astype(jnp.bfloat16)
    weighted = weighted * factor[..., None] + jnp.einsum(
        "hqk,kd->hqd", weights, key_value[1], preferred_element_type=jnp.float32
    )
    return (new_peak, row_total, weighted)


def row_scale(inputs):
    floats = inputs.astype(jnp.float32)
    return lax.rsqrt(jnp.mean(floats * floats, axis=-1, keepdims=True) + epsilon)


def scaled_rows(inputs, scale, gain):
    return (inputs.astype(jnp.float32) * scale * gain.astype(jnp.float32)).astype(jnp.bfloat16)


def project(hidden, norm_gain, w_query, w_key, w_value):
    local_rows, width = hidden.shape
    lines, slabs = (lax.axis_size("line"), lax.axis_size("ctx"))
    depth = w_query.shape[0]
    side = lax.axis_index("pair")
    swap = [(0, 1), (1, 0)]
    split = hidden.reshape(local_rows, lines, 2, depth)
    half_width = lines * depth

    def half(array, which):
        return lax.dynamic_index_in_dim(array, which, array.ndim - 2, keepdims=False)

    sent = half(split, 1 - side).reshape(local_rows, half_width)
    kept = half(split, side).reshape(local_rows, half_width)
    gain = half(norm_gain.reshape(lines, 2, depth), side).reshape(half_width)
    came = lax.ppermute(sent, "pair", swap)
    scale = row_scale(hidden)
    came_scale = lax.ppermute(scale, "pair", swap)
    piece = depth // slabs
    start = lax.axis_index("ctx") * piece
    packed = jnp.concatenate(
        [lax.dynamic_slice_in_dim(w, start, piece, 0) for w in (w_query, w_key, w_value)], axis=1
    )
    weights = lax.all_gather(packed, ("line", "ctx"), axis=0, tiled=True)
    rows = jnp.concatenate(
        [scaled_rows(kept, scale, gain), scaled_rows(came, came_scale, gain)], axis=0
    )
    sums = jnp.dot(rows, weights, preferred_element_type=jnp.float32)
    back = lax.ppermute(sums[local_rows:].astype(jnp.bfloat16), "pair", swap)
    return sums[:local_rows] + back.astype(jnp.float32)


def normed_rows(block, scale, gain):
    return (block.astype(jnp.float32) * scale * gain).astype(jnp.bfloat16)


def slot_lines():
    line = lax.axis_index("line")
    inner = (line == 1) | (line == 2)
    third = jnp.where(inner, line ^ 3, line ^ 2)
    fourth = jnp.where(inner, line ^ 2, line ^ 3)
    return [line, line ^ 1, third, fourth]


def started(copies, sems, first):
    flights = [
        pltpu.make_async_copy(source, target, sems.at[first + number])
        for number, (source, target) in enumerate(copies)
    ]
    for flight in flights:
        flight.start()
    return flights


def piece_copies(pieces, wide, slab):
    piece = pieces[0].shape[0]
    return [
        (source, wide.at[pl.ds(pl.multiple_of(jnp.bitwise_xor(slab, flip) * piece, piece), piece), :])
        for source, flip in zip(pieces, (0, 2, 1, 3))
    ]


def pack_body(sent_parts, weights, depth, *refs):
    tokens, refs = (refs[0], refs[1:])
    sources, refs = (refs[:weights], refs[weights:])
    sems = refs[-1]
    copies = []
    outs = refs[:-1]
    if weights:
        mine, outs = (outs[0], outs[1:])
        piece = mine.shape[0]
        row = pl.multiple_of(lax.axis_index("ctx") * piece, piece)
        at = 0
        for source in sources:
            target = mine.at[:, pl.ds(at, source.shape[1])]
            copies.append((source.at[pl.ds(row, piece), :], target))
            at += source.shape[1]
    lines = slot_lines()
    other = 1 - lax.axis_index("pair")
    for out, parts in zip(outs, sent_parts):
        at = 0
        for slot, first, count in parts:
            column = pl.multiple_of((2 * lines[slot] + other) * depth + first, 128)
            copies.append((tokens.at[:, pl.ds(column, count)], out.at[:, pl.ds(at, count)]))
            at += count
    for flight in started(copies, sems, 0):
        flight.wait()


def pack(tokens, depth, sent_parts, weights=()):
    rows = tokens.shape[0]
    outside = pl.BlockSpec(memory_space=pltpu.HBM)
    outs = []
    if weights:
        piece = weights[0].shape[0] // 4
        outs.append(jax.ShapeDtypeStruct((piece, sum(w.shape[1] for w in weights)), jnp.bfloat16))
    for parts in sent_parts:
        outs.append(jax.ShapeDtypeStruct((rows, sum(p[2] for p in parts)), jnp.bfloat16))
    copies = len(weights) + sum(len(parts) for parts in sent_parts)
    moved = 4 * sum(out.shape[0] * out.shape[1] for out in outs)
    return pl.pallas_call(
        functools.partial(pack_body, sent_parts, len(weights), depth),
        out_shape=outs,
        in_specs=[outside] * (1 + len(weights)),
        out_specs=[pl.BlockSpec(memory_space=pltpu.VMEM)] * len(outs),
        scratch_shapes=[pltpu.SemaphoreType.DMA((copies,))],
        cost_estimate=pl.CostEstimate(flops=0, bytes_accessed=moved, transcendentals=0),
        name="pack",
    )(tokens, *weights)


def prepare_body(sent_parts, depth, tokens, *refs):
    outs, refs = (refs[: len(sent_parts)], refs[len(sent_parts) :])
    column_scale, line_scale, held, sems = refs
    rows, width = held.shape
    lines = slot_lines()
    other = 1 - lax.axis_index("pair")
    loads = [
        (tokens.at[:, pl.ds(at, depth)], held.at[:, pl.ds(at, depth)])
        for at in range(0, width, depth)
    ]
    loads = started(loads, sems, 0)
    copies = []
    for out, parts in zip(outs, sent_parts):
        at = 0
        for slot, first, count in parts:
            column = pl.multiple_of((2 * lines[slot] + other) * depth + first, 128)
            copies.append((tokens.at[:, pl.ds(column, count)], out.at[:, pl.ds(at, count)]))
            at += count
    copies = started(copies, sems, len(loads))
    squares = jnp.zeros((rows, 128), jnp.float32)
    for number, load in enumerate(loads):
        load.wait()
        for at in range(number * depth, (number + 1) * depth, 128):
            floats = held[:, at : at + 128].astype(jnp.float32)
            squares = squares + floats * floats
    mean = jnp.sum(squares, axis=1, keepdims=True) / width
    wide = jnp.broadcast_to(lax.rsqrt(mean + epsilon), (rows, 128))
    column_scale[...] = wide
    line_scale[...] = jnp.transpose(wide)[:1]
    for copy in copies:
        copy.wait()


def prepare(tokens, depth, sent_parts):
    rows, width = tokens.shape
    outs = [
        jax.ShapeDtypeStruct((rows, sum(p[2] for p in parts)), jnp.bfloat16)
        for parts in sent_parts
    ]
    outs.append(jax.ShapeDtypeStruct((rows, 128), jnp.float32))
    outs.append(jax.ShapeDtypeStruct((1, rows), jnp.float32))
    copies = width // depth + sum(len(parts) for parts in sent_parts)
    return pl.pallas_call(
        functools.partial(prepare_body, sent_parts, depth),
        out_shape=outs,
        in_specs=[pl.BlockSpec(memory_space=pltpu.HBM)],
        out_specs=[pl.BlockSpec(memory_space=pltpu.VMEM)] * len(outs),
        scratch_shapes=[
            pltpu.VMEM((rows, width), jnp.bfloat16),
            pltpu.SemaphoreType.DMA((copies,)),
        ],
        cost_estimate=pl.CostEstimate(
            flops=2 * rows * width, bytes_accessed=4 * rows * width, transcendentals=rows
        ),
        name="prepare",
    )(tokens)


def early_body(slots, guests, local, final, hidden, *refs):
    count = 1 + max(part[0] for part in guests)
    cames, refs = (refs[:count], refs[count:])
    scale, came_scale, gain, *refs = refs
    summed = slots[:-1] if final else slots
    number = 3 * local + 4 * (len(summed) - local)
    weights, refs = (refs[:number], refs[number:])
    before = None
    if not local:
        before, *refs = refs
    total, *refs = refs
    if final:
        last_rows, *refs = refs
    held, guest, wide, stacked, sems = refs
    _, rows, depth = held.shape
    slab = lax.axis_index("ctx")
    blocks = [2 * which + lax.axis_index("pair") for which in slot_lines()]
    number = 0
    parts = []
    at = 0
    for source, first, width in guests:
        parts.append(
            (cames[source].at[:, pl.ds(first, width)], guest.at[:, pl.ds(at, width)])
        )
        at += width
    guest_flights = started(parts, sems, number)
    number += len(parts)
    flights = []
    pending = list(weights)
    for place, slot in enumerate(slots):
        column = pl.multiple_of(blocks[slot] * depth, depth)
        copies = [(hidden.at[:, pl.ds(column, depth)], held.at[place])]
        if slot == 0:
            at = 0
            for _ in range(3):
                weight = pending.pop(0)
                copies.append((weight, wide.at[place, :, pl.ds(at, weight.shape[1])]))
                at += weight.shape[1]
        elif slot in summed:
            copies += piece_copies(pending[:4], wide.at[place], slab)
            pending = pending[4:]
        flights.append(started(copies, sems, number))
        number += len(copies)
    turned_scale = jnp.transpose(jnp.broadcast_to(came_scale[...], (128, rows)))[:, :1]
    for flight in guest_flights:
        flight.wait()
    width = total.shape[1]
    step = 256
    for place, slot in enumerate(slots):
        for flight in flights[place]:
            flight.wait()
        column = pl.multiple_of(blocks[slot] * depth, depth)
        row_gain = gain[:, pl.ds(column, depth)].astype(jnp.float32)
        target = stacked.at[place] if slot in summed else last_rows
        target[:rows] = normed_rows(held[place], scale[:, :1], row_gain)
        target[rows:] = normed_rows(
            guest[:, place * depth : (place + 1) * depth], turned_scale, row_gain
        )
        if slot not in summed:
            continue
        for at in range(0, width, step):
            cols = pl.ds(at, step)
            product = jnp.dot(
                stacked[place], wide[place, :, cols], preferred_element_type=jnp.float32
            )
            if place > 0:
                product = product + total[:, cols]
            elif before is not None:
                product = product + before[:, cols]
            total[:, cols] = product


def early_slots(
    slots, guests, local, final, hidden, cames, scale, came_scale, gain, weights, before=None
):
    rows = hidden.shape[0]
    depth = weights[0].shape[0] if local else 4 * weights[0].shape[0]
    width = sum(w.shape[1] for w in weights[:3]) if local else weights[0].shape[1]
    outside = pl.BlockSpec(memory_space=pltpu.HBM)
    anywhere = pl.BlockSpec(memory_space=pl.ANY)
    inside = pl.BlockSpec(memory_space=pltpu.VMEM)
    summed = len(slots) - final
    flops = 4 * rows * depth * summed * width
    moved = 2 * (depth * width * summed + 2 * rows * depth * len(slots)) + 8 * rows * width
    outs = [jax.ShapeDtypeStruct((2 * rows, width), jnp.float32)]
    if final:
        outs.append(jax.ShapeDtypeStruct((2 * rows, depth), jnp.bfloat16))
    args = [hidden, *cames, scale, came_scale, gain, *weights]
    in_specs = [outside] + [anywhere] * len(cames)
    in_specs += [inside] * 3 + [outside] * (3 * local) + [anywhere] * (len(weights) - 3 * local)
    if before is not None:
        args.append(before)
        in_specs.append(inside)
    return pl.pallas_call(
        functools.partial(early_body, slots, guests, local, final),
        out_shape=outs,
        in_specs=in_specs,
        out_specs=[inside] * len(outs),
        scratch_shapes=[
            pltpu.VMEM((len(slots), rows, depth), jnp.bfloat16),
            pltpu.VMEM((rows, len(slots) * depth), jnp.bfloat16),
            pltpu.VMEM((summed, depth, width), jnp.bfloat16),
            pltpu.VMEM((summed, 2 * rows, depth), jnp.bfloat16),
            pltpu.SemaphoreType.DMA((len(guests) + len(slots) + len(weights),)),
        ],
        cost_estimate=pl.CostEstimate(flops=flops, bytes_accessed=moved, transcendentals=0),
        compiler_params=pltpu.CompilerParams(vmem_limit_bytes=60 * 2**20),
        name="early_slots",
    )(*args)


def late_body(first, splits, before, last_rows, *refs):
    pieces, refs = (refs[:4], refs[4:])
    kept, (sent, wide, sems) = (refs[: len(splits)], refs[len(splits) :])
    rows, width = sent.shape
    pieces = [p if p.shape[1] == width else p.at[:, pl.ds(first, width)] for p in pieces]
    for flight in started(piece_copies(pieces, wide, lax.axis_index("ctx")), sems, 0):
        flight.wait()
    at = 0
    for own, columns in zip(kept, splits):
        cols = slice(at, at + columns)
        product = jnp.dot(last_rows[...], wide[:, cols], preferred_element_type=jnp.float32)
        product = product + before[:, first + at : first + at + columns]
        own[...] = product[:rows]
        sent[:, cols] = product[rows:].astype(jnp.bfloat16)
        at += columns


def late_slot(first, splits, before, last_rows, pieces):
    rows, depth = (last_rows.shape[0] // 2, last_rows.shape[1])
    anywhere = pl.BlockSpec(memory_space=pl.ANY)
    inside = pl.BlockSpec(memory_space=pltpu.VMEM)
    width = sum(splits)
    outs = [jax.ShapeDtypeStruct((rows, w), jnp.float32) for w in splits]
    outs.append(jax.ShapeDtypeStruct((rows, width), jnp.bfloat16))
    return pl.pallas_call(
        functools.partial(late_body, first, splits),
        out_shape=outs,
        in_specs=[inside] * 2 + [anywhere] * 4,
        out_specs=[inside] * len(outs),
        scratch_shapes=[
            pltpu.VMEM((depth, width), jnp.bfloat16),
            pltpu.SemaphoreType.DMA((4,)),
        ],
        cost_estimate=pl.CostEstimate(
            flops=4 * rows * depth * width, bytes_accessed=2 * depth * width, transcendentals=0
        ),
        compiler_params=pltpu.CompilerParams(vmem_limit_bytes=16 * 2**20),
        name="late_slot",
    )(before, last_rows, *pieces)


def turned(tensor, cosine, sine_table):
    half = tensor.shape[-1] // 2
    return tensor * cosine + pltpu.roll(tensor, half, 1) * sine_table


def key_value_body(sums, back, bias, cosine, sine_table, out):
    head = out.shape[1] // 2
    total = sums[...] + back[:, : 2 * head].astype(jnp.float32) + bias[...]
    out[:, :head] = turned(total[:, :head], cosine[...], sine_table[...]).astype(jnp.bfloat16)
    out[:, head:] = total[:, head:].astype(jnp.bfloat16)


def attention_body(scale, first, sums, back, bias, cosine, sine_table, *refs):
    blocks, refs = (refs[:4], refs[4:])
    if first:
        done, *refs = refs
    out, keys, values = refs
    rows = out.shape[0]
    head = cosine.shape[1]
    slab = lax.axis_index("ctx")
    for block, flip in zip(blocks, (0, 1, 2, 3)):
        row = pl.multiple_of(jnp.bitwise_xor(slab, flip) * rows, rows)
        keys[pl.ds(row, rows), :] = block[:, :head]
        values[pl.ds(row, rows), :] = block[:, head:]
    total_keys = keys.shape[0]
    row_ids = slab * rows + lax.broadcasted_iota(jnp.int32, (rows, total_keys), 0)
    visible = lax.broadcasted_iota(jnp.int32, (rows, total_keys), 1) <= row_ids
    if first:
        out[:, :first] = done[...]
    for at in range(0, sums.shape[1], head):
        cols = pl.ds(at, head)
        skipped = back.shape[1] - sums.shape[1]
        query = sums[:, cols] + back[:, skipped + at : skipped + at + head].astype(jnp.float32)
        query = query + bias[:, first + at : first + at + head]
        query = turned(query, cosine[...], sine_table[...]).astype(jnp.bfloat16)
        scores = lax.dot_general(
            query, keys[...], (((1,), (1,)), ((), ())), preferred_element_type=jnp.float32
        )
        scores = jnp.where(visible, scores * scale, masked_score)
        exps = jnp.exp(scores - jnp.max(scores, axis=1, keepdims=True))
        length = jnp.sum(exps, axis=1, keepdims=True)
        mixed = jnp.dot(exps.astype(jnp.bfloat16), values[...], preferred_element_type=jnp.float32)
        out[:, first + at : first + at + head] = (mixed / length).astype(jnp.bfloat16)


def attention(sums, back, bias, cosine, sine_table, blocks, done=None):
    rows, width = sums.shape
    head = cosine.shape[1]
    first = 0 if done is None else done.shape[1]
    inside = pl.BlockSpec(memory_space=pltpu.VMEM)
    args = [sums, back, bias, cosine, sine_table, *blocks]
    if first:
        args.append(done)
    total = 4 * rows * rows * (width // head)
    return pl.pallas_call(
        functools.partial(attention_body, head ** (-0.5), first),
        out_shape=jax.ShapeDtypeStruct((rows, first + width), jnp.bfloat16),
        in_specs=[inside] * len(args),
        out_specs=inside,
        scratch_shapes=[
            pltpu.VMEM((4 * rows, head), jnp.bfloat16),
            pltpu.VMEM((4 * rows, head), jnp.bfloat16),
        ],
        cost_estimate=pl.CostEstimate(
            flops=4 * total * head, bytes_accessed=8 * rows * width, transcendentals=total
        ),
        compiler_params=pltpu.CompilerParams(vmem_limit_bytes=24 * 2**20),
        name="attention",
    )(*args)


def planned(hidden, norm_gain, w_query, w_key, w_value, bias_query, bias_key, bias_value):
    tokens = hidden[0]
    rows = tokens.shape[0]
    depth = w_query.shape[0]
    head = w_key.shape[1]
    line, slab = (lax.axis_index("line"), lax.axis_index("ctx"))
    inner = (line == 1) | (line == 2)
    swap = [(0, 1), (1, 0)]
    ends = [(0, 1), (1, 0), (2, 3), (3, 2)]
    middle = [(1, 2), (2, 1)]
    outward = [(1, 0), (2, 3)]
    across = [(i, i ^ 2) for i in range(4)]
    beside = [(i, i ^ 1) for i in range(4)]
    held = lax.optimization_barrier
    cut = depth // 8
    parts_1 = ((0, 0, depth), (1, 0, cut))
    parts_2 = ((1, cut, 7 * cut), (2, 0, 5 * cut))
    parts_3 = ((2, 5 * cut, 3 * cut), (3, 0, depth))
    mine, sent_1 = pack(tokens, depth, (parts_1,), (w_key, w_value, w_query))
    half = mine.shape[1] // 2
    kv_width = 2 * head
    second = lax.ppermute(mine, "line", ends)
    third_in = lax.ppermute(mine, "line", middle)
    fourth_in = lax.ppermute(second, "line", middle)
    came_1 = lax.ppermute(sent_1, "pair", swap)
    sent_2, sent_3, scale, line_scale = prepare(tokens, depth, (parts_2, parts_3))
    came_scale = lax.ppermute(line_scale, "pair", swap)
    gain = norm_gain.reshape(1, -1)
    bias_kv = jnp.concatenate([bias_key, bias_value]).reshape(1, -1).astype(jnp.float32)
    bias_q = bias_query.reshape(1, -1).astype(jnp.float32)
    positions = slab * rows + jnp.arange(rows, dtype=jnp.int32)
    cosine, sine_table = rotary_tables(positions, head)
    cosine = jnp.concatenate([cosine, cosine], axis=-1).reshape(rows, head)
    sine_table = jnp.concatenate([-sine_table, sine_table], axis=-1).reshape(rows, head)
    small = (scale, came_scale, gain, bias_kv, bias_q, cosine, sine_table)
    second, third_in, came_1, sent_2, sent_3, small = held(
        (second, third_in, came_1, sent_2, sent_3, small)
    )
    scale, came_scale, gain, bias_kv, bias_q, cosine, sine_table = small
    third_out = lax.ppermute(third_in, "line", outward)
    second_far = lax.ppermute(second, "ctx", across)
    came_2 = lax.ppermute(sent_2, "pair", swap)
    second_side = lax.ppermute(second, "ctx", beside)
    fourth_out = lax.ppermute(fourth_in, "line", outward)
    third = jnp.where(inner, third_in, third_out)
    third, second_far, came_2, second_side, sent_3 = held(
        (third, second_far, came_2, second_side, sent_3)
    )
    third_far = lax.ppermute(third, "ctx", across)
    came_3 = lax.ppermute(sent_3, "pair", swap)
    second_corner = lax.ppermute(second_far, "ctx", beside)
    third_side = lax.ppermute(third, "ctx", beside)
    before = early_slots(
        (0, 1),
        ((0, 0, 9 * cut), (1, 0, 7 * cut)),
        True,
        False,
        tokens,
        (came_1, came_2),
        scale,
        came_scale,
        gain,
        [w_key, w_value, w_query, second, second_far, second_side, second_corner],
    )[0]
    fourth = jnp.where(inner, fourth_in, fourth_out)
    fourth, third_far, came_3, third_side, before = held(
        (fourth, third_far, came_3, third_side, before)
    )
    fourth_far_1 = lax.ppermute(fourth[:, :half], "ctx", across)
    third_corner = lax.ppermute(third_far, "ctx", beside)
    fourth_side = lax.ppermute(fourth, "ctx", beside)
    before, last_rows = early_slots(
        (2, 3),
        ((0, 7 * cut, 5 * cut), (1, 0, 11 * cut)),
        False,
        True,
        tokens,
        (came_2, came_3),
        scale,
        came_scale,
        gain,
        [third, third_far, third_side, third_corner],
        before,
    )
    fourth_far_1, fourth, before, last_rows, fourth_side = held(
        (fourth_far_1, fourth, before, last_rows, fourth_side)
    )
    fourth_far_2 = lax.ppermute(fourth[:, half:], "ctx", across)
    fourth_corner_1 = lax.ppermute(fourth_far_1, "ctx", beside)
    kv_sums, q_sums_1, back_1 = late_slot(
        0,
        (kv_width, half - kv_width),
        before,
        last_rows,
        (fourth, fourth_far_1, fourth_side, fourth_corner_1),
    )
    back_1, fourth_far_2 = held((back_1, fourth_far_2))
    back_1 = lax.ppermute(back_1, "pair", swap)
    fourth_corner_2 = lax.ppermute(fourth_far_2, "ctx", beside)
    q_sums_2, back_2 = late_slot(
        half,
        (half,),
        before,
        last_rows,
        (fourth, fourth_far_2, fourth_side, fourth_corner_2),
    )
    back_2 = lax.ppermute(back_2, "pair", swap)

    inside = pl.BlockSpec(memory_space=pltpu.VMEM)
    key_value = pl.pallas_call(
        key_value_body,
        out_shape=jax.ShapeDtypeStruct((rows, kv_width), jnp.bfloat16),
        in_specs=[inside] * 5,
        out_specs=inside,
        name="key_value",
    )(kv_sums, back_1, bias_kv, cosine, sine_table)
    kv_across = lax.ppermute(key_value, "ctx", [(0, 2), (1, 3)])
    kv_beside = lax.ppermute(key_value, "ctx", beside)
    kv_corner = lax.ppermute(key_value, "ctx", [(0, 3), (1, 2)])
    blocks = (key_value, kv_beside, kv_across, kv_corner)
    attended = attention(q_sums_1, back_1, bias_q, cosine, sine_table, blocks)
    attended = attention(q_sums_2, back_2, bias_q, cosine, sine_table, blocks, attended)
    return attended[None]


def shards(hidden, norm_gain, w_query, w_key, w_value, bias_query, bias_key, bias_value):
    if lax.axis_size("line") == 4 and lax.axis_size("ctx") == 4:
        return planned(
            hidden, norm_gain, w_query, w_key, w_value, bias_query, bias_key, bias_value
        )
    local_rows = hidden.shape[1]
    head_width = w_key.shape[1]
    query_width = w_query.shape[1]
    query_heads = query_width // head_width
    sums = project(hidden[0], norm_gain, w_query, w_key, w_value)
    query_sums = sums[:, :query_width]
    key_sums = sums[:, query_width : query_width + head_width]
    value_sums = sums[:, query_width + head_width :]
    slab_index = lax.axis_index("ctx")
    slab_count = lax.axis_size("ctx")
    positions = slab_index * local_rows + jnp.arange(local_rows, dtype=jnp.int32)
    cosine, sine_table = rotary_tables(positions, head_width)
    queries = rotate(
        (query_sums + bias_query.astype(jnp.float32)).reshape(local_rows, query_heads, head_width),
        cosine,
        sine_table,
    ).astype(jnp.bfloat16)
    keys = rotate((key_sums + bias_key.astype(jnp.float32))[:, None, :], cosine, sine_table)[
        :, 0, :
    ].astype(jnp.bfloat16)
    values = (value_sums + bias_value.astype(jnp.float32)).astype(jnp.bfloat16)
    score_scale = head_width ** (-0.5)
    start_state = (
        jnp.full((query_heads, local_rows), masked_score, jnp.float32),
        jnp.zeros((query_heads, local_rows), jnp.float32),
        jnp.zeros((query_heads, local_rows, head_width), jnp.float32),
    )
    key_value = jnp.stack([keys, values])
    column_ids = jnp.arange(local_rows, dtype=jnp.int32)
    causal = column_ids[None, :] <= column_ids[:, None]
    running = attend(queries, score_scale, start_state, key_value, causal[None])

    def forward_step(step_number, state):
        held_running, blocks = state
        blocks = shifted(blocks, "ctx", 1)
        visible = step_number <= slab_index
        held_running = attend(queries, score_scale, held_running, blocks, visible)
        return (held_running, blocks)

    running, key_value = lax.fori_loop(1, slab_count, forward_step, (running, key_value))
    row_peak, row_total, weighted = running
    attended = (
        (weighted / row_total[..., None])
        .transpose(1, 0, 2)
        .reshape(local_rows, query_width)
        .astype(jnp.bfloat16)
    )
    return attended[None]


def solution(mesh):
    groups, slabs = (mesh.shape["fsdp"], mesh.shape["ctx"])
    pairs = Mesh(mesh.devices.reshape(groups // 2, 2, slabs), ("line", "pair", "ctx"))
    both = ("line", "pair")
    in_specs = (
        P(both, "ctx", None),
        P(),
        P(both, None),
        P(both, None),
        P(both, None),
        P(),
        P(),
        P(),
    )
    out_specs = P(both, "ctx", None)
    return jax.shard_map(shards, mesh=pairs, in_specs=in_specs, out_specs=out_specs, check_vma=False)
```

```python
import functools
import math

import jax
import jax.numpy as jnp
from jax import lax
from jax.experimental import pallas as pl
from jax.experimental.pallas import tpu as pltpu
from jax.sharding import Mesh, PartitionSpec as P

epsilon = 1e-06
rotary_base = 1000000.0
masked_score = -1e30


def shifted(value, axis, steps):
    count = lax.axis_size(axis)
    first, last = (max(0, -steps), min(count, count - steps))
    return lax.ppermute(value, axis, [(source, source + steps) for source in range(first, last)])


def rotary_tables(positions, head_width):
    half_width = head_width // 2
    frequency = jnp.exp(
        -(jnp.arange(half_width, dtype=jnp.float32) * (2.0 / head_width)) * math.log(rotary_base)
    )
    angles = positions.astype(jnp.float32)[:, None] * frequency[None, :]
    return (jnp.cos(angles)[:, None, :], jnp.sin(angles)[:, None, :])


def rotate(tensor, cosine, sine_table):
    half_width = tensor.shape[-1] // 2
    lower_half = tensor[..., :half_width]
    upper_half = tensor[..., half_width:]
    return jnp.concatenate(
        [
            lower_half * cosine - upper_half * sine_table,
            upper_half * cosine + lower_half * sine_table,
        ],
        axis=-1,
    )


def attend(work_queries, score_scale, running, key_value, visible):
    row_peak, row_total, weighted = running
    scores = (
        jnp.einsum("qhd,kd->hqk", work_queries, key_value[0], preferred_element_type=jnp.float32)
        * score_scale
    )
    scores = jnp.where(visible, scores, masked_score)
    new_peak = jnp.maximum(row_peak, jnp.max(scores, axis=-1))
    factor = jnp.exp(row_peak - new_peak)
    expsum = jnp.exp(scores - new_peak[..., None])
    row_total = row_total * factor + jnp.sum(expsum, axis=-1)
    weights = expsum.astype(jnp.bfloat16)
    weighted = weighted * factor[..., None] + jnp.einsum(
        "hqk,kd->hqd", weights, key_value[1], preferred_element_type=jnp.float32
    )
    return (new_peak, row_total, weighted)


def row_scale(inputs):
    floats = inputs.astype(jnp.float32)
    return lax.rsqrt(jnp.mean(floats * floats, axis=-1, keepdims=True) + epsilon)


def scaled_rows(inputs, scale, gain):
    return (inputs.astype(jnp.float32) * scale * gain.astype(jnp.float32)).astype(jnp.bfloat16)


def project(hidden, norm_gain, w_query, w_key, w_value):
    local_rows, width = hidden.shape
    lines, slabs = (lax.axis_size("line"), lax.axis_size("ctx"))
    depth = w_query.shape[0]
    side = lax.axis_index("pair")
    swap = [(0, 1), (1, 0)]
    split = hidden.reshape(local_rows, lines, 2, depth)
    half_width = lines * depth

    def half(array, which):
        return lax.dynamic_index_in_dim(array, which, array.ndim - 2, keepdims=False)

    sent = half(split, 1 - side).reshape(local_rows, half_width)
    kept = half(split, side).reshape(local_rows, half_width)
    gain = half(norm_gain.reshape(lines, 2, depth), side).reshape(half_width)
    came = lax.ppermute(sent, "pair", swap)
    scale = row_scale(hidden)
    came_scale = lax.ppermute(scale, "pair", swap)
    piece = depth // slabs
    start = lax.axis_index("ctx") * piece
    packed = jnp.concatenate(
        [lax.dynamic_slice_in_dim(w, start, piece, 0) for w in (w_query, w_key, w_value)], axis=1
    )
    weights = lax.all_gather(packed, ("line", "ctx"), axis=0, tiled=True)
    rows = jnp.concatenate(
        [scaled_rows(kept, scale, gain), scaled_rows(came, came_scale, gain)], axis=0
    )
    sums = jnp.dot(rows, weights, preferred_element_type=jnp.float32)
    back = lax.ppermute(sums[local_rows:].astype(jnp.bfloat16), "pair", swap)
    return sums[:local_rows] + back.astype(jnp.float32)


def normed_rows(block, scale, gain):
    return (block.astype(jnp.float32) * scale * gain).astype(jnp.bfloat16)


def slot_lines():
    line = lax.axis_index("line")
    inner = (line == 1) | (line == 2)
    third = jnp.where(inner, line ^ 3, line ^ 2)
    fourth = jnp.where(inner, line ^ 2, line ^ 3)
    return [line, line ^ 1, third, fourth]


def started(copies, sems, first):
    flights = [
        pltpu.make_async_copy(source, target, sems.at[first + number])
        for number, (source, target) in enumerate(copies)
    ]
    for flight in flights:
        flight.start()
    return flights


def piece_copies(pieces, wide, slab):
    piece = pieces[0].shape[0]
    return [
        (source, wide.at[pl.ds(pl.multiple_of(jnp.bitwise_xor(slab, flip) * piece, piece), piece), :])
        for source, flip in zip(pieces, (0, 2, 1, 3))
    ]


def pack_body(sent_parts, weights, depth, *refs):
    tokens, refs = (refs[0], refs[1:])
    sources, refs = (refs[:weights], refs[weights:])
    sems = refs[-1]
    copies = []
    outs = refs[:-1]
    if weights:
        mine, outs = (outs[0], outs[1:])
        piece = mine.shape[0]
        row = pl.multiple_of(lax.axis_index("ctx") * piece, piece)
        at = 0
        for source in sources:
            target = mine.at[:, pl.ds(at, source.shape[1])]
            copies.append((source.at[pl.ds(row, piece), :], target))
            at += source.shape[1]
    lines = slot_lines()
    other = 1 - lax.axis_index("pair")
    for out, parts in zip(outs, sent_parts):
        at = 0
        for slot, first, count in parts:
            column = pl.multiple_of((2 * lines[slot] + other) * depth + first, 128)
            copies.append((tokens.at[:, pl.ds(column, count)], out.at[:, pl.ds(at, count)]))
            at += count
    for flight in started(copies, sems, 0):
        flight.wait()


def pack(tokens, depth, sent_parts, weights=()):
    rows = tokens.shape[0]
    outside = pl.BlockSpec(memory_space=pltpu.HBM)
    outs = []
    if weights:
        piece = weights[0].shape[0] // 4
        outs.append(jax.ShapeDtypeStruct((piece, sum(w.shape[1] for w in weights)), jnp.bfloat16))
    for parts in sent_parts:
        outs.append(jax.ShapeDtypeStruct((rows, sum(p[2] for p in parts)), jnp.bfloat16))
    copies = len(weights) + sum(len(parts) for parts in sent_parts)
    moved = 4 * sum(out.shape[0] * out.shape[1] for out in outs)
    return pl.pallas_call(
        functools.partial(pack_body, sent_parts, len(weights), depth),
        out_shape=outs,
        in_specs=[outside] * (1 + len(weights)),
        out_specs=[pl.BlockSpec(memory_space=pltpu.VMEM)] * len(outs),
        scratch_shapes=[pltpu.SemaphoreType.DMA((copies,))],
        cost_estimate=pl.CostEstimate(flops=0, bytes_accessed=0, transcendentals=0),
        name="pack",
    )(tokens, *weights)


def prepare_body(sent_parts, depth, tokens, *refs):
    outs, refs = (refs[: len(sent_parts)], refs[len(sent_parts) :])
    column_scale, line_scale, held, sems = refs
    rows, width = held.shape
    lines = slot_lines()
    other = 1 - lax.axis_index("pair")
    loads = [
        (tokens.at[:, pl.ds(at, depth)], held.at[:, pl.ds(at, depth)])
        for at in range(0, width, depth)
    ]
    loads = started(loads, sems, 0)
    copies = []
    for out, parts in zip(outs, sent_parts):
        at = 0
        for slot, first, count in parts:
            column = pl.multiple_of((2 * lines[slot] + other) * depth + first, 128)
            copies.append((tokens.at[:, pl.ds(column, count)], out.at[:, pl.ds(at, count)]))
            at += count
    copies = started(copies, sems, len(loads))
    squares = jnp.zeros((rows, 128), jnp.float32)
    for number, load in enumerate(loads):
        load.wait()
        for at in range(number * depth, (number + 1) * depth, 128):
            floats = held[:, at : at + 128].astype(jnp.float32)
            squares = squares + floats * floats
    mean = jnp.sum(squares, axis=1, keepdims=True) / width
    wide = jnp.broadcast_to(lax.rsqrt(mean + epsilon), (rows, 128))
    column_scale[...] = wide
    line_scale[...] = jnp.transpose(wide)[:1]
    for copy in copies:
        copy.wait()


def prepare(tokens, depth, sent_parts):
    rows, width = tokens.shape
    outs = [
        jax.ShapeDtypeStruct((rows, sum(p[2] for p in parts)), jnp.bfloat16)
        for parts in sent_parts
    ]
    outs.append(jax.ShapeDtypeStruct((rows, 128), jnp.float32))
    outs.append(jax.ShapeDtypeStruct((1, rows), jnp.float32))
    copies = width // depth + sum(len(parts) for parts in sent_parts)
    return pl.pallas_call(
        functools.partial(prepare_body, sent_parts, depth),
        out_shape=outs,
        in_specs=[pl.BlockSpec(memory_space=pltpu.HBM)],
        out_specs=[pl.BlockSpec(memory_space=pltpu.VMEM)] * len(outs),
        scratch_shapes=[
            pltpu.VMEM((rows, width), jnp.bfloat16),
            pltpu.SemaphoreType.DMA((copies,)),
        ],
        cost_estimate=pl.CostEstimate(flops=0, bytes_accessed=0, transcendentals=0),
        compiler_params=pltpu.CompilerParams(vmem_limit_bytes=10 * 2**20),
        name="prepare",
    )(tokens)


def early_body(slots, guests, local, final, hidden, *refs):
    count = 1 + max(part[0] for part in guests)
    cames, refs = (refs[:count], refs[count:])
    scale, came_scale, gain, *refs = refs
    summed = slots[:-1] if final else slots
    number = 3 * local + 4 * (len(summed) - local)
    weights, refs = (refs[:number], refs[number:])
    before = None
    if not local:
        before, *refs = refs
    total, *refs = refs
    if final:
        last_rows, *refs = refs
    held, guest, wide, stacked, sems = refs
    _, rows, depth = held.shape
    slab = lax.axis_index("ctx")
    blocks = [2 * which + lax.axis_index("pair") for which in slot_lines()]
    number = 0
    parts = []
    at = 0
    for source, first, width in guests:
        parts.append(
            (cames[source].at[:, pl.ds(first, width)], guest.at[:, pl.ds(at, width)])
        )
        at += width
    guest_flights = started(parts, sems, number)
    number += len(parts)
    flights = []
    pending = list(weights)
    for place, slot in enumerate(slots):
        column = pl.multiple_of(blocks[slot] * depth, depth)
        copies = [(hidden.at[:, pl.ds(column, depth)], held.at[place])]
        if slot == 0:
            at = 0
            for _ in range(3):
                weight = pending.pop(0)
                copies.append((weight, wide.at[place, :, pl.ds(at, weight.shape[1])]))
                at += weight.shape[1]
        elif slot in summed:
            copies += piece_copies(pending[:4], wide.at[place], slab)
            pending = pending[4:]
        flights.append(started(copies, sems, number))
        number += len(copies)
    turned_scale = jnp.transpose(jnp.broadcast_to(came_scale[...], (128, rows)))[:, :1]
    for flight in guest_flights:
        flight.wait()
    width = total.shape[1]
    step = 256
    for place, slot in enumerate(slots):
        for flight in flights[place]:
            flight.wait()
        column = pl.multiple_of(blocks[slot] * depth, depth)
        row_gain = gain[:, pl.ds(column, depth)].astype(jnp.float32)
        target = stacked.at[place] if slot in summed else last_rows
        target[:rows] = normed_rows(held[place], scale[:, :1], row_gain)
        target[rows:] = normed_rows(
            guest[:, place * depth : (place + 1) * depth], turned_scale, row_gain
        )
        if slot not in summed:
            continue
        for at in range(0, width, step):
            cols = pl.ds(at, step)
            product = jnp.dot(
                stacked[place], wide[place, :, cols], preferred_element_type=jnp.float32
            )
            if place > 0:
                product = product + total[:, cols]
            elif before is not None:
                product = product + before[:, cols]
            total[:, cols] = product


def early_slots(
    slots, guests, local, final, hidden, cames, scale, came_scale, gain, weights, before=None
):
    rows = hidden.shape[0]
    depth = weights[0].shape[0] if local else 4 * weights[0].shape[0]
    width = sum(w.shape[1] for w in weights[:3]) if local else weights[0].shape[1]
    outside = pl.BlockSpec(memory_space=pltpu.HBM)
    anywhere = pl.BlockSpec(memory_space=pl.ANY)
    inside = pl.BlockSpec(memory_space=pltpu.VMEM)
    summed = len(slots) - final
    flops = 4 * rows * depth * summed * width
    moved = 2 * (depth * width * summed + 2 * rows * depth * len(slots)) + 8 * rows * width
    outs = [jax.ShapeDtypeStruct((2 * rows, width), jnp.float32)]
    if final:
        outs.append(jax.ShapeDtypeStruct((2 * rows, depth), jnp.bfloat16))
    args = [hidden, *cames, scale, came_scale, gain, *weights]
    in_specs = [outside] + [anywhere] * len(cames)
    in_specs += [inside] * 3 + [outside] * (3 * local) + [anywhere] * (len(weights) - 3 * local)
    if before is not None:
        args.append(before)
        in_specs.append(inside)
    return pl.pallas_call(
        functools.partial(early_body, slots, guests, local, final),
        out_shape=outs,
        in_specs=in_specs,
        out_specs=[inside] * len(outs),
        scratch_shapes=[
            pltpu.VMEM((len(slots), rows, depth), jnp.bfloat16),
            pltpu.VMEM((rows, len(slots) * depth), jnp.bfloat16),
            pltpu.VMEM((summed, depth, width), jnp.bfloat16),
            pltpu.VMEM((summed, 2 * rows, depth), jnp.bfloat16),
            pltpu.SemaphoreType.DMA((len(guests) + len(slots) + len(weights),)),
        ],
        cost_estimate=pl.CostEstimate(flops=flops, bytes_accessed=moved, transcendentals=0),
        compiler_params=pltpu.CompilerParams(vmem_limit_bytes=60 * 2**20),
        name="early_slots",
    )(*args)


def late_body(first, splits, before, last_rows, *refs):
    pieces, refs = (refs[:4], refs[4:])
    kept, sent = (refs[: len(splits)], refs[len(splits) : 2 * len(splits)])
    wide, sems = refs[2 * len(splits) :]
    rows, width = (kept[0].shape[0], wide.shape[1])
    pieces = [p if p.shape[1] == width else p.at[:, pl.ds(first, width)] for p in pieces]
    for flight in started(piece_copies(pieces, wide, lax.axis_index("ctx")), sems, 0):
        flight.wait()
    at = 0
    for own, other, columns in zip(kept, sent, splits):
        cols = slice(at, at + columns)
        product = jnp.dot(last_rows[...], wide[:, cols], preferred_element_type=jnp.float32)
        product = product + before[:, first + at : first + at + columns]
        own[...] = product[:rows]
        other[...] = product[rows:].astype(jnp.bfloat16)
        at += columns


def late_slot(first, splits, before, last_rows, pieces):
    rows, depth = (last_rows.shape[0] // 2, last_rows.shape[1])
    anywhere = pl.BlockSpec(memory_space=pl.ANY)
    inside = pl.BlockSpec(memory_space=pltpu.VMEM)
    width = sum(splits)
    outs = [jax.ShapeDtypeStruct((rows, w), jnp.float32) for w in splits]
    outs += [jax.ShapeDtypeStruct((rows, w), jnp.bfloat16) for w in splits]
    return pl.pallas_call(
        functools.partial(late_body, first, splits),
        out_shape=outs,
        in_specs=[inside] * 2 + [anywhere] * 4,
        out_specs=[inside] * len(outs),
        scratch_shapes=[
            pltpu.VMEM((depth, width), jnp.bfloat16),
            pltpu.SemaphoreType.DMA((4,)),
        ],
        cost_estimate=pl.CostEstimate(
            flops=4 * rows * depth * width, bytes_accessed=2 * depth * width, transcendentals=0
        ),
        compiler_params=pltpu.CompilerParams(vmem_limit_bytes=10 * 2**20),
        name="late_slot",
    )(before, last_rows, *pieces)


def turned(tensor, cosine, sine_table):
    half = tensor.shape[-1] // 2
    return tensor * cosine + pltpu.roll(tensor, half, 1) * sine_table


def key_value_body(sums, back, bias, cosine, sine_table, out):
    head = out.shape[1] // 2
    total = sums[...] + back[:, : 2 * head].astype(jnp.float32) + bias[...]
    out[:, :head] = turned(total[:, :head], cosine[...], sine_table[...]).astype(jnp.bfloat16)
    out[:, head:] = total[:, head:].astype(jnp.bfloat16)


def attention_body(scale, first, sums, back, bias, cosine, sine_table, *refs):
    blocks, refs = (refs[:4], refs[4:])
    if first:
        done, *refs = refs
    out, keys, values = refs
    rows = out.shape[0]
    head = cosine.shape[1]
    slab = lax.axis_index("ctx")
    for block, flip in zip(blocks, (0, 1, 2, 3)):
        row = pl.multiple_of(jnp.bitwise_xor(slab, flip) * rows, rows)
        keys[pl.ds(row, rows), :] = block[:, :head]
        values[pl.ds(row, rows), :] = block[:, head:]
    total_keys = keys.shape[0]
    row_ids = slab * rows + lax.broadcasted_iota(jnp.int32, (rows, total_keys), 0)
    visible = lax.broadcasted_iota(jnp.int32, (rows, total_keys), 1) <= row_ids
    if first:
        out[:, :first] = done[...]
    for at in range(0, sums.shape[1], head):
        cols = pl.ds(at, head)
        skipped = back.shape[1] - sums.shape[1]
        query = sums[:, cols] + back[:, skipped + at : skipped + at + head].astype(jnp.float32)
        query = query + bias[:, first + at : first + at + head]
        query = turned(query, cosine[...], sine_table[...]).astype(jnp.bfloat16)
        scores = lax.dot_general(
            query, keys[...], (((1,), (1,)), ((), ())), preferred_element_type=jnp.float32
        )
        scores = jnp.where(visible, scores * scale, masked_score)
        exps = jnp.exp(scores - jnp.max(scores, axis=1, keepdims=True))
        length = jnp.sum(exps, axis=1, keepdims=True)
        mixed = jnp.dot(exps.astype(jnp.bfloat16), values[...], preferred_element_type=jnp.float32)
        out[:, first + at : first + at + head] = (mixed / length).astype(jnp.bfloat16)


def attention(sums, back, bias, cosine, sine_table, blocks, done=None):
    rows, width = sums.shape
    head = cosine.shape[1]
    first = 0 if done is None else done.shape[1]
    inside = pl.BlockSpec(memory_space=pltpu.VMEM)
    args = [sums, back, bias, cosine, sine_table, *blocks]
    if first:
        args.append(done)
    total = 4 * rows * rows * (width // head)
    return pl.pallas_call(
        functools.partial(attention_body, head ** (-0.5), first),
        out_shape=jax.ShapeDtypeStruct((rows, first + width), jnp.bfloat16),
        in_specs=[inside] * len(args),
        out_specs=inside,
        scratch_shapes=[
            pltpu.VMEM((4 * rows, head), jnp.bfloat16),
            pltpu.VMEM((4 * rows, head), jnp.bfloat16),
        ],
        cost_estimate=pl.CostEstimate(
            flops=4 * total * head, bytes_accessed=8 * rows * width, transcendentals=total
        ),
        compiler_params=pltpu.CompilerParams(vmem_limit_bytes=12 * 2**20),
        name="attention",
    )(*args)


def planned(hidden, norm_gain, w_query, w_key, w_value, bias_query, bias_key, bias_value):
    tokens = hidden[0]
    rows = tokens.shape[0]
    depth = w_query.shape[0]
    head = w_key.shape[1]
    line, slab = (lax.axis_index("line"), lax.axis_index("ctx"))
    inner = (line == 1) | (line == 2)
    swap = [(0, 1), (1, 0)]
    ends = [(0, 1), (1, 0), (2, 3), (3, 2)]
    middle = [(1, 2), (2, 1)]
    outward = [(1, 0), (2, 3)]
    across = [(i, i ^ 2) for i in range(4)]
    beside = [(i, i ^ 1) for i in range(4)]
    held = lax.optimization_barrier
    cut = depth // 8
    parts_1 = ((0, 0, depth), (1, 0, cut))
    parts_2 = ((1, cut, 7 * cut), (2, 0, 5 * cut))
    parts_3 = ((2, 5 * cut, 3 * cut), (3, 0, depth))
    mine, sent_1 = pack(tokens, depth, (parts_1,), (w_key, w_value, w_query))
    kv_width = 2 * head
    half = kv_width + w_query.shape[1] // 2
    rest = mine.shape[1] - half
    second = lax.ppermute(mine, "line", ends)
    third_in = lax.ppermute(mine, "line", middle)
    came_1 = lax.ppermute(sent_1, "pair", swap)
    (sent_2,) = pack(tokens, depth, (parts_2,))
    gain = norm_gain.reshape(1, -1)
    bias_kv = jnp.concatenate([bias_key, bias_value]).reshape(1, -1).astype(jnp.float32)
    bias_q = bias_query.reshape(1, -1).astype(jnp.float32)
    positions = slab * rows + jnp.arange(rows, dtype=jnp.int32)
    cosine, sine_table = rotary_tables(positions, head)
    cosine = jnp.concatenate([cosine, cosine], axis=-1).reshape(rows, head)
    sine_table = jnp.concatenate([-sine_table, sine_table], axis=-1).reshape(rows, head)
    small = (gain, bias_kv, bias_q, cosine, sine_table)
    second, third_in, came_1, sent_2, small, later_tokens = held(
        (second, third_in, came_1, sent_2, small, tokens)
    )
    gain, bias_kv, bias_q, cosine, sine_table = small
    fourth_in = lax.ppermute(second, "line", middle)
    third_out = lax.ppermute(third_in, "line", outward)
    second_far = lax.ppermute(second, "ctx", across)
    came_2 = lax.ppermute(sent_2, "pair", swap)
    second_side = lax.ppermute(second, "ctx", beside)
    sent_3, scale, line_scale = prepare(later_tokens, depth, (parts_3,))
    came_scale = lax.ppermute(line_scale, "pair", swap)
    third = jnp.where(inner, third_in, third_out)
    fourth_in, came_scale, third, second_far, came_2, second_side, sent_3, scale = held(
        (fourth_in, came_scale, third, second_far, came_2, second_side, sent_3, scale)
    )
    fourth_out = lax.ppermute(fourth_in, "line", outward)
    third_far = lax.ppermute(third, "ctx", across)
    came_3 = lax.ppermute(sent_3, "pair", swap)
    second_corner = lax.ppermute(second_far, "ctx", beside)
    third_side = lax.ppermute(third, "ctx", beside)
    before = early_slots(
        (0, 1),
        ((0, 0, 9 * cut), (1, 0, 7 * cut)),
        True,
        False,
        tokens,
        (came_1, came_2),
        scale,
        came_scale,
        gain,
        [w_key, w_value, w_query, second, second_far, second_side, second_corner],
    )[0]
    fourth = jnp.where(inner, fourth_in, fourth_out)
    fourth, third_far, came_3, third_side, before = held(
        (fourth, third_far, came_3, third_side, before)
    )
    fourth_far_1 = lax.ppermute(fourth[:, :half], "ctx", across)
    third_corner = lax.ppermute(third_far, "ctx", beside)
    fourth_side = lax.ppermute(fourth, "ctx", beside)
    before, last_rows = early_slots(
        (2, 3),
        ((0, 7 * cut, 5 * cut), (1, 0, 11 * cut)),
        False,
        True,
        tokens,
        (came_2, came_3),
        scale,
        came_scale,
        gain,
        [third, third_far, third_side, third_corner],
        before,
    )
    fourth_far_1, fourth, before, last_rows, fourth_side = held(
        (fourth_far_1, fourth, before, last_rows, fourth_side)
    )
    fourth_far_2 = lax.ppermute(fourth[:, half:], "ctx", across)
    fourth_corner_1 = lax.ppermute(fourth_far_1, "ctx", beside)
    kv_sums, q_sums_1, back_kv, back_1 = late_slot(
        0,
        (kv_width, half - kv_width),
        before,
        last_rows,
        (fourth, fourth_far_1, fourth_side, fourth_corner_1),
    )
    back_kv, back_1, fourth_far_2 = held((back_kv, back_1, fourth_far_2))
    back_kv = lax.ppermute(back_kv, "pair", swap)
    back_1 = lax.ppermute(back_1, "pair", swap)
    fourth_corner_2 = lax.ppermute(fourth_far_2, "ctx", beside)
    back_kv, fourth_corner_2 = held((back_kv, fourth_corner_2))
    q_sums_2, back_2 = late_slot(
        half,
        (rest,),
        before,
        last_rows,
        (fourth, fourth_far_2, fourth_side, fourth_corner_2),
    )
    back_2 = lax.ppermute(back_2, "pair", swap)

    inside = pl.BlockSpec(memory_space=pltpu.VMEM)
    key_value = pl.pallas_call(
        key_value_body,
        out_shape=jax.ShapeDtypeStruct((rows, kv_width), jnp.bfloat16),
        in_specs=[inside] * 5,
        out_specs=inside,
        compiler_params=pltpu.CompilerParams(vmem_limit_bytes=4 * 2**20),
        name="key_value",
    )(kv_sums, back_kv, bias_kv, cosine, sine_table)
    kv_across = lax.ppermute(key_value, "ctx", [(0, 2), (1, 3)])
    kv_beside = lax.ppermute(key_value, "ctx", beside)
    kv_corner = lax.ppermute(kv_across, "ctx", [(2, 3), (3, 2)])
    blocks = (key_value, kv_beside, kv_across, kv_corner)
    attended = attention(q_sums_1, back_1, bias_q, cosine, sine_table, blocks)
    attended = attention(q_sums_2, back_2, bias_q, cosine, sine_table, blocks, attended)
    return attended[None]


def shards(hidden, norm_gain, w_query, w_key, w_value, bias_query, bias_key, bias_value):
    if lax.axis_size("line") == 4 and lax.axis_size("ctx") == 4:
        return planned(
            hidden, norm_gain, w_query, w_key, w_value, bias_query, bias_key, bias_value
        )
    local_rows = hidden.shape[1]
    head_width = w_key.shape[1]
    query_width = w_query.shape[1]
    query_heads = query_width // head_width
    sums = project(hidden[0], norm_gain, w_query, w_key, w_value)
    query_sums = sums[:, :query_width]
    key_sums = sums[:, query_width : query_width + head_width]
    value_sums = sums[:, query_width + head_width :]
    slab_index = lax.axis_index("ctx")
    slab_count = lax.axis_size("ctx")
    positions = slab_index * local_rows + jnp.arange(local_rows, dtype=jnp.int32)
    cosine, sine_table = rotary_tables(positions, head_width)
    queries = rotate(
        (query_sums + bias_query.astype(jnp.float32)).reshape(local_rows, query_heads, head_width),
        cosine,
        sine_table,
    ).astype(jnp.bfloat16)
    keys = rotate((key_sums + bias_key.astype(jnp.float32))[:, None, :], cosine, sine_table)[
        :, 0, :
    ].astype(jnp.bfloat16)
    values = (value_sums + bias_value.astype(jnp.float32)).astype(jnp.bfloat16)
    score_scale = head_width ** (-0.5)
    start_state = (
        jnp.full((query_heads, local_rows), masked_score, jnp.float32),
        jnp.zeros((query_heads, local_rows), jnp.float32),
        jnp.zeros((query_heads, local_rows, head_width), jnp.float32),
    )
    key_value = jnp.stack([keys, values])
    column_ids = jnp.arange(local_rows, dtype=jnp.int32)
    causal = column_ids[None, :] <= column_ids[:, None]
    running = attend(queries, score_scale, start_state, key_value, causal[None])

    def forward_step(step_number, state):
        held_running, blocks = state
        blocks = shifted(blocks, "ctx", 1)
        visible = step_number <= slab_index
        held_running = attend(queries, score_scale, held_running, blocks, visible)
        return (held_running, blocks)

    running, key_value = lax.fori_loop(1, slab_count, forward_step, (running, key_value))
    row_peak, row_total, weighted = running
    attended = (
        (weighted / row_total[..., None])
        .transpose(1, 0, 2)
        .reshape(local_rows, query_width)
        .astype(jnp.bfloat16)
    )
    return attended[None]


def solution(mesh):
    groups, slabs = (mesh.shape["fsdp"], mesh.shape["ctx"])
    pairs = Mesh(mesh.devices.reshape(groups // 2, 2, slabs), ("line", "pair", "ctx"))
    both = ("line", "pair")
    in_specs = (
        P(both, "ctx", None),
        P(),
        P(both, None),
        P(both, None),
        P(both, None),
        P(),
        P(),
        P(),
    )
    out_specs = P(both, "ctx", None)
    return jax.shard_map(shards, mesh=pairs, in_specs=in_specs, out_specs=out_specs, check_vma=False)
```

```python
import functools
import math

import jax
import jax.numpy as jnp
from jax import lax
from jax.experimental import pallas as pl
from jax.experimental.pallas import tpu as pltpu
from jax.sharding import Mesh, PartitionSpec as P

epsilon = 1e-06
rotary_base = 1000000.0
masked_score = -1e30


def shifted(value, axis, steps):
    count = lax.axis_size(axis)
    first, last = (max(0, -steps), min(count, count - steps))
    return lax.ppermute(value, axis, [(source, source + steps) for source in range(first, last)])


def rotary_tables(positions, head_width):
    half_width = head_width // 2
    frequency = jnp.exp(
        -(jnp.arange(half_width, dtype=jnp.float32) * (2.0 / head_width)) * math.log(rotary_base)
    )
    angles = positions.astype(jnp.float32)[:, None] * frequency[None, :]
    return (jnp.cos(angles)[:, None, :], jnp.sin(angles)[:, None, :])


def rotate(tensor, cosine, sine_table):
    half_width = tensor.shape[-1] // 2
    lower_half = tensor[..., :half_width]
    upper_half = tensor[..., half_width:]
    return jnp.concatenate(
        [
            lower_half * cosine - upper_half * sine_table,
            upper_half * cosine + lower_half * sine_table,
        ],
        axis=-1,
    )


def attend(work_queries, score_scale, running, key_value, visible):
    row_peak, row_total, weighted = running
    scores = (
        jnp.einsum("qhd,kd->hqk", work_queries, key_value[0], preferred_element_type=jnp.float32)
        * score_scale
    )
    scores = jnp.where(visible, scores, masked_score)
    new_peak = jnp.maximum(row_peak, jnp.max(scores, axis=-1))
    factor = jnp.exp(row_peak - new_peak)
    expsum = jnp.exp(scores - new_peak[..., None])
    row_total = row_total * factor + jnp.sum(expsum, axis=-1)
    weights = expsum.astype(jnp.bfloat16)
    weighted = weighted * factor[..., None] + jnp.einsum(
        "hqk,kd->hqd", weights, key_value[1], preferred_element_type=jnp.float32
    )
    return (new_peak, row_total, weighted)


def row_scale(inputs):
    floats = inputs.astype(jnp.float32)
    return lax.rsqrt(jnp.mean(floats * floats, axis=-1, keepdims=True) + epsilon)


def scaled_rows(inputs, scale, gain):
    return (inputs.astype(jnp.float32) * scale * gain.astype(jnp.float32)).astype(jnp.bfloat16)


def project(hidden, norm_gain, w_query, w_key, w_value):
    local_rows, width = hidden.shape
    lines, slabs = (lax.axis_size("line"), lax.axis_size("ctx"))
    depth = w_query.shape[0]
    side = lax.axis_index("pair")
    swap = [(0, 1), (1, 0)]
    split = hidden.reshape(local_rows, lines, 2, depth)
    half_width = lines * depth

    def half(array, which):
        return lax.dynamic_index_in_dim(array, which, array.ndim - 2, keepdims=False)

    sent = half(split, 1 - side).reshape(local_rows, half_width)
    kept = half(split, side).reshape(local_rows, half_width)
    gain = half(norm_gain.reshape(lines, 2, depth), side).reshape(half_width)
    came = lax.ppermute(sent, "pair", swap)
    scale = row_scale(hidden)
    came_scale = lax.ppermute(scale, "pair", swap)
    piece = depth // slabs
    start = lax.axis_index("ctx") * piece
    packed = jnp.concatenate(
        [lax.dynamic_slice_in_dim(w, start, piece, 0) for w in (w_query, w_key, w_value)], axis=1
    )
    weights = lax.all_gather(packed, ("line", "ctx"), axis=0, tiled=True)
    rows = jnp.concatenate(
        [scaled_rows(kept, scale, gain), scaled_rows(came, came_scale, gain)], axis=0
    )
    sums = jnp.dot(rows, weights, preferred_element_type=jnp.float32)
    back = lax.ppermute(sums[local_rows:].astype(jnp.bfloat16), "pair", swap)
    return sums[:local_rows] + back.astype(jnp.float32)


def normed_rows(block, scale, gain):
    return (block.astype(jnp.float32) * scale * gain).astype(jnp.bfloat16)


def slot_lines():
    line = lax.axis_index("line")
    inner = (line == 1) | (line == 2)
    third = jnp.where(inner, line ^ 3, line ^ 2)
    fourth = jnp.where(inner, line ^ 2, line ^ 3)
    return [line, line ^ 1, third, fourth]


def started(copies, sems, first):
    flights = [
        pltpu.make_async_copy(source, target, sems.at[first + number])
        for number, (source, target) in enumerate(copies)
    ]
    for flight in flights:
        flight.start()
    return flights


def piece_copies(pieces, wide, slab):
    piece = pieces[0].shape[0]
    return [
        (source, wide.at[pl.ds(pl.multiple_of(jnp.bitwise_xor(slab, flip) * piece, piece), piece), :])
        for source, flip in zip(pieces, (0, 2, 1, 3))
    ]


def pack_body(sent_parts, weights, depth, *refs):
    tokens, refs = (refs[0], refs[1:])
    sources, refs = (refs[:weights], refs[weights:])
    sems = refs[-1]
    copies = []
    outs = refs[:-1]
    if weights:
        mine, outs = (outs[0], outs[1:])
        piece = mine.shape[0]
        row = pl.multiple_of(lax.axis_index("ctx") * piece, piece)
        at = 0
        for source in sources:
            target = mine.at[:, pl.ds(at, source.shape[1])]
            copies.append((source.at[pl.ds(row, piece), :], target))
            at += source.shape[1]
    lines = slot_lines()
    other = 1 - lax.axis_index("pair")
    for out, parts in zip(outs, sent_parts):
        at = 0
        for slot, first, count in parts:
            column = pl.multiple_of((2 * lines[slot] + other) * depth + first, 128)
            copies.append((tokens.at[:, pl.ds(column, count)], out.at[:, pl.ds(at, count)]))
            at += count
    for flight in started(copies, sems, 0):
        flight.wait()


def pack(tokens, depth, sent_parts, weights=()):
    rows = tokens.shape[0]
    outside = pl.BlockSpec(memory_space=pltpu.HBM)
    outs = []
    if weights:
        piece = weights[0].shape[0] // 4
        outs.append(jax.ShapeDtypeStruct((piece, sum(w.shape[1] for w in weights)), jnp.bfloat16))
    for parts in sent_parts:
        outs.append(jax.ShapeDtypeStruct((rows, sum(p[2] for p in parts)), jnp.bfloat16))
    copies = len(weights) + sum(len(parts) for parts in sent_parts)
    moved = 4 * sum(out.shape[0] * out.shape[1] for out in outs)
    return pl.pallas_call(
        functools.partial(pack_body, sent_parts, len(weights), depth),
        out_shape=outs,
        in_specs=[outside] * (1 + len(weights)),
        out_specs=[pl.BlockSpec(memory_space=pltpu.VMEM)] * len(outs),
        scratch_shapes=[pltpu.SemaphoreType.DMA((copies,))],
        cost_estimate=pl.CostEstimate(flops=0, bytes_accessed=0, transcendentals=0),
        name="pack",
    )(tokens, *weights)


def prepare_body(sent_parts, depth, tokens, *refs):
    outs, refs = (refs[: len(sent_parts)], refs[len(sent_parts) :])
    column_scale, line_scale, held, sems = refs
    rows, width = held.shape
    lines = slot_lines()
    other = 1 - lax.axis_index("pair")
    loads = [
        (tokens.at[:, pl.ds(at, depth)], held.at[:, pl.ds(at, depth)])
        for at in range(0, width, depth)
    ]
    loads = started(loads, sems, 0)
    copies = []
    for out, parts in zip(outs, sent_parts):
        at = 0
        for slot, first, count in parts:
            column = pl.multiple_of((2 * lines[slot] + other) * depth + first, 128)
            copies.append((tokens.at[:, pl.ds(column, count)], out.at[:, pl.ds(at, count)]))
            at += count
    copies = started(copies, sems, len(loads))
    squares = jnp.zeros((rows, 128), jnp.float32)
    for number, load in enumerate(loads):
        load.wait()
        for at in range(number * depth, (number + 1) * depth, 128):
            floats = held[:, at : at + 128].astype(jnp.float32)
            squares = squares + floats * floats
    mean = jnp.sum(squares, axis=1, keepdims=True) / width
    wide = jnp.broadcast_to(lax.rsqrt(mean + epsilon), (rows, 128))
    column_scale[...] = wide
    line_scale[...] = jnp.transpose(wide)[:1]
    for copy in copies:
        copy.wait()


def prepare(tokens, depth, sent_parts):
    rows, width = tokens.shape
    outs = [
        jax.ShapeDtypeStruct((rows, sum(p[2] for p in parts)), jnp.bfloat16)
        for parts in sent_parts
    ]
    outs.append(jax.ShapeDtypeStruct((rows, 128), jnp.float32))
    outs.append(jax.ShapeDtypeStruct((1, rows), jnp.float32))
    copies = width // depth + sum(len(parts) for parts in sent_parts)
    return pl.pallas_call(
        functools.partial(prepare_body, sent_parts, depth),
        out_shape=outs,
        in_specs=[pl.BlockSpec(memory_space=pltpu.HBM)],
        out_specs=[pl.BlockSpec(memory_space=pltpu.VMEM)] * len(outs),
        scratch_shapes=[
            pltpu.VMEM((rows, width), jnp.bfloat16),
            pltpu.SemaphoreType.DMA((copies,)),
        ],
        cost_estimate=pl.CostEstimate(flops=0, bytes_accessed=0, transcendentals=0),
        compiler_params=pltpu.CompilerParams(vmem_limit_bytes=10 * 2**20),
        name="prepare",
    )(tokens)


def early_body(slots, guests, local, final, hidden, *refs):
    count = 1 + max(part[0] for part in guests)
    cames, refs = (refs[:count], refs[count:])
    scale, came_scale, gain, *refs = refs
    summed = slots[:-1] if final else slots
    number = 3 * local + 4 * (len(summed) - local)
    weights, refs = (refs[:number], refs[number:])
    before = None
    if not local:
        before, *refs = refs
    total, *refs = refs
    if final:
        last_rows, *refs = refs
    held, guest, wide, stacked, sems = refs
    _, rows, depth = held.shape
    slab = lax.axis_index("ctx")
    blocks = [2 * which + lax.axis_index("pair") for which in slot_lines()]
    number = 0
    parts = []
    at = 0
    for source, first, width in guests:
        parts.append(
            (cames[source].at[:, pl.ds(first, width)], guest.at[:, pl.ds(at, width)])
        )
        at += width
    guest_flights = started(parts, sems, number)
    number += len(parts)
    flights = []
    pending = list(weights)
    for place, slot in enumerate(slots):
        column = pl.multiple_of(blocks[slot] * depth, depth)
        copies = [(hidden.at[:, pl.ds(column, depth)], held.at[place])]
        if slot == 0:
            at = 0
            for _ in range(3):
                weight = pending.pop(0)
                copies.append((weight, wide.at[place, :, pl.ds(at, weight.shape[1])]))
                at += weight.shape[1]
        elif slot in summed:
            copies += piece_copies(pending[:4], wide.at[place], slab)
            pending = pending[4:]
        flights.append(started(copies, sems, number))
        number += len(copies)
    turned_scale = jnp.transpose(jnp.broadcast_to(came_scale[...], (128, rows)))[:, :1]
    for flight in guest_flights:
        flight.wait()
    width = total.shape[1]
    step = 256
    for place, slot in enumerate(slots):
        for flight in flights[place]:
            flight.wait()
        column = pl.multiple_of(blocks[slot] * depth, depth)
        row_gain = gain[:, pl.ds(column, depth)].astype(jnp.float32)
        target = stacked.at[place] if slot in summed else last_rows
        target[:rows] = normed_rows(held[place], scale[:, :1], row_gain)
        target[rows:] = normed_rows(
            guest[:, place * depth : (place + 1) * depth], turned_scale, row_gain
        )
        if slot not in summed:
            continue
        for at in range(0, width, step):
            cols = pl.ds(at, step)
            product = jnp.dot(
                stacked[place], wide[place, :, cols], preferred_element_type=jnp.float32
            )
            if place > 0:
                product = product + total[:, cols]
            elif before is not None:
                product = product + before[:, cols]
            total[:, cols] = product


def early_slots(
    slots, guests, local, final, hidden, cames, scale, came_scale, gain, weights, before=None
):
    rows = hidden.shape[0]
    depth = weights[0].shape[0] if local else 4 * weights[0].shape[0]
    width = sum(w.shape[1] for w in weights[:3]) if local else weights[0].shape[1]
    outside = pl.BlockSpec(memory_space=pltpu.HBM)
    anywhere = pl.BlockSpec(memory_space=pl.ANY)
    inside = pl.BlockSpec(memory_space=pltpu.VMEM)
    summed = len(slots) - final
    flops = 4 * rows * depth * summed * width
    moved = 2 * (depth * width * summed + 2 * rows * depth * len(slots)) + 8 * rows * width
    outs = [jax.ShapeDtypeStruct((2 * rows, width), jnp.float32)]
    if final:
        outs.append(jax.ShapeDtypeStruct((2 * rows, depth), jnp.bfloat16))
    args = [hidden, *cames, scale, came_scale, gain, *weights]
    in_specs = [outside] + [anywhere] * len(cames)
    in_specs += [inside] * 3 + [outside] * (3 * local) + [anywhere] * (len(weights) - 3 * local)
    if before is not None:
        args.append(before)
        in_specs.append(inside)
    return pl.pallas_call(
        functools.partial(early_body, slots, guests, local, final),
        out_shape=outs,
        in_specs=in_specs,
        out_specs=[inside] * len(outs),
        scratch_shapes=[
            pltpu.VMEM((len(slots), rows, depth), jnp.bfloat16),
            pltpu.VMEM((rows, len(slots) * depth), jnp.bfloat16),
            pltpu.VMEM((summed, depth, width), jnp.bfloat16),
            pltpu.VMEM((summed, 2 * rows, depth), jnp.bfloat16),
            pltpu.SemaphoreType.DMA((len(guests) + len(slots) + len(weights),)),
        ],
        cost_estimate=pl.CostEstimate(flops=flops, bytes_accessed=moved, transcendentals=0),
        compiler_params=pltpu.CompilerParams(vmem_limit_bytes=24 * 2**20),
        name="early_slots",
    )(*args)


def late_body(first, splits, before, last_rows, *refs):
    pieces, refs = (refs[:4], refs[4:])
    kept, sent = (refs[: len(splits)], refs[len(splits) : 2 * len(splits)])
    wide, sems = refs[2 * len(splits) :]
    rows, width = (kept[0].shape[0], wide.shape[1])
    pieces = [p if p.shape[1] == width else p.at[:, pl.ds(first, width)] for p in pieces]
    for flight in started(piece_copies(pieces, wide, lax.axis_index("ctx")), sems, 0):
        flight.wait()
    at = 0
    for own, other, columns in zip(kept, sent, splits):
        cols = slice(at, at + columns)
        product = jnp.dot(last_rows[...], wide[:, cols], preferred_element_type=jnp.float32)
        product = product + before[:, first + at : first + at + columns]
        own[...] = product[:rows]
        other[...] = product[rows:].astype(jnp.bfloat16)
        at += columns


def late_slot(first, splits, before, last_rows, pieces):
    rows, depth = (last_rows.shape[0] // 2, last_rows.shape[1])
    anywhere = pl.BlockSpec(memory_space=pl.ANY)
    inside = pl.BlockSpec(memory_space=pltpu.VMEM)
    width = sum(splits)
    outs = [jax.ShapeDtypeStruct((rows, w), jnp.float32) for w in splits]
    outs += [jax.ShapeDtypeStruct((rows, w), jnp.bfloat16) for w in splits]
    return pl.pallas_call(
        functools.partial(late_body, first, splits),
        out_shape=outs,
        in_specs=[inside] * 2 + [anywhere] * 4,
        out_specs=[inside] * len(outs),
        scratch_shapes=[
            pltpu.VMEM((depth, width), jnp.bfloat16),
            pltpu.SemaphoreType.DMA((4,)),
        ],
        cost_estimate=pl.CostEstimate(
            flops=4 * rows * depth * width, bytes_accessed=2 * depth * width, transcendentals=0
        ),
        compiler_params=pltpu.CompilerParams(vmem_limit_bytes=10 * 2**20),
        name="late_slot",
    )(before, last_rows, *pieces)


def turned(tensor, cosine, sine_table):
    half = tensor.shape[-1] // 2
    return tensor * cosine + pltpu.roll(tensor, half, 1) * sine_table


def key_value_body(sums, back, bias, cosine, sine_table, out):
    head = out.shape[1] // 2
    total = sums[...] + back[:, : 2 * head].astype(jnp.float32) + bias[...]
    out[:, :head] = turned(total[:, :head], cosine[...], sine_table[...]).astype(jnp.bfloat16)
    out[:, head:] = total[:, head:].astype(jnp.bfloat16)


def attention_body(scale, first, sums, back, bias, cosine, sine_table, *refs):
    blocks, refs = (refs[:4], refs[4:])
    if first:
        done, *refs = refs
    out, keys, values = refs
    rows = out.shape[0]
    head = cosine.shape[1]
    slab = lax.axis_index("ctx")
    for block, flip in zip(blocks, (0, 1, 2, 3)):
        row = pl.multiple_of(jnp.bitwise_xor(slab, flip) * rows, rows)
        keys[pl.ds(row, rows), :] = block[:, :head]
        values[pl.ds(row, rows), :] = block[:, head:]
    total_keys = keys.shape[0]
    row_ids = slab * rows + lax.broadcasted_iota(jnp.int32, (rows, total_keys), 0)
    visible = lax.broadcasted_iota(jnp.int32, (rows, total_keys), 1) <= row_ids
    if first:
        out[:, :first] = done[...]
    for at in range(0, sums.shape[1], head):
        cols = pl.ds(at, head)
        skipped = back.shape[1] - sums.shape[1]
        query = sums[:, cols] + back[:, skipped + at : skipped + at + head].astype(jnp.float32)
        query = query + bias[:, first + at : first + at + head]
        query = turned(query, cosine[...], sine_table[...]).astype(jnp.bfloat16)
        scores = lax.dot_general(
            query, keys[...], (((1,), (1,)), ((), ())), preferred_element_type=jnp.float32
        )
        scores = jnp.where(visible, scores * scale, masked_score)
        exps = jnp.exp(scores - jnp.max(scores, axis=1, keepdims=True))
        length = jnp.sum(exps, axis=1, keepdims=True)
        mixed = jnp.dot(exps.astype(jnp.bfloat16), values[...], preferred_element_type=jnp.float32)
        out[:, first + at : first + at + head] = (mixed / length).astype(jnp.bfloat16)


def attention(sums, back, bias, cosine, sine_table, blocks, done=None):
    rows, width = sums.shape
    head = cosine.shape[1]
    first = 0 if done is None else done.shape[1]
    inside = pl.BlockSpec(memory_space=pltpu.VMEM)
    args = [sums, back, bias, cosine, sine_table, *blocks]
    if first:
        args.append(done)
    total = 4 * rows * rows * (width // head)
    return pl.pallas_call(
        functools.partial(attention_body, head ** (-0.5), first),
        out_shape=jax.ShapeDtypeStruct((rows, first + width), jnp.bfloat16),
        in_specs=[inside] * len(args),
        out_specs=inside,
        scratch_shapes=[
            pltpu.VMEM((4 * rows, head), jnp.bfloat16),
            pltpu.VMEM((4 * rows, head), jnp.bfloat16),
        ],
        cost_estimate=pl.CostEstimate(
            flops=4 * total * head, bytes_accessed=8 * rows * width, transcendentals=total
        ),
        compiler_params=pltpu.CompilerParams(vmem_limit_bytes=12 * 2**20),
        name="attention",
    )(*args)


def planned(hidden, norm_gain, w_query, w_key, w_value, bias_query, bias_key, bias_value):
    tokens = hidden[0]
    rows = tokens.shape[0]
    depth = w_query.shape[0]
    head = w_key.shape[1]
    line, slab = (lax.axis_index("line"), lax.axis_index("ctx"))
    inner = (line == 1) | (line == 2)
    swap = [(0, 1), (1, 0)]
    ends = [(0, 1), (1, 0), (2, 3), (3, 2)]
    middle = [(1, 2), (2, 1)]
    outward = [(1, 0), (2, 3)]
    across = [(i, i ^ 2) for i in range(4)]
    beside = [(i, i ^ 1) for i in range(4)]
    held = lax.optimization_barrier
    cut = depth // 8
    parts_1 = ((0, 0, depth), (1, 0, cut))
    parts_2 = ((1, cut, 7 * cut), (2, 0, 5 * cut))
    parts_3 = ((2, 5 * cut, 3 * cut), (3, 0, depth))
    mine, sent_1 = pack(tokens, depth, (parts_1,), (w_key, w_value, w_query))
    kv_width = 2 * head
    half = kv_width + w_query.shape[1] // 2
    rest = mine.shape[1] - half
    second = lax.ppermute(mine, "line", ends)
    third_in = lax.ppermute(mine, "line", middle)
    came_1 = lax.ppermute(sent_1, "pair", swap)
    (sent_2,) = pack(tokens, depth, (parts_2,))
    gain = norm_gain.reshape(1, -1)
    bias_kv = jnp.concatenate([bias_key, bias_value]).reshape(1, -1).astype(jnp.float32)
    bias_q = bias_query.reshape(1, -1).astype(jnp.float32)
    positions = slab * rows + jnp.arange(rows, dtype=jnp.int32)
    cosine, sine_table = rotary_tables(positions, head)
    cosine = jnp.concatenate([cosine, cosine], axis=-1).reshape(rows, head)
    sine_table = jnp.concatenate([-sine_table, sine_table], axis=-1).reshape(rows, head)
    small = (gain, bias_kv, bias_q, cosine, sine_table)
    second, third_in, came_1, sent_2, small, later_tokens = held(
        (second, third_in, came_1, sent_2, small, tokens)
    )
    gain, bias_kv, bias_q, cosine, sine_table = small
    fourth_in = lax.ppermute(second, "line", middle)
    third_out = lax.ppermute(third_in, "line", outward)
    second_far = lax.ppermute(second, "ctx", across)
    came_2 = lax.ppermute(sent_2, "pair", swap)
    second_side = lax.ppermute(second, "ctx", beside)
    sent_3, scale, line_scale = prepare(later_tokens, depth, (parts_3,))
    came_scale = lax.ppermute(line_scale, "pair", swap)
    third = jnp.where(inner, third_in, third_out)
    fourth_in, came_scale, third, second_far, came_2, second_side, sent_3, scale = held(
        (fourth_in, came_scale, third, second_far, came_2, second_side, sent_3, scale)
    )
    fourth_out = lax.ppermute(fourth_in, "line", outward)
    third_far = lax.ppermute(third, "ctx", across)
    came_3 = lax.ppermute(sent_3, "pair", swap)
    second_corner = lax.ppermute(second_far, "ctx", beside)
    third_side = lax.ppermute(third, "ctx", beside)
    before = early_slots(
        (0, 1),
        ((0, 0, 9 * cut), (1, 0, 7 * cut)),
        True,
        False,
        tokens,
        (came_1, came_2),
        scale,
        came_scale,
        gain,
        [w_key, w_value, w_query, second, second_far, second_side, second_corner],
    )[0]
    fourth = jnp.where(inner, fourth_in, fourth_out)
    fourth, third_far, came_3, third_side, before = held(
        (fourth, third_far, came_3, third_side, before)
    )
    fourth_far_1 = lax.ppermute(fourth[:, :half], "ctx", across)
    third_corner = lax.ppermute(third_far, "ctx", beside)
    fourth_side = lax.ppermute(fourth, "ctx", beside)
    before, last_rows = early_slots(
        (2, 3),
        ((0, 7 * cut, 5 * cut), (1, 0, 11 * cut)),
        False,
        True,
        tokens,
        (came_2, came_3),
        scale,
        came_scale,
        gain,
        [third, third_far, third_side, third_corner],
        before,
    )
    fourth_far_1, fourth, before, last_rows, fourth_side = held(
        (fourth_far_1, fourth, before, last_rows, fourth_side)
    )
    fourth_far_2 = lax.ppermute(fourth[:, half:], "ctx", across)
    fourth_corner_1 = lax.ppermute(fourth_far_1, "ctx", beside)
    kv_sums, q_sums_1, back_kv, back_1 = late_slot(
        0,
        (kv_width, half - kv_width),
        before,
        last_rows,
        (fourth, fourth_far_1, fourth_side, fourth_corner_1),
    )
    back_kv = lax.ppermute(back_kv, "pair", swap)
    back_1 = lax.ppermute(back_1, "pair", swap)
    back_kv, fourth_far_2 = held((back_kv, fourth_far_2))
    fourth_corner_2 = lax.ppermute(fourth_far_2, "ctx", beside)
    q_sums_2, back_2 = late_slot(
        half,
        (rest,),
        before,
        last_rows,
        (fourth, fourth_far_2, fourth_side, fourth_corner_2),
    )
    back_2 = lax.ppermute(back_2, "pair", swap)

    inside = pl.BlockSpec(memory_space=pltpu.VMEM)
    key_value = pl.pallas_call(
        key_value_body,
        out_shape=jax.ShapeDtypeStruct((rows, kv_width), jnp.bfloat16),
        in_specs=[inside] * 5,
        out_specs=inside,
        compiler_params=pltpu.CompilerParams(vmem_limit_bytes=4 * 2**20),
        name="key_value",
    )(kv_sums, back_kv, bias_kv, cosine, sine_table)
    kv_across = lax.ppermute(key_value, "ctx", [(0, 2), (1, 3)])
    kv_beside = lax.ppermute(key_value, "ctx", beside)
    kv_corner = lax.ppermute(kv_across, "ctx", [(2, 3), (3, 2)])
    blocks = (key_value, kv_beside, kv_across, kv_corner)
    attended = attention(q_sums_1, back_1, bias_q, cosine, sine_table, blocks)
    attended = attention(q_sums_2, back_2, bias_q, cosine, sine_table, blocks, attended)
    return attended[None]


def shards(hidden, norm_gain, w_query, w_key, w_value, bias_query, bias_key, bias_value):
    if lax.axis_size("line") == 4 and lax.axis_size("ctx") == 4:
        return planned(
            hidden, norm_gain, w_query, w_key, w_value, bias_query, bias_key, bias_value
        )
    local_rows = hidden.shape[1]
    head_width = w_key.shape[1]
    query_width = w_query.shape[1]
    query_heads = query_width // head_width
    sums = project(hidden[0], norm_gain, w_query, w_key, w_value)
    query_sums = sums[:, :query_width]
    key_sums = sums[:, query_width : query_width + head_width]
    value_sums = sums[:, query_width + head_width :]
    slab_index = lax.axis_index("ctx")
    slab_count = lax.axis_size("ctx")
    positions = slab_index * local_rows + jnp.arange(local_rows, dtype=jnp.int32)
    cosine, sine_table = rotary_tables(positions, head_width)
    queries = rotate(
        (query_sums + bias_query.astype(jnp.float32)).reshape(local_rows, query_heads, head_width),
        cosine,
        sine_table,
    ).astype(jnp.bfloat16)
    keys = rotate((key_sums + bias_key.astype(jnp.float32))[:, None, :], cosine, sine_table)[
        :, 0, :
    ].astype(jnp.bfloat16)
    values = (value_sums + bias_value.astype(jnp.float32)).astype(jnp.bfloat16)
    score_scale = head_width ** (-0.5)
    start_state = (
        jnp.full((query_heads, local_rows), masked_score, jnp.float32),
        jnp.zeros((query_heads, local_rows), jnp.float32),
        jnp.zeros((query_heads, local_rows, head_width), jnp.float32),
    )
    key_value = jnp.stack([keys, values])
    column_ids = jnp.arange(local_rows, dtype=jnp.int32)
    causal = column_ids[None, :] <= column_ids[:, None]
    running = attend(queries, score_scale, start_state, key_value, causal[None])

    def forward_step(step_number, state):
        held_running, blocks = state
        blocks = shifted(blocks, "ctx", 1)
        visible = step_number <= slab_index
        held_running = attend(queries, score_scale, held_running, blocks, visible)
        return (held_running, blocks)

    running, key_value = lax.fori_loop(1, slab_count, forward_step, (running, key_value))
    row_peak, row_total, weighted = running
    attended = (
        (weighted / row_total[..., None])
        .transpose(1, 0, 2)
        .reshape(local_rows, query_width)
        .astype(jnp.bfloat16)
    )
    return attended[None]


def solution(mesh):
    groups, slabs = (mesh.shape["fsdp"], mesh.shape["ctx"])
    pairs = Mesh(mesh.devices.reshape(groups // 2, 2, slabs), ("line", "pair", "ctx"))
    both = ("line", "pair")
    in_specs = (
        P(both, "ctx", None),
        P(),
        P(both, None),
        P(both, None),
        P(both, None),
        P(),
        P(),
        P(),
    )
    out_specs = P(both, "ctx", None)
    return jax.shard_map(shards, mesh=pairs, in_specs=in_specs, out_specs=out_specs, check_vma=False)
```

```python
import functools
import math

import jax
import jax.numpy as jnp
from jax import lax
from jax.experimental import pallas as pl
from jax.experimental.pallas import tpu as pltpu
from jax.sharding import Mesh, PartitionSpec as P

epsilon = 1e-06
rotary_base = 1000000.0
masked_score = -1e30


def shifted(value, axis, steps):
    count = lax.axis_size(axis)
    first, last = (max(0, -steps), min(count, count - steps))
    return lax.ppermute(value, axis, [(source, source + steps) for source in range(first, last)])


def rotary_tables(positions, head_width):
    half_width = head_width // 2
    frequency = jnp.exp(
        -(jnp.arange(half_width, dtype=jnp.float32) * (2.0 / head_width)) * math.log(rotary_base)
    )
    angles = positions.astype(jnp.float32)[:, None] * frequency[None, :]
    return (jnp.cos(angles)[:, None, :], jnp.sin(angles)[:, None, :])


def rotate(tensor, cosine, sine_table):
    half_width = tensor.shape[-1] // 2
    lower_half = tensor[..., :half_width]
    upper_half = tensor[..., half_width:]
    return jnp.concatenate(
        [
            lower_half * cosine - upper_half * sine_table,
            upper_half * cosine + lower_half * sine_table,
        ],
        axis=-1,
    )


def attend(work_queries, score_scale, running, key_value, visible):
    row_peak, row_total, weighted = running
    scores = (
        jnp.einsum("qhd,kd->hqk", work_queries, key_value[0], preferred_element_type=jnp.float32)
        * score_scale
    )
    scores = jnp.where(visible, scores, masked_score)
    new_peak = jnp.maximum(row_peak, jnp.max(scores, axis=-1))
    factor = jnp.exp(row_peak - new_peak)
    expsum = jnp.exp(scores - new_peak[..., None])
    row_total = row_total * factor + jnp.sum(expsum, axis=-1)
    weights = expsum.astype(jnp.bfloat16)
    weighted = weighted * factor[..., None] + jnp.einsum(
        "hqk,kd->hqd", weights, key_value[1], preferred_element_type=jnp.float32
    )
    return (new_peak, row_total, weighted)


def row_scale(inputs):
    floats = inputs.astype(jnp.float32)
    return lax.rsqrt(jnp.mean(floats * floats, axis=-1, keepdims=True) + epsilon)


def scaled_rows(inputs, scale, gain):
    return (inputs.astype(jnp.float32) * scale * gain.astype(jnp.float32)).astype(jnp.bfloat16)


def project(hidden, norm_gain, w_query, w_key, w_value):
    local_rows, width = hidden.shape
    lines, slabs = (lax.axis_size("line"), lax.axis_size("ctx"))
    depth = w_query.shape[0]
    side = lax.axis_index("pair")
    swap = [(0, 1), (1, 0)]
    split = hidden.reshape(local_rows, lines, 2, depth)
    half_width = lines * depth

    def half(array, which):
        return lax.dynamic_index_in_dim(array, which, array.ndim - 2, keepdims=False)

    sent = half(split, 1 - side).reshape(local_rows, half_width)
    kept = half(split, side).reshape(local_rows, half_width)
    gain = half(norm_gain.reshape(lines, 2, depth), side).reshape(half_width)
    came = lax.ppermute(sent, "pair", swap)
    scale = row_scale(hidden)
    came_scale = lax.ppermute(scale, "pair", swap)
    piece = depth // slabs
    start = lax.axis_index("ctx") * piece
    packed = jnp.concatenate(
        [lax.dynamic_slice_in_dim(w, start, piece, 0) for w in (w_query, w_key, w_value)], axis=1
    )
    weights = lax.all_gather(packed, ("line", "ctx"), axis=0, tiled=True)
    rows = jnp.concatenate(
        [scaled_rows(kept, scale, gain), scaled_rows(came, came_scale, gain)], axis=0
    )
    sums = jnp.dot(rows, weights, preferred_element_type=jnp.float32)
    back = lax.ppermute(sums[local_rows:].astype(jnp.bfloat16), "pair", swap)
    return sums[:local_rows] + back.astype(jnp.float32)


def normed_rows(block, scale, gain):
    return (block.astype(jnp.float32) * scale * gain).astype(jnp.bfloat16)


def slot_lines():
    line = lax.axis_index("line")
    inner = (line == 1) | (line == 2)
    third = jnp.where(inner, line ^ 3, line ^ 2)
    fourth = jnp.where(inner, line ^ 2, line ^ 3)
    return [line, line ^ 1, third, fourth]


def started(copies, sems, first):
    flights = [
        pltpu.make_async_copy(source, target, sems.at[first + number])
        for number, (source, target) in enumerate(copies)
    ]
    for flight in flights:
        flight.start()
    return flights


def piece_copies(pieces, wide, slab):
    piece = pieces[0].shape[0]
    return [
        (source, wide.at[pl.ds(pl.multiple_of(jnp.bitwise_xor(slab, flip) * piece, piece), piece), :])
        for source, flip in zip(pieces, (0, 2, 1, 3))
    ]


def pack_body(sent_parts, weights, depth, *refs):
    tokens, refs = (refs[0], refs[1:])
    sources, refs = (refs[:weights], refs[weights:])
    sems = refs[-1]
    copies = []
    outs = refs[:-1]
    if weights:
        mine, outs = (outs[0], outs[1:])
        piece = mine.shape[0]
        row = pl.multiple_of(lax.axis_index("ctx") * piece, piece)
        at = 0
        for source in sources:
            target = mine.at[:, pl.ds(at, source.shape[1])]
            copies.append((source.at[pl.ds(row, piece), :], target))
            at += source.shape[1]
    lines = slot_lines()
    other = 1 - lax.axis_index("pair")
    for out, parts in zip(outs, sent_parts):
        at = 0
        for slot, first, count in parts:
            column = pl.multiple_of((2 * lines[slot] + other) * depth + first, 128)
            copies.append((tokens.at[:, pl.ds(column, count)], out.at[:, pl.ds(at, count)]))
            at += count
    for flight in started(copies, sems, 0):
        flight.wait()


def pack(tokens, depth, sent_parts, weights=()):
    rows = tokens.shape[0]
    outside = pl.BlockSpec(memory_space=pltpu.HBM)
    outs = []
    if weights:
        piece = weights[0].shape[0] // 4
        outs.append(jax.ShapeDtypeStruct((piece, sum(w.shape[1] for w in weights)), jnp.bfloat16))
    for parts in sent_parts:
        outs.append(jax.ShapeDtypeStruct((rows, sum(p[2] for p in parts)), jnp.bfloat16))
    copies = len(weights) + sum(len(parts) for parts in sent_parts)
    moved = 4 * sum(out.shape[0] * out.shape[1] for out in outs)
    return pl.pallas_call(
        functools.partial(pack_body, sent_parts, len(weights), depth),
        out_shape=outs,
        in_specs=[outside] * (1 + len(weights)),
        out_specs=[pl.BlockSpec(memory_space=pltpu.VMEM)] * len(outs),
        scratch_shapes=[pltpu.SemaphoreType.DMA((copies,))],
        cost_estimate=pl.CostEstimate(flops=0, bytes_accessed=0, transcendentals=0),
        name="pack",
    )(tokens, *weights)


def prepare_body(sent_parts, depth, tokens, *refs):
    outs, refs = (refs[: len(sent_parts)], refs[len(sent_parts) :])
    column_scale, line_scale, held, sems = refs
    rows, width = held.shape
    lines = slot_lines()
    other = 1 - lax.axis_index("pair")
    loads = [
        (tokens.at[:, pl.ds(at, depth)], held.at[:, pl.ds(at, depth)])
        for at in range(0, width, depth)
    ]
    loads = started(loads, sems, 0)
    copies = []
    for out, parts in zip(outs, sent_parts):
        at = 0
        for slot, first, count in parts:
            column = pl.multiple_of((2 * lines[slot] + other) * depth + first, 128)
            copies.append((tokens.at[:, pl.ds(column, count)], out.at[:, pl.ds(at, count)]))
            at += count
    copies = started(copies, sems, len(loads))
    squares = jnp.zeros((rows, 128), jnp.float32)
    for number, load in enumerate(loads):
        load.wait()
        for at in range(number * depth, (number + 1) * depth, 128):
            floats = held[:, at : at + 128].astype(jnp.float32)
            squares = squares + floats * floats
    mean = jnp.sum(squares, axis=1, keepdims=True) / width
    wide = jnp.broadcast_to(lax.rsqrt(mean + epsilon), (rows, 128))
    column_scale[...] = wide
    line_scale[...] = jnp.transpose(wide)[:1]
    for copy in copies:
        copy.wait()


def prepare(tokens, depth, sent_parts):
    rows, width = tokens.shape
    outs = [
        jax.ShapeDtypeStruct((rows, sum(p[2] for p in parts)), jnp.bfloat16)
        for parts in sent_parts
    ]
    outs.append(jax.ShapeDtypeStruct((rows, 128), jnp.float32))
    outs.append(jax.ShapeDtypeStruct((1, rows), jnp.float32))
    copies = width // depth + sum(len(parts) for parts in sent_parts)
    return pl.pallas_call(
        functools.partial(prepare_body, sent_parts, depth),
        out_shape=outs,
        in_specs=[pl.BlockSpec(memory_space=pltpu.HBM)],
        out_specs=[pl.BlockSpec(memory_space=pltpu.VMEM)] * len(outs),
        scratch_shapes=[
            pltpu.VMEM((rows, width), jnp.bfloat16),
            pltpu.SemaphoreType.DMA((copies,)),
        ],
        cost_estimate=pl.CostEstimate(flops=0, bytes_accessed=0, transcendentals=0),
        compiler_params=pltpu.CompilerParams(vmem_limit_bytes=10 * 2**20),
        name="prepare",
    )(tokens)


def early_body(slots, guests, local, final, hidden, *refs):
    count = 1 + max(part[0] for part in guests)
    cames, refs = (refs[:count], refs[count:])
    scale, came_scale, gain, *refs = refs
    summed = slots[:-1] if final else slots
    number = 3 * local + 4 * (len(summed) - local)
    weights, refs = (refs[:number], refs[number:])
    before = None
    if not local:
        before, *refs = refs
    total, *refs = refs
    if final:
        last_rows, *refs = refs
    held, guest, wide, stacked, sems = refs
    _, rows, depth = held.shape
    slab = lax.axis_index("ctx")
    blocks = [2 * which + lax.axis_index("pair") for which in slot_lines()]
    number = 0
    parts = []
    at = 0
    for source, first, width in guests:
        parts.append(
            (cames[source].at[:, pl.ds(first, width)], guest.at[:, pl.ds(at, width)])
        )
        at += width
    guest_flights = started(parts, sems, number)
    number += len(parts)
    flights = []
    pending = list(weights)
    for place, slot in enumerate(slots):
        column = pl.multiple_of(blocks[slot] * depth, depth)
        copies = [(hidden.at[:, pl.ds(column, depth)], held.at[place])]
        if slot == 0:
            at = 0
            for _ in range(3):
                weight = pending.pop(0)
                copies.append((weight, wide.at[place, :, pl.ds(at, weight.shape[1])]))
                at += weight.shape[1]
        elif slot in summed:
            copies += piece_copies(pending[:4], wide.at[place], slab)
            pending = pending[4:]
        flights.append(started(copies, sems, number))
        number += len(copies)
    turned_scale = jnp.transpose(jnp.broadcast_to(came_scale[...], (128, rows)))[:, :1]
    for flight in guest_flights:
        flight.wait()
    width = total.shape[1]
    step = 256
    for place, slot in enumerate(slots):
        for flight in flights[place]:
            flight.wait()
        column = pl.multiple_of(blocks[slot] * depth, depth)
        row_gain = gain[:, pl.ds(column, depth)].astype(jnp.float32)
        target = stacked.at[place] if slot in summed else last_rows
        target[:rows] = normed_rows(held[place], scale[:, :1], row_gain)
        target[rows:] = normed_rows(
            guest[:, place * depth : (place + 1) * depth], turned_scale, row_gain
        )
        if slot not in summed:
            continue
        for at in range(0, width, step):
            cols = pl.ds(at, step)
            product = jnp.dot(
                stacked[place], wide[place, :, cols], preferred_element_type=jnp.float32
            )
            if place > 0:
                product = product + total[:, cols]
            elif before is not None:
                product = product + before[:, cols]
            total[:, cols] = product


def early_slots(
    slots, guests, local, final, hidden, cames, scale, came_scale, gain, weights, before=None
):
    rows = hidden.shape[0]
    depth = weights[0].shape[0] if local else 4 * weights[0].shape[0]
    width = sum(w.shape[1] for w in weights[:3]) if local else weights[0].shape[1]
    outside = pl.BlockSpec(memory_space=pltpu.HBM)
    anywhere = pl.BlockSpec(memory_space=pl.ANY)
    inside = pl.BlockSpec(memory_space=pltpu.VMEM)
    summed = len(slots) - final
    flops = 4 * rows * depth * summed * width
    moved = 2 * (depth * width * summed + 2 * rows * depth * len(slots)) + 8 * rows * width
    outs = [jax.ShapeDtypeStruct((2 * rows, width), jnp.float32)]
    if final:
        outs.append(jax.ShapeDtypeStruct((2 * rows, depth), jnp.bfloat16))
    args = [hidden, *cames, scale, came_scale, gain, *weights]
    in_specs = [outside] + [anywhere] * len(cames)
    in_specs += [inside] * 3 + [outside] * (3 * local) + [anywhere] * (len(weights) - 3 * local)
    if before is not None:
        args.append(before)
        in_specs.append(inside)
    return pl.pallas_call(
        functools.partial(early_body, slots, guests, local, final),
        out_shape=outs,
        in_specs=in_specs,
        out_specs=[inside] * len(outs),
        scratch_shapes=[
            pltpu.VMEM((len(slots), rows, depth), jnp.bfloat16),
            pltpu.VMEM((rows, len(slots) * depth), jnp.bfloat16),
            pltpu.VMEM((summed, depth, width), jnp.bfloat16),
            pltpu.VMEM((summed, 2 * rows, depth), jnp.bfloat16),
            pltpu.SemaphoreType.DMA((len(guests) + len(slots) + len(weights),)),
        ],
        cost_estimate=pl.CostEstimate(flops=flops, bytes_accessed=moved, transcendentals=0),
        compiler_params=pltpu.CompilerParams(vmem_limit_bytes=24 * 2**20),
        name="early_slots",
    )(*args)


def late_body(first, splits, before, last_rows, *refs):
    pieces, refs = (refs[:4], refs[4:])
    kept, sent = (refs[: len(splits)], refs[len(splits) : 2 * len(splits)])
    wide, sems = refs[2 * len(splits) :]
    rows, width = (kept[0].shape[0], wide.shape[1])
    pieces = [p if p.shape[1] == width else p.at[:, pl.ds(first, width)] for p in pieces]
    for flight in started(piece_copies(pieces, wide, lax.axis_index("ctx")), sems, 0):
        flight.wait()
    at = 0
    for own, other, columns in zip(kept, sent, splits):
        cols = slice(at, at + columns)
        product = jnp.dot(last_rows[...], wide[:, cols], preferred_element_type=jnp.float32)
        product = product + before[:, first + at : first + at + columns]
        own[...] = product[:rows]
        other[...] = product[rows:].astype(jnp.bfloat16)
        at += columns


def late_slot(first, splits, before, last_rows, pieces):
    rows, depth = (last_rows.shape[0] // 2, last_rows.shape[1])
    anywhere = pl.BlockSpec(memory_space=pl.ANY)
    inside = pl.BlockSpec(memory_space=pltpu.VMEM)
    width = sum(splits)
    outs = [jax.ShapeDtypeStruct((rows, w), jnp.float32) for w in splits]
    outs += [jax.ShapeDtypeStruct((rows, w), jnp.bfloat16) for w in splits]
    return pl.pallas_call(
        functools.partial(late_body, first, splits),
        out_shape=outs,
        in_specs=[inside] * 2 + [anywhere] * 4,
        out_specs=[inside] * len(outs),
        scratch_shapes=[
            pltpu.VMEM((depth, width), jnp.bfloat16),
            pltpu.SemaphoreType.DMA((4,)),
        ],
        cost_estimate=pl.CostEstimate(
            flops=4 * rows * depth * width, bytes_accessed=2 * depth * width, transcendentals=0
        ),
        compiler_params=pltpu.CompilerParams(vmem_limit_bytes=10 * 2**20),
        name="late_slot",
    )(before, last_rows, *pieces)


def turned(tensor, cosine, sine_table):
    half = tensor.shape[-1] // 2
    return tensor * cosine + pltpu.roll(tensor, half, 1) * sine_table


def key_value_body(sums, back, bias, cosine, sine_table, out):
    head = out.shape[1] // 2
    total = sums[:, : 2 * head] + back[:, : 2 * head].astype(jnp.float32) + bias[...]
    out[:, :head] = turned(total[:, :head], cosine[...], sine_table[...]).astype(jnp.bfloat16)
    out[:, head:] = total[:, head:].astype(jnp.bfloat16)


def attention_body(scale, first, skips, *refs):
    groups = len(skips)
    sums, refs = (refs[:groups], refs[groups:])
    backs, refs = (refs[:groups], refs[groups:])
    bias, cosine, sine_table, *refs = refs
    blocks, refs = (refs[:4], refs[4:])
    if first:
        done, *refs = refs
    out, keys, values = refs
    rows = out.shape[0]
    head = cosine.shape[1]
    slab = lax.axis_index("ctx")
    for block, flip in zip(blocks, (0, 1, 2, 3)):
        row = pl.multiple_of(jnp.bitwise_xor(slab, flip) * rows, rows)
        keys[pl.ds(row, rows), :] = block[:, :head]
        values[pl.ds(row, rows), :] = block[:, head:]
    total_keys = keys.shape[0]
    row_ids = slab * rows + lax.broadcasted_iota(jnp.int32, (rows, total_keys), 0)
    visible = lax.broadcasted_iota(jnp.int32, (rows, total_keys), 1) <= row_ids
    if first:
        out[:, :first] = done[...]
    at = first
    for own, other, skip in zip(sums, backs, skips):
        for column in range(skip, own.shape[1], head):
            cols = slice(column, column + head)
            query = own[:, cols] + other[:, cols].astype(jnp.float32) + bias[:, at : at + head]
            query = turned(query, cosine[...], sine_table[...]).astype(jnp.bfloat16)
            scores = lax.dot_general(
                query, keys[...], (((1,), (1,)), ((), ())), preferred_element_type=jnp.float32
            )
            scores = jnp.where(visible, scores * scale, masked_score)
            exps = jnp.exp(scores - jnp.max(scores, axis=1, keepdims=True))
            length = jnp.sum(exps, axis=1, keepdims=True)
            mixed = jnp.dot(
                exps.astype(jnp.bfloat16), values[...], preferred_element_type=jnp.float32
            )
            out[:, at : at + head] = (mixed / length).astype(jnp.bfloat16)
            at += head


def attention(sums, backs, skips, bias, cosine, sine_table, blocks, done=None):
    rows = sums[0].shape[0]
    width = sum(own.shape[1] - skip for own, skip in zip(sums, skips))
    head = cosine.shape[1]
    first = 0 if done is None else done.shape[1]
    inside = pl.BlockSpec(memory_space=pltpu.VMEM)
    args = [*sums, *backs, bias, cosine, sine_table, *blocks]
    if first:
        args.append(done)
    total = 4 * rows * rows * (width // head)
    return pl.pallas_call(
        functools.partial(attention_body, head ** (-0.5), first, skips),
        out_shape=jax.ShapeDtypeStruct((rows, first + width), jnp.bfloat16),
        in_specs=[inside] * len(args),
        out_specs=inside,
        scratch_shapes=[
            pltpu.VMEM((4 * rows, head), jnp.bfloat16),
            pltpu.VMEM((4 * rows, head), jnp.bfloat16),
        ],
        cost_estimate=pl.CostEstimate(
            flops=4 * total * head, bytes_accessed=8 * rows * width, transcendentals=total
        ),
        compiler_params=pltpu.CompilerParams(vmem_limit_bytes=12 * 2**20),
        name="attention",
    )(*args)


def planned(hidden, norm_gain, w_query, w_key, w_value, bias_query, bias_key, bias_value):
    tokens = hidden[0]
    rows = tokens.shape[0]
    depth = w_query.shape[0]
    head = w_key.shape[1]
    line, slab = (lax.axis_index("line"), lax.axis_index("ctx"))
    inner = (line == 1) | (line == 2)
    swap = [(0, 1), (1, 0)]
    ends = [(0, 1), (1, 0), (2, 3), (3, 2)]
    middle = [(1, 2), (2, 1)]
    outward = [(1, 0), (2, 3)]
    across = [(i, i ^ 2) for i in range(4)]
    beside = [(i, i ^ 1) for i in range(4)]
    held = lax.optimization_barrier
    cut = depth // 8
    parts_1 = ((0, 0, depth), (1, 0, 2 * cut))
    parts_2 = ((1, 2 * cut, 6 * cut), (2, 0, 6 * cut))
    parts_3 = ((2, 6 * cut, 2 * cut), (3, 0, depth))
    mine, sent_1 = pack(tokens, depth, (parts_1,), (w_key, w_value, w_query))
    kv_width = 2 * head
    half = kv_width + w_query.shape[1] // 2
    rest = mine.shape[1] - half
    second = lax.ppermute(mine, "line", ends)
    third_in = lax.ppermute(mine, "line", middle)
    came_1 = lax.ppermute(sent_1, "pair", swap)
    (sent_2,) = pack(tokens, depth, (parts_2,))
    gain = norm_gain.reshape(1, -1)
    bias_kv = jnp.concatenate([bias_key, bias_value]).reshape(1, -1).astype(jnp.float32)
    bias_q = bias_query.reshape(1, -1).astype(jnp.float32)
    positions = slab * rows + jnp.arange(rows, dtype=jnp.int32)
    cosine, sine_table = rotary_tables(positions, head)
    cosine = jnp.concatenate([cosine, cosine], axis=-1).reshape(rows, head)
    sine_table = jnp.concatenate([-sine_table, sine_table], axis=-1).reshape(rows, head)
    small = (gain, bias_kv, bias_q, cosine, sine_table)
    second, third_in, came_1, sent_2, small, later_tokens = held(
        (second, third_in, came_1, sent_2, small, tokens)
    )
    gain, bias_kv, bias_q, cosine, sine_table = small
    fourth_in = lax.ppermute(second, "line", middle)
    third_out = lax.ppermute(third_in, "line", outward)
    second_far = lax.ppermute(second, "ctx", across)
    came_2 = lax.ppermute(sent_2, "pair", swap)
    second_side = lax.ppermute(second, "ctx", beside)
    sent_3, scale, line_scale = prepare(later_tokens, depth, (parts_3,))
    came_scale = lax.ppermute(line_scale, "pair", swap)
    third = jnp.where(inner, third_in, third_out)
    fourth_in, came_scale, third, second_far, came_2, second_side, sent_3, scale = held(
        (fourth_in, came_scale, third, second_far, came_2, second_side, sent_3, scale)
    )
    fourth_out = lax.ppermute(fourth_in, "line", outward)
    third_far = lax.ppermute(third, "ctx", across)
    came_3 = lax.ppermute(sent_3, "pair", swap)
    second_corner = lax.ppermute(second_far, "ctx", beside)
    third_side = lax.ppermute(third, "ctx", beside)
    before = early_slots(
        (0, 1),
        ((0, 0, 10 * cut), (1, 0, 6 * cut)),
        True,
        False,
        tokens,
        (came_1, came_2),
        scale,
        came_scale,
        gain,
        [w_key, w_value, w_query, second, second_far, second_side, second_corner],
    )[0]
    fourth = jnp.where(inner, fourth_in, fourth_out)
    fourth, third_far, came_3, third_side, before = held(
        (fourth, third_far, came_3, third_side, before)
    )
    fourth_far_1 = lax.ppermute(fourth[:, :half], "ctx", across)
    third_corner = lax.ppermute(third_far, "ctx", beside)
    fourth_side = lax.ppermute(fourth, "ctx", beside)
    before, last_rows = early_slots(
        (2, 3),
        ((0, 6 * cut, 6 * cut), (1, 0, 10 * cut)),
        False,
        True,
        tokens,
        (came_2, came_3),
        scale,
        came_scale,
        gain,
        [third, third_far, third_side, third_corner],
        before,
    )
    fourth_far_1, fourth, before, last_rows, fourth_side = held(
        (fourth_far_1, fourth, before, last_rows, fourth_side)
    )
    fourth_far_2 = lax.ppermute(fourth[:, half:], "ctx", across)
    fourth_corner_1 = lax.ppermute(fourth_far_1, "ctx", beside)
    early_width = kv_width
    sums_0, sums_1, back_0, back_1 = late_slot(
        0,
        (early_width, half - early_width),
        before,
        last_rows,
        (fourth, fourth_far_1, fourth_side, fourth_corner_1),
    )
    back_0 = lax.ppermute(back_0, "pair", swap)
    back_1 = lax.ppermute(back_1, "pair", swap)
    back_0, fourth_far_2 = held((back_0, fourth_far_2))
    fourth_corner_2 = lax.ppermute(fourth_far_2, "ctx", beside)
    sums_2, back_2 = late_slot(
        half,
        (rest,),
        before,
        last_rows,
        (fourth, fourth_far_2, fourth_side, fourth_corner_2),
    )
    back_2 = lax.ppermute(back_2, "pair", swap)

    inside = pl.BlockSpec(memory_space=pltpu.VMEM)
    key_value = pl.pallas_call(
        key_value_body,
        out_shape=jax.ShapeDtypeStruct((rows, kv_width), jnp.bfloat16),
        in_specs=[inside] * 5,
        out_specs=inside,
        compiler_params=pltpu.CompilerParams(vmem_limit_bytes=4 * 2**20),
        name="key_value",
    )(sums_0, back_0, bias_kv, cosine, sine_table)
    kv_across = lax.ppermute(key_value, "ctx", [(0, 2), (1, 3)])
    kv_beside = lax.ppermute(key_value, "ctx", beside)
    kv_corner = lax.ppermute(kv_across, "ctx", [(2, 3), (3, 2)])
    blocks = (key_value, kv_beside, kv_across, kv_corner)
    tables = (bias_q, cosine, sine_table, blocks)
    attended = attention((sums_0, sums_1), (back_0, back_1), (kv_width, 0), *tables)
    attended = attention((sums_2,), (back_2,), (0,), *tables, attended)
    return attended[None]


def shards(hidden, norm_gain, w_query, w_key, w_value, bias_query, bias_key, bias_value):
    if lax.axis_size("line") == 4 and lax.axis_size("ctx") == 4:
        return planned(
            hidden, norm_gain, w_query, w_key, w_value, bias_query, bias_key, bias_value
        )
    local_rows = hidden.shape[1]
    head_width = w_key.shape[1]
    query_width = w_query.shape[1]
    query_heads = query_width // head_width
    sums = project(hidden[0], norm_gain, w_query, w_key, w_value)
    query_sums = sums[:, :query_width]
    key_sums = sums[:, query_width : query_width + head_width]
    value_sums = sums[:, query_width + head_width :]
    slab_index = lax.axis_index("ctx")
    slab_count = lax.axis_size("ctx")
    positions = slab_index * local_rows + jnp.arange(local_rows, dtype=jnp.int32)
    cosine, sine_table = rotary_tables(positions, head_width)
    queries = rotate(
        (query_sums + bias_query.astype(jnp.float32)).reshape(local_rows, query_heads, head_width),
        cosine,
        sine_table,
    ).astype(jnp.bfloat16)
    keys = rotate((key_sums + bias_key.astype(jnp.float32))[:, None, :], cosine, sine_table)[
        :, 0, :
    ].astype(jnp.bfloat16)
    values = (value_sums + bias_value.astype(jnp.float32)).astype(jnp.bfloat16)
    score_scale = head_width ** (-0.5)
    start_state = (
        jnp.full((query_heads, local_rows), masked_score, jnp.float32),
        jnp.zeros((query_heads, local_rows), jnp.float32),
        jnp.zeros((query_heads, local_rows, head_width), jnp.float32),
    )
    key_value = jnp.stack([keys, values])
    column_ids = jnp.arange(local_rows, dtype=jnp.int32)
    causal = column_ids[None, :] <= column_ids[:, None]
    running = attend(queries, score_scale, start_state, key_value, causal[None])

    def forward_step(step_number, state):
        held_running, blocks = state
        blocks = shifted(blocks, "ctx", 1)
        visible = step_number <= slab_index
        held_running = attend(queries, score_scale, held_running, blocks, visible)
        return (held_running, blocks)

    running, key_value = lax.fori_loop(1, slab_count, forward_step, (running, key_value))
    row_peak, row_total, weighted = running
    attended = (
        (weighted / row_total[..., None])
        .transpose(1, 0, 2)
        .reshape(local_rows, query_width)
        .astype(jnp.bfloat16)
    )
    return attended[None]


def solution(mesh):
    groups, slabs = (mesh.shape["fsdp"], mesh.shape["ctx"])
    pairs = Mesh(mesh.devices.reshape(groups // 2, 2, slabs), ("line", "pair", "ctx"))
    both = ("line", "pair")
    in_specs = (
        P(both, "ctx", None),
        P(),
        P(both, None),
        P(both, None),
        P(both, None),
        P(),
        P(),
        P(),
    )
    out_specs = P(both, "ctx", None)
    return jax.shard_map(shards, mesh=pairs, in_specs=in_specs, out_specs=out_specs, check_vma=False)
```

```python
import functools
import math

import jax
import jax.numpy as jnp
from jax import lax
from jax.experimental import pallas as pl
from jax.experimental.pallas import tpu as pltpu
from jax.sharding import Mesh, PartitionSpec as P

epsilon = 1e-06
rotary_base = 1000000.0
masked_score = -1e30


def shifted(value, axis, steps):
    count = lax.axis_size(axis)
    first, last = (max(0, -steps), min(count, count - steps))
    return lax.ppermute(value, axis, [(source, source + steps) for source in range(first, last)])


def rotary_tables(positions, head_width):
    half_width = head_width // 2
    frequency = jnp.exp(
        -(jnp.arange(half_width, dtype=jnp.float32) * (2.0 / head_width)) * math.log(rotary_base)
    )
    angles = positions.astype(jnp.float32)[:, None] * frequency[None, :]
    return (jnp.cos(angles)[:, None, :], jnp.sin(angles)[:, None, :])


def rotate(tensor, cosine, sine_table):
    half_width = tensor.shape[-1] // 2
    lower_half = tensor[..., :half_width]
    upper_half = tensor[..., half_width:]
    return jnp.concatenate(
        [
            lower_half * cosine - upper_half * sine_table,
            upper_half * cosine + lower_half * sine_table,
        ],
        axis=-1,
    )


def attend(work_queries, score_scale, running, key_value, visible):
    row_peak, row_total, weighted = running
    scores = (
        jnp.einsum("qhd,kd->hqk", work_queries, key_value[0], preferred_element_type=jnp.float32)
        * score_scale
    )
    scores = jnp.where(visible, scores, masked_score)
    new_peak = jnp.maximum(row_peak, jnp.max(scores, axis=-1))
    factor = jnp.exp(row_peak - new_peak)
    expsum = jnp.exp(scores - new_peak[..., None])
    row_total = row_total * factor + jnp.sum(expsum, axis=-1)
    weights = expsum.astype(jnp.bfloat16)
    weighted = weighted * factor[..., None] + jnp.einsum(
        "hqk,kd->hqd", weights, key_value[1], preferred_element_type=jnp.float32
    )
    return (new_peak, row_total, weighted)


def row_scale(inputs):
    floats = inputs.astype(jnp.float32)
    return lax.rsqrt(jnp.mean(floats * floats, axis=-1, keepdims=True) + epsilon)


def scaled_rows(inputs, scale, gain):
    return (inputs.astype(jnp.float32) * scale * gain.astype(jnp.float32)).astype(jnp.bfloat16)


def project(hidden, norm_gain, w_query, w_key, w_value):
    local_rows, width = hidden.shape
    lines, slabs = (lax.axis_size("line"), lax.axis_size("ctx"))
    depth = w_query.shape[0]
    side = lax.axis_index("pair")
    swap = [(0, 1), (1, 0)]
    split = hidden.reshape(local_rows, lines, 2, depth)
    half_width = lines * depth

    def half(array, which):
        return lax.dynamic_index_in_dim(array, which, array.ndim - 2, keepdims=False)

    sent = half(split, 1 - side).reshape(local_rows, half_width)
    kept = half(split, side).reshape(local_rows, half_width)
    gain = half(norm_gain.reshape(lines, 2, depth), side).reshape(half_width)
    came = lax.ppermute(sent, "pair", swap)
    scale = row_scale(hidden)
    came_scale = lax.ppermute(scale, "pair", swap)
    piece = depth // slabs
    start = lax.axis_index("ctx") * piece
    packed = jnp.concatenate(
        [lax.dynamic_slice_in_dim(w, start, piece, 0) for w in (w_query, w_key, w_value)], axis=1
    )
    weights = lax.all_gather(packed, ("line", "ctx"), axis=0, tiled=True)
    rows = jnp.concatenate(
        [scaled_rows(kept, scale, gain), scaled_rows(came, came_scale, gain)], axis=0
    )
    sums = jnp.dot(rows, weights, preferred_element_type=jnp.float32)
    back = lax.ppermute(sums[local_rows:].astype(jnp.bfloat16), "pair", swap)
    return sums[:local_rows] + back.astype(jnp.float32)


def normed_rows(block, scale, gain):
    return (block.astype(jnp.float32) * scale * gain).astype(jnp.bfloat16)


def slot_lines():
    line = lax.axis_index("line")
    inner = (line == 1) | (line == 2)
    third = jnp.where(inner, line ^ 3, line ^ 2)
    fourth = jnp.where(inner, line ^ 2, line ^ 3)
    return [line, line ^ 1, third, fourth]


def started(copies, sems, first):
    flights = [
        pltpu.make_async_copy(source, target, sems.at[first + number])
        for number, (source, target) in enumerate(copies)
    ]
    for flight in flights:
        flight.start()
    return flights


def piece_copies(pieces, wide, slab):
    piece = pieces[0].shape[0]
    return [
        (source, wide.at[pl.ds(pl.multiple_of(jnp.bitwise_xor(slab, flip) * piece, piece), piece), :])
        for source, flip in zip(pieces, (0, 2, 1, 3))
    ]


def pack_body(sent_parts, weights, depth, *refs):
    tokens, refs = (refs[0], refs[1:])
    sources, refs = (refs[:weights], refs[weights:])
    sems = refs[-1]
    copies = []
    outs = refs[:-1]
    if weights:
        mine, outs = (outs[0], outs[1:])
        piece = mine.shape[0]
        row = pl.multiple_of(lax.axis_index("ctx") * piece, piece)
        at = 0
        for source in sources:
            target = mine.at[:, pl.ds(at, source.shape[1])]
            copies.append((source.at[pl.ds(row, piece), :], target))
            at += source.shape[1]
    lines = slot_lines()
    other = 1 - lax.axis_index("pair")
    for out, parts in zip(outs, sent_parts):
        at = 0
        for slot, first, count in parts:
            column = pl.multiple_of((2 * lines[slot] + other) * depth + first, 128)
            copies.append((tokens.at[:, pl.ds(column, count)], out.at[:, pl.ds(at, count)]))
            at += count
    for flight in started(copies, sems, 0):
        flight.wait()


def pack(tokens, depth, sent_parts, weights=()):
    rows = tokens.shape[0]
    outside = pl.BlockSpec(memory_space=pltpu.HBM)
    outs = []
    if weights:
        piece = weights[0].shape[0] // 4
        outs.append(jax.ShapeDtypeStruct((piece, sum(w.shape[1] for w in weights)), jnp.bfloat16))
    for parts in sent_parts:
        outs.append(jax.ShapeDtypeStruct((rows, sum(p[2] for p in parts)), jnp.bfloat16))
    copies = len(weights) + sum(len(parts) for parts in sent_parts)
    moved = 4 * sum(out.shape[0] * out.shape[1] for out in outs)
    return pl.pallas_call(
        functools.partial(pack_body, sent_parts, len(weights), depth),
        out_shape=outs,
        in_specs=[outside] * (1 + len(weights)),
        out_specs=[pl.BlockSpec(memory_space=pltpu.VMEM)] * len(outs),
        scratch_shapes=[pltpu.SemaphoreType.DMA((copies,))],
        cost_estimate=pl.CostEstimate(flops=0, bytes_accessed=0, transcendentals=0),
        name="pack",
    )(tokens, *weights)


def prepare_body(sent_parts, depth, tokens, *refs):
    outs, refs = (refs[: len(sent_parts)], refs[len(sent_parts) :])
    column_scale, line_scale, held, sems = refs
    rows, width = held.shape
    lines = slot_lines()
    other = 1 - lax.axis_index("pair")
    loads = [
        (tokens.at[:, pl.ds(at, depth)], held.at[:, pl.ds(at, depth)])
        for at in range(0, width, depth)
    ]
    loads = started(loads, sems, 0)
    copies = []
    for out, parts in zip(outs, sent_parts):
        at = 0
        for slot, first, count in parts:
            column = pl.multiple_of((2 * lines[slot] + other) * depth + first, 128)
            copies.append((tokens.at[:, pl.ds(column, count)], out.at[:, pl.ds(at, count)]))
            at += count
    copies = started(copies, sems, len(loads))
    squares = jnp.zeros((rows, 128), jnp.float32)
    for number, load in enumerate(loads):
        load.wait()
        for at in range(number * depth, (number + 1) * depth, 128):
            floats = held[:, at : at + 128].astype(jnp.float32)
            squares = squares + floats * floats
    mean = jnp.sum(squares, axis=1, keepdims=True) / width
    wide = jnp.broadcast_to(lax.rsqrt(mean + epsilon), (rows, 128))
    column_scale[...] = wide
    line_scale[...] = jnp.transpose(wide)[:1]
    for copy in copies:
        copy.wait()


def prepare(tokens, depth, sent_parts):
    rows, width = tokens.shape
    outs = [
        jax.ShapeDtypeStruct((rows, sum(p[2] for p in parts)), jnp.bfloat16)
        for parts in sent_parts
    ]
    outs.append(jax.ShapeDtypeStruct((rows, 128), jnp.float32))
    outs.append(jax.ShapeDtypeStruct((1, rows), jnp.float32))
    copies = width // depth + sum(len(parts) for parts in sent_parts)
    return pl.pallas_call(
        functools.partial(prepare_body, sent_parts, depth),
        out_shape=outs,
        in_specs=[pl.BlockSpec(memory_space=pltpu.HBM)],
        out_specs=[pl.BlockSpec(memory_space=pltpu.VMEM)] * len(outs),
        scratch_shapes=[
            pltpu.VMEM((rows, width), jnp.bfloat16),
            pltpu.SemaphoreType.DMA((copies,)),
        ],
        cost_estimate=pl.CostEstimate(flops=0, bytes_accessed=0, transcendentals=0),
        compiler_params=pltpu.CompilerParams(vmem_limit_bytes=10 * 2**20),
        name="prepare",
    )(tokens)


def early_body(slots, guests, local, final, hidden, *refs):
    count = 1 + max(part[0] for part in guests)
    cames, refs = (refs[:count], refs[count:])
    scale, came_scale, gain, *refs = refs
    summed = slots[:-1] if final else slots
    number = 3 * local + 4 * (len(summed) - local)
    weights, refs = (refs[:number], refs[number:])
    before = None
    if not local:
        before, *refs = refs
    total, *refs = refs
    if final:
        last_rows, *refs = refs
    held, guest, wide, stacked, sems = refs
    _, rows, depth = held.shape
    slab = lax.axis_index("ctx")
    blocks = [2 * which + lax.axis_index("pair") for which in slot_lines()]
    number = 0
    parts = []
    at = 0
    for source, first, width in guests:
        parts.append(
            (cames[source].at[:, pl.ds(first, width)], guest.at[:, pl.ds(at, width)])
        )
        at += width
    guest_flights = started(parts, sems, number)
    number += len(parts)
    flights = []
    pending = list(weights)
    for place, slot in enumerate(slots):
        column = pl.multiple_of(blocks[slot] * depth, depth)
        copies = [(hidden.at[:, pl.ds(column, depth)], held.at[place])]
        if slot == 0:
            at = 0
            for _ in range(3):
                weight = pending.pop(0)
                copies.append((weight, wide.at[place, :, pl.ds(at, weight.shape[1])]))
                at += weight.shape[1]
        elif slot in summed:
            copies += piece_copies(pending[:4], wide.at[place], slab)
            pending = pending[4:]
        flights.append(started(copies, sems, number))
        number += len(copies)
    turned_scale = jnp.transpose(jnp.broadcast_to(came_scale[...], (128, rows)))[:, :1]
    for flight in guest_flights:
        flight.wait()
    width = total.shape[1]
    step = 256
    for place, slot in enumerate(slots):
        for flight in flights[place]:
            flight.wait()
        column = pl.multiple_of(blocks[slot] * depth, depth)
        row_gain = gain[:, pl.ds(column, depth)].astype(jnp.float32)
        target = stacked.at[place] if slot in summed else last_rows
        target[:rows] = normed_rows(held[place], scale[:, :1], row_gain)
        target[rows:] = normed_rows(
            guest[:, place * depth : (place + 1) * depth], turned_scale, row_gain
        )
        if slot not in summed:
            continue
        for at in range(0, width, step):
            cols = pl.ds(at, step)
            product = jnp.dot(
                stacked[place], wide[place, :, cols], preferred_element_type=jnp.float32
            )
            if place > 0:
                product = product + total[:, cols]
            elif before is not None:
                product = product + before[:, cols]
            total[:, cols] = product


def early_slots(
    slots, guests, local, final, hidden, cames, scale, came_scale, gain, weights, before=None
):
    rows = hidden.shape[0]
    depth = weights[0].shape[0] if local else 4 * weights[0].shape[0]
    width = sum(w.shape[1] for w in weights[:3]) if local else weights[0].shape[1]
    outside = pl.BlockSpec(memory_space=pltpu.HBM)
    anywhere = pl.BlockSpec(memory_space=pl.ANY)
    inside = pl.BlockSpec(memory_space=pltpu.VMEM)
    summed = len(slots) - final
    flops = 4 * rows * depth * summed * width
    moved = 2 * (depth * width * summed + 2 * rows * depth * len(slots)) + 8 * rows * width
    outs = [jax.ShapeDtypeStruct((2 * rows, width), jnp.float32)]
    if final:
        outs.append(jax.ShapeDtypeStruct((2 * rows, depth), jnp.bfloat16))
    args = [hidden, *cames, scale, came_scale, gain, *weights]
    in_specs = [outside] + [anywhere] * len(cames)
    in_specs += [inside] * 3 + [outside] * (3 * local) + [anywhere] * (len(weights) - 3 * local)
    if before is not None:
        args.append(before)
        in_specs.append(inside)
    return pl.pallas_call(
        functools.partial(early_body, slots, guests, local, final),
        out_shape=outs,
        in_specs=in_specs,
        out_specs=[inside] * len(outs),
        scratch_shapes=[
            pltpu.VMEM((len(slots), rows, depth), jnp.bfloat16),
            pltpu.VMEM((rows, len(slots) * depth), jnp.bfloat16),
            pltpu.VMEM((summed, depth, width), jnp.bfloat16),
            pltpu.VMEM((summed, 2 * rows, depth), jnp.bfloat16),
            pltpu.SemaphoreType.DMA((len(guests) + len(slots) + len(weights),)),
        ],
        cost_estimate=pl.CostEstimate(flops=flops, bytes_accessed=moved, transcendentals=0),
        compiler_params=pltpu.CompilerParams(vmem_limit_bytes=24 * 2**20),
        name="early_slots",
    )(*args)


def late_body(first, splits, before, last_rows, *refs):
    pieces, refs = (refs[:4], refs[4:])
    kept, sent = (refs[: len(splits)], refs[len(splits) : 2 * len(splits)])
    wide, sems = refs[2 * len(splits) :]
    rows, width = (kept[0].shape[0], wide.shape[1])
    pieces = [p if p.shape[1] == width else p.at[:, pl.ds(first, width)] for p in pieces]
    for flight in started(piece_copies(pieces, wide, lax.axis_index("ctx")), sems, 0):
        flight.wait()
    at = 0
    for own, other, columns in zip(kept, sent, splits):
        cols = slice(at, at + columns)
        product = jnp.dot(last_rows[...], wide[:, cols], preferred_element_type=jnp.float32)
        product = product + before[:, first + at : first + at + columns]
        own[...] = product[:rows]
        other[...] = product[rows:].astype(jnp.bfloat16)
        at += columns


def late_slot(first, splits, before, last_rows, pieces):
    rows, depth = (last_rows.shape[0] // 2, last_rows.shape[1])
    anywhere = pl.BlockSpec(memory_space=pl.ANY)
    inside = pl.BlockSpec(memory_space=pltpu.VMEM)
    width = sum(splits)
    outs = [jax.ShapeDtypeStruct((rows, w), jnp.float32) for w in splits]
    outs += [jax.ShapeDtypeStruct((rows, w), jnp.bfloat16) for w in splits]
    return pl.pallas_call(
        functools.partial(late_body, first, splits),
        out_shape=outs,
        in_specs=[inside] * 2 + [anywhere] * 4,
        out_specs=[inside] * len(outs),
        scratch_shapes=[
            pltpu.VMEM((depth, width), jnp.bfloat16),
            pltpu.SemaphoreType.DMA((4,)),
        ],
        cost_estimate=pl.CostEstimate(
            flops=4 * rows * depth * width, bytes_accessed=2 * depth * width, transcendentals=0
        ),
        compiler_params=pltpu.CompilerParams(vmem_limit_bytes=10 * 2**20),
        name="late_slot",
    )(before, last_rows, *pieces)


def turned(tensor, cosine, sine_table):
    half = tensor.shape[-1] // 2
    return tensor * cosine + pltpu.roll(tensor, half, 1) * sine_table


def key_value_body(sums, back, bias, cosine, sine_table, out):
    head = out.shape[1] // 2
    total = sums[:, : 2 * head] + back[:, : 2 * head].astype(jnp.float32) + bias[...]
    out[:, :head] = turned(total[:, :head], cosine[...], sine_table[...]).astype(jnp.bfloat16)
    out[:, head:] = total[:, head:].astype(jnp.bfloat16)


def attention_body(scale, first, skips, *refs):
    groups = len(skips)
    sums, refs = (refs[:groups], refs[groups:])
    backs, refs = (refs[:groups], refs[groups:])
    bias, cosine, sine_table, *refs = refs
    blocks, refs = (refs[:4], refs[4:])
    if first:
        done, *refs = refs
    out, keys, values = refs
    rows = out.shape[0]
    head = cosine.shape[1]
    slab = lax.axis_index("ctx")
    odd = lax.rem(slab, 2)
    own_block, beside, across, corner = blocks
    for block, place in ((own_block, odd), (beside, 1 - odd)):
        row = pl.multiple_of(place * rows, rows)
        keys[pl.ds(row, rows), :] = block[:, :head]
        values[pl.ds(row, rows), :] = block[:, head:]
    near = (rows, keys.shape[0])
    row_ids = odd * rows + lax.broadcasted_iota(jnp.int32, near, 0)
    visible = lax.broadcasted_iota(jnp.int32, near, 1) <= row_ids
    power = scale * math.log2(math.e)
    if first:
        out[:, :first] = done[...]

    def all_heads(far):
        at = first
        for own, other, skip in zip(sums, backs, skips):
            for column in range(skip, own.shape[1], head):
                cols = slice(column, column + head)
                query = own[:, cols] + other[:, cols].astype(jnp.float32) + bias[:, at : at + head]
                query = turned(query, cosine[...], sine_table[...]).astype(jnp.bfloat16)
                pairs = [(keys[...], values[...])]
                pairs += [(block[:, :head], block[:, head:]) for block in far]
                scores = [
                    lax.dot_general(
                        query, key, (((1,), (1,)), ((), ())), preferred_element_type=jnp.float32
                    )
                    for key, _ in pairs
                ]
                scores[0] = jnp.where(visible, scores[0], masked_score)
                peak = jnp.max(scores[0], axis=1, keepdims=True)
                for block in scores[1:]:
                    peak = jnp.maximum(peak, jnp.max(block, axis=1, keepdims=True))
                length = jnp.zeros((rows, 1), jnp.float32)
                mixed = jnp.zeros((rows, head), jnp.float32)
                for block, (_, value) in zip(scores, pairs):
                    exps = jnp.exp2((block - peak) * power)
                    length = length + jnp.sum(exps, axis=1, keepdims=True)
                    mixed = mixed + jnp.dot(
                        exps.astype(jnp.bfloat16), value, preferred_element_type=jnp.float32
                    )
                out[:, at : at + head] = (mixed / length).astype(jnp.bfloat16)
                at += head

    @pl.when(slab < 2)
    def _():
        all_heads(())

    @pl.when(slab >= 2)
    def _():
        all_heads((across, corner))


def attention(sums, backs, skips, bias, cosine, sine_table, blocks, done=None):
    rows = sums[0].shape[0]
    width = sum(own.shape[1] - skip for own, skip in zip(sums, skips))
    head = cosine.shape[1]
    first = 0 if done is None else done.shape[1]
    inside = pl.BlockSpec(memory_space=pltpu.VMEM)
    args = [*sums, *backs, bias, cosine, sine_table, *blocks]
    if first:
        args.append(done)
    total = 4 * rows * rows * (width // head)
    return pl.pallas_call(
        functools.partial(attention_body, head ** (-0.5), first, skips),
        out_shape=jax.ShapeDtypeStruct((rows, first + width), jnp.bfloat16),
        in_specs=[inside] * len(args),
        out_specs=inside,
        scratch_shapes=[
            pltpu.VMEM((2 * rows, head), jnp.bfloat16),
            pltpu.VMEM((2 * rows, head), jnp.bfloat16),
        ],
        cost_estimate=pl.CostEstimate(
            flops=4 * total * head, bytes_accessed=8 * rows * width, transcendentals=total
        ),
        compiler_params=pltpu.CompilerParams(vmem_limit_bytes=12 * 2**20),
        name="attention",
    )(*args)


def planned(hidden, norm_gain, w_query, w_key, w_value, bias_query, bias_key, bias_value):
    tokens = hidden[0]
    rows = tokens.shape[0]
    depth = w_query.shape[0]
    head = w_key.shape[1]
    line, slab = (lax.axis_index("line"), lax.axis_index("ctx"))
    inner = (line == 1) | (line == 2)
    swap = [(0, 1), (1, 0)]
    ends = [(0, 1), (1, 0), (2, 3), (3, 2)]
    middle = [(1, 2), (2, 1)]
    outward = [(1, 0), (2, 3)]
    across = [(i, i ^ 2) for i in range(4)]
    beside = [(i, i ^ 1) for i in range(4)]
    held = lax.optimization_barrier
    cut = depth // 8
    parts_1 = ((0, 0, depth), (1, 0, 2 * cut))
    parts_2 = ((1, 2 * cut, 6 * cut), (2, 0, 6 * cut))
    parts_3 = ((2, 6 * cut, 2 * cut), (3, 0, depth))
    mine, sent_1 = pack(tokens, depth, (parts_1,), (w_key, w_value, w_query))
    kv_width = 2 * head
    half = kv_width + w_query.shape[1] // 2
    rest = mine.shape[1] - half
    second = lax.ppermute(mine, "line", ends)
    third_in = lax.ppermute(mine, "line", middle)
    came_1 = lax.ppermute(sent_1, "pair", swap)
    (sent_2,) = pack(tokens, depth, (parts_2,))
    gain = norm_gain.reshape(1, -1)
    bias_kv = jnp.concatenate([bias_key, bias_value]).reshape(1, -1).astype(jnp.float32)
    bias_q = bias_query.reshape(1, -1).astype(jnp.float32)
    positions = slab * rows + jnp.arange(rows, dtype=jnp.int32)
    cosine, sine_table = rotary_tables(positions, head)
    cosine = jnp.concatenate([cosine, cosine], axis=-1).reshape(rows, head)
    sine_table = jnp.concatenate([-sine_table, sine_table], axis=-1).reshape(rows, head)
    small = (gain, bias_kv, bias_q, cosine, sine_table)
    second, third_in, came_1, sent_2, small, later_tokens = held(
        (second, third_in, came_1, sent_2, small, tokens)
    )
    gain, bias_kv, bias_q, cosine, sine_table = small
    fourth_in = lax.ppermute(second, "line", middle)
    third_out = lax.ppermute(third_in, "line", outward)
    second_far = lax.ppermute(second, "ctx", across)
    came_2 = lax.ppermute(sent_2, "pair", swap)
    second_side = lax.ppermute(second, "ctx", beside)
    sent_3, scale, line_scale = prepare(later_tokens, depth, (parts_3,))
    came_scale = lax.ppermute(line_scale, "pair", swap)
    third = jnp.where(inner, third_in, third_out)
    fourth_in, came_scale, third, second_far, came_2, second_side, sent_3, scale = held(
        (fourth_in, came_scale, third, second_far, came_2, second_side, sent_3, scale)
    )
    fourth_out = lax.ppermute(fourth_in, "line", outward)
    third_far = lax.ppermute(third, "ctx", across)
    came_3 = lax.ppermute(sent_3, "pair", swap)
    second_corner = lax.ppermute(second_far, "ctx", beside)
    third_side = lax.ppermute(third, "ctx", beside)
    before = early_slots(
        (0, 1),
        ((0, 0, 10 * cut), (1, 0, 6 * cut)),
        True,
        False,
        tokens,
        (came_1, came_2),
        scale,
        came_scale,
        gain,
        [w_key, w_value, w_query, second, second_far, second_side, second_corner],
    )[0]
    fourth = jnp.where(inner, fourth_in, fourth_out)
    fourth, third_far, came_3, third_side, before = held(
        (fourth, third_far, came_3, third_side, before)
    )
    fourth_far_1 = lax.ppermute(fourth[:, :half], "ctx", across)
    third_corner = lax.ppermute(third_far, "ctx", beside)
    fourth_side = lax.ppermute(fourth, "ctx", beside)
    before, last_rows = early_slots(
        (2, 3),
        ((0, 6 * cut, 6 * cut), (1, 0, 10 * cut)),
        False,
        True,
        tokens,
        (came_2, came_3),
        scale,
        came_scale,
        gain,
        [third, third_far, third_side, third_corner],
        before,
    )
    fourth_far_1, fourth, before, last_rows, fourth_side = held(
        (fourth_far_1, fourth, before, last_rows, fourth_side)
    )
    fourth_far_2 = lax.ppermute(fourth[:, half:], "ctx", across)
    fourth_corner_1 = lax.ppermute(fourth_far_1, "ctx", beside)
    early_width = kv_width
    sums_0, sums_1, back_0, back_1 = late_slot(
        0,
        (early_width, half - early_width),
        before,
        last_rows,
        (fourth, fourth_far_1, fourth_side, fourth_corner_1),
    )
    back_0 = lax.ppermute(back_0, "pair", swap)
    back_1 = lax.ppermute(back_1, "pair", swap)
    back_0, fourth_far_2 = held((back_0, fourth_far_2))
    fourth_corner_2 = lax.ppermute(fourth_far_2, "ctx", beside)
    sums_2, back_2 = late_slot(
        half,
        (rest,),
        before,
        last_rows,
        (fourth, fourth_far_2, fourth_side, fourth_corner_2),
    )
    back_2 = lax.ppermute(back_2, "pair", swap)

    inside = pl.BlockSpec(memory_space=pltpu.VMEM)
    key_value = pl.pallas_call(
        key_value_body,
        out_shape=jax.ShapeDtypeStruct((rows, kv_width), jnp.bfloat16),
        in_specs=[inside] * 5,
        out_specs=inside,
        compiler_params=pltpu.CompilerParams(vmem_limit_bytes=4 * 2**20),
        name="key_value",
    )(sums_0, back_0, bias_kv, cosine, sine_table)
    kv_across = lax.ppermute(key_value, "ctx", [(0, 2), (1, 3)])
    kv_beside = lax.ppermute(key_value, "ctx", beside)
    kv_corner = lax.ppermute(kv_across, "ctx", [(2, 3), (3, 2)])
    blocks = (key_value, kv_beside, kv_across, kv_corner)
    tables = (bias_q, cosine, sine_table, blocks)
    attended = attention((sums_0, sums_1), (back_0, back_1), (kv_width, 0), *tables)
    attended = attention((sums_2,), (back_2,), (0,), *tables, attended)
    return attended[None]


def shards(hidden, norm_gain, w_query, w_key, w_value, bias_query, bias_key, bias_value):
    if lax.axis_size("line") == 4 and lax.axis_size("ctx") == 4:
        return planned(
            hidden, norm_gain, w_query, w_key, w_value, bias_query, bias_key, bias_value
        )
    local_rows = hidden.shape[1]
    head_width = w_key.shape[1]
    query_width = w_query.shape[1]
    query_heads = query_width // head_width
    sums = project(hidden[0], norm_gain, w_query, w_key, w_value)
    query_sums = sums[:, :query_width]
    key_sums = sums[:, query_width : query_width + head_width]
    value_sums = sums[:, query_width + head_width :]
    slab_index = lax.axis_index("ctx")
    slab_count = lax.axis_size("ctx")
    positions = slab_index * local_rows + jnp.arange(local_rows, dtype=jnp.int32)
    cosine, sine_table = rotary_tables(positions, head_width)
    queries = rotate(
        (query_sums + bias_query.astype(jnp.float32)).reshape(local_rows, query_heads, head_width),
        cosine,
        sine_table,
    ).astype(jnp.bfloat16)
    keys = rotate((key_sums + bias_key.astype(jnp.float32))[:, None, :], cosine, sine_table)[
        :, 0, :
    ].astype(jnp.bfloat16)
    values = (value_sums + bias_value.astype(jnp.float32)).astype(jnp.bfloat16)
    score_scale = head_width ** (-0.5)
    start_state = (
        jnp.full((query_heads, local_rows), masked_score, jnp.float32),
        jnp.zeros((query_heads, local_rows), jnp.float32),
        jnp.zeros((query_heads, local_rows, head_width), jnp.float32),
    )
    key_value = jnp.stack([keys, values])
    column_ids = jnp.arange(local_rows, dtype=jnp.int32)
    causal = column_ids[None, :] <= column_ids[:, None]
    running = attend(queries, score_scale, start_state, key_value, causal[None])

    def forward_step(step_number, state):
        held_running, blocks = state
        blocks = shifted(blocks, "ctx", 1)
        visible = step_number <= slab_index
        held_running = attend(queries, score_scale, held_running, blocks, visible)
        return (held_running, blocks)

    running, key_value = lax.fori_loop(1, slab_count, forward_step, (running, key_value))
    row_peak, row_total, weighted = running
    attended = (
        (weighted / row_total[..., None])
        .transpose(1, 0, 2)
        .reshape(local_rows, query_width)
        .astype(jnp.bfloat16)
    )
    return attended[None]


def solution(mesh):
    groups, slabs = (mesh.shape["fsdp"], mesh.shape["ctx"])
    pairs = Mesh(mesh.devices.reshape(groups // 2, 2, slabs), ("line", "pair", "ctx"))
    both = ("line", "pair")
    in_specs = (
        P(both, "ctx", None),
        P(),
        P(both, None),
        P(both, None),
        P(both, None),
        P(),
        P(),
        P(),
    )
    out_specs = P(both, "ctx", None)
    return jax.shard_map(shards, mesh=pairs, in_specs=in_specs, out_specs=out_specs, check_vma=False)
```

```python
import functools
import math

import jax
import jax.numpy as jnp
from jax import lax
from jax.experimental import pallas as pl
from jax.experimental.pallas import tpu as pltpu
from jax.sharding import Mesh, PartitionSpec as P

epsilon = 1e-06
rotary_base = 1000000.0
masked_score = -1e30


def shifted(value, axis, steps):
    count = lax.axis_size(axis)
    first, last = (max(0, -steps), min(count, count - steps))
    return lax.ppermute(value, axis, [(source, source + steps) for source in range(first, last)])


def rotary_tables(positions, head_width):
    half_width = head_width // 2
    frequency = jnp.exp(
        -(jnp.arange(half_width, dtype=jnp.float32) * (2.0 / head_width)) * math.log(rotary_base)
    )
    angles = positions.astype(jnp.float32)[:, None] * frequency[None, :]
    return (jnp.cos(angles)[:, None, :], jnp.sin(angles)[:, None, :])


def rotate(tensor, cosine, sine_table):
    half_width = tensor.shape[-1] // 2
    lower_half = tensor[..., :half_width]
    upper_half = tensor[..., half_width:]
    return jnp.concatenate(
        [
            lower_half * cosine - upper_half * sine_table,
            upper_half * cosine + lower_half * sine_table,
        ],
        axis=-1,
    )


def attend(work_queries, score_scale, running, key_value, visible):
    row_peak, row_total, weighted = running
    scores = (
        jnp.einsum("qhd,kd->hqk", work_queries, key_value[0], preferred_element_type=jnp.float32)
        * score_scale
    )
    scores = jnp.where(visible, scores, masked_score)
    new_peak = jnp.maximum(row_peak, jnp.max(scores, axis=-1))
    factor = jnp.exp(row_peak - new_peak)
    expsum = jnp.exp(scores - new_peak[..., None])
    row_total = row_total * factor + jnp.sum(expsum, axis=-1)
    weights = expsum.astype(jnp.bfloat16)
    weighted = weighted * factor[..., None] + jnp.einsum(
        "hqk,kd->hqd", weights, key_value[1], preferred_element_type=jnp.float32
    )
    return (new_peak, row_total, weighted)


def row_scale(inputs):
    floats = inputs.astype(jnp.float32)
    return lax.rsqrt(jnp.mean(floats * floats, axis=-1, keepdims=True) + epsilon)


def scaled_rows(inputs, scale, gain):
    return (inputs.astype(jnp.float32) * scale * gain.astype(jnp.float32)).astype(jnp.bfloat16)


def project(hidden, norm_gain, w_query, w_key, w_value):
    local_rows, width = hidden.shape
    lines, slabs = (lax.axis_size("line"), lax.axis_size("ctx"))
    depth = w_query.shape[0]
    side = lax.axis_index("pair")
    swap = [(0, 1), (1, 0)]
    split = hidden.reshape(local_rows, lines, 2, depth)
    half_width = lines * depth

    def half(array, which):
        return lax.dynamic_index_in_dim(array, which, array.ndim - 2, keepdims=False)

    sent = half(split, 1 - side).reshape(local_rows, half_width)
    kept = half(split, side).reshape(local_rows, half_width)
    gain = half(norm_gain.reshape(lines, 2, depth), side).reshape(half_width)
    came = lax.ppermute(sent, "pair", swap)
    scale = row_scale(hidden)
    came_scale = lax.ppermute(scale, "pair", swap)
    piece = depth // slabs
    start = lax.axis_index("ctx") * piece
    packed = jnp.concatenate(
        [lax.dynamic_slice_in_dim(w, start, piece, 0) for w in (w_query, w_key, w_value)], axis=1
    )
    weights = lax.all_gather(packed, ("line", "ctx"), axis=0, tiled=True)
    rows = jnp.concatenate(
        [scaled_rows(kept, scale, gain), scaled_rows(came, came_scale, gain)], axis=0
    )
    sums = jnp.dot(rows, weights, preferred_element_type=jnp.float32)
    back = lax.ppermute(sums[local_rows:].astype(jnp.bfloat16), "pair", swap)
    return sums[:local_rows] + back.astype(jnp.float32)


def normed_rows(block, scale, gain):
    return (block.astype(jnp.float32) * scale * gain).astype(jnp.bfloat16)


def slot_lines():
    line = lax.axis_index("line")
    inner = (line == 1) | (line == 2)
    third = jnp.where(inner, line ^ 3, line ^ 2)
    fourth = jnp.where(inner, line ^ 2, line ^ 3)
    return [line, line ^ 1, third, fourth]


def started(copies, sems, first):
    flights = [
        pltpu.make_async_copy(source, target, sems.at[first + number])
        for number, (source, target) in enumerate(copies)
    ]
    for flight in flights:
        flight.start()
    return flights


def piece_copies(pieces, wide, slab):
    piece = pieces[0].shape[0]
    return [
        (source, wide.at[pl.ds(pl.multiple_of(jnp.bitwise_xor(slab, flip) * piece, piece), piece), :])
        for source, flip in zip(pieces, (0, 2, 1, 3))
    ]


def pack_body(sent_parts, weights, depth, *refs):
    tokens, refs = (refs[0], refs[1:])
    sources, refs = (refs[:weights], refs[weights:])
    sems = refs[-1]
    copies = []
    outs = refs[:-1]
    if weights:
        mine, outs = (outs[0], outs[1:])
        piece = mine.shape[0]
        row = pl.multiple_of(lax.axis_index("ctx") * piece, piece)
        at = 0
        for source in sources:
            target = mine.at[:, pl.ds(at, source.shape[1])]
            copies.append((source.at[pl.ds(row, piece), :], target))
            at += source.shape[1]
    lines = slot_lines()
    other = 1 - lax.axis_index("pair")
    for out, parts in zip(outs, sent_parts):
        at = 0
        for slot, first, count in parts:
            column = pl.multiple_of((2 * lines[slot] + other) * depth + first, 128)
            copies.append((tokens.at[:, pl.ds(column, count)], out.at[:, pl.ds(at, count)]))
            at += count
    for flight in started(copies, sems, 0):
        flight.wait()


def pack(tokens, depth, sent_parts, weights=()):
    rows = tokens.shape[0]
    outside = pl.BlockSpec(memory_space=pltpu.HBM)
    outs = []
    if weights:
        piece = weights[0].shape[0] // 4
        outs.append(jax.ShapeDtypeStruct((piece, sum(w.shape[1] for w in weights)), jnp.bfloat16))
    for parts in sent_parts:
        outs.append(jax.ShapeDtypeStruct((rows, sum(p[2] for p in parts)), jnp.bfloat16))
    copies = len(weights) + sum(len(parts) for parts in sent_parts)
    moved = 4 * sum(out.shape[0] * out.shape[1] for out in outs)
    return pl.pallas_call(
        functools.partial(pack_body, sent_parts, len(weights), depth),
        out_shape=outs,
        in_specs=[outside] * (1 + len(weights)),
        out_specs=[pl.BlockSpec(memory_space=pltpu.VMEM)] * len(outs),
        scratch_shapes=[pltpu.SemaphoreType.DMA((copies,))],
        cost_estimate=pl.CostEstimate(flops=0, bytes_accessed=0, transcendentals=0),
        name="pack",
    )(tokens, *weights)


def prepare_body(sent_parts, depth, tokens, *refs):
    outs, refs = (refs[: len(sent_parts)], refs[len(sent_parts) :])
    column_scale, line_scale, held, sems = refs
    rows, width = held.shape
    lines = slot_lines()
    other = 1 - lax.axis_index("pair")
    loads = [
        (tokens.at[:, pl.ds(at, depth)], held.at[:, pl.ds(at, depth)])
        for at in range(0, width, depth)
    ]
    loads = started(loads, sems, 0)
    copies = []
    for out, parts in zip(outs, sent_parts):
        at = 0
        for slot, first, count in parts:
            column = pl.multiple_of((2 * lines[slot] + other) * depth + first, 128)
            copies.append((tokens.at[:, pl.ds(column, count)], out.at[:, pl.ds(at, count)]))
            at += count
    copies = started(copies, sems, len(loads))
    squares = jnp.zeros((rows, 128), jnp.float32)
    for number, load in enumerate(loads):
        load.wait()
        for at in range(number * depth, (number + 1) * depth, 128):
            floats = held[:, at : at + 128].astype(jnp.float32)
            squares = squares + floats * floats
    mean = jnp.sum(squares, axis=1, keepdims=True) / width
    wide = jnp.broadcast_to(lax.rsqrt(mean + epsilon), (rows, 128))
    column_scale[...] = wide
    line_scale[...] = jnp.transpose(wide)[:1]
    for copy in copies:
        copy.wait()


def prepare(tokens, depth, sent_parts):
    rows, width = tokens.shape
    outs = [
        jax.ShapeDtypeStruct((rows, sum(p[2] for p in parts)), jnp.bfloat16)
        for parts in sent_parts
    ]
    outs.append(jax.ShapeDtypeStruct((rows, 128), jnp.float32))
    outs.append(jax.ShapeDtypeStruct((1, rows), jnp.float32))
    copies = width // depth + sum(len(parts) for parts in sent_parts)
    return pl.pallas_call(
        functools.partial(prepare_body, sent_parts, depth),
        out_shape=outs,
        in_specs=[pl.BlockSpec(memory_space=pltpu.HBM)],
        out_specs=[pl.BlockSpec(memory_space=pltpu.VMEM)] * len(outs),
        scratch_shapes=[
            pltpu.VMEM((rows, width), jnp.bfloat16),
            pltpu.SemaphoreType.DMA((copies,)),
        ],
        cost_estimate=pl.CostEstimate(flops=0, bytes_accessed=0, transcendentals=0),
        compiler_params=pltpu.CompilerParams(vmem_limit_bytes=10 * 2**20),
        name="prepare",
    )(tokens)


def early_body(slots, guests, local, final, hidden, *refs):
    count = 1 + max(part[0] for part in guests)
    cames, refs = (refs[:count], refs[count:])
    scale, came_scale, gain, *refs = refs
    summed = slots[:-1] if final else slots
    number = 3 * local + 4 * (len(summed) - local)
    weights, refs = (refs[:number], refs[number:])
    before = None
    if not local:
        before, *refs = refs
    total, *refs = refs
    if final:
        last_rows, *refs = refs
    held, guest, wide, stacked, sems = refs
    _, rows, depth = held.shape
    slab = lax.axis_index("ctx")
    blocks = [2 * which + lax.axis_index("pair") for which in slot_lines()]
    number = 0
    parts = []
    at = 0
    for source, first, width in guests:
        parts.append(
            (cames[source].at[:, pl.ds(first, width)], guest.at[:, pl.ds(at, width)])
        )
        at += width
    guest_flights = started(parts, sems, number)
    number += len(parts)
    flights = []
    pending = list(weights)
    for place, slot in enumerate(slots):
        column = pl.multiple_of(blocks[slot] * depth, depth)
        copies = [(hidden.at[:, pl.ds(column, depth)], held.at[place])]
        if slot == 0:
            at = 0
            for _ in range(3):
                weight = pending.pop(0)
                copies.append((weight, wide.at[place, :, pl.ds(at, weight.shape[1])]))
                at += weight.shape[1]
        elif slot in summed:
            copies += piece_copies(pending[:4], wide.at[place], slab)
            pending = pending[4:]
        flights.append(started(copies, sems, number))
        number += len(copies)
    turned_scale = jnp.transpose(jnp.broadcast_to(came_scale[...], (128, rows)))[:, :1]
    for flight in guest_flights:
        flight.wait()
    width = total.shape[1]
    step = 256
    for place, slot in enumerate(slots):
        for flight in flights[place]:
            flight.wait()
        column = pl.multiple_of(blocks[slot] * depth, depth)
        row_gain = gain[:, pl.ds(column, depth)].astype(jnp.float32)
        target = stacked.at[place] if slot in summed else last_rows
        target[:rows] = normed_rows(held[place], scale[:, :1], row_gain)
        target[rows:] = normed_rows(
            guest[:, place * depth : (place + 1) * depth], turned_scale, row_gain
        )
        if slot not in summed:
            continue
        for at in range(0, width, step):
            cols = pl.ds(at, step)
            product = jnp.dot(
                stacked[place], wide[place, :, cols], preferred_element_type=jnp.float32
            )
            if place > 0:
                product = product + total[:, cols]
            elif before is not None:
                product = product + before[:, cols]
            total[:, cols] = product


def early_slots(
    slots, guests, local, final, hidden, cames, scale, came_scale, gain, weights, before=None
):
    rows = hidden.shape[0]
    depth = weights[0].shape[0] if local else 4 * weights[0].shape[0]
    width = sum(w.shape[1] for w in weights[:3]) if local else weights[0].shape[1]
    outside = pl.BlockSpec(memory_space=pltpu.HBM)
    anywhere = pl.BlockSpec(memory_space=pl.ANY)
    inside = pl.BlockSpec(memory_space=pltpu.VMEM)
    summed = len(slots) - final
    flops = 4 * rows * depth * summed * width
    moved = 2 * (depth * width * summed + 2 * rows * depth * len(slots)) + 8 * rows * width
    outs = [jax.ShapeDtypeStruct((2 * rows, width), jnp.float32)]
    if final:
        outs.append(jax.ShapeDtypeStruct((2 * rows, depth), jnp.bfloat16))
    args = [hidden, *cames, scale, came_scale, gain, *weights]
    in_specs = [outside] + [anywhere] * len(cames)
    in_specs += [inside] * 3 + [outside] * (3 * local) + [anywhere] * (len(weights) - 3 * local)
    if before is not None:
        args.append(before)
        in_specs.append(inside)
    return pl.pallas_call(
        functools.partial(early_body, slots, guests, local, final),
        out_shape=outs,
        in_specs=in_specs,
        out_specs=[inside] * len(outs),
        scratch_shapes=[
            pltpu.VMEM((len(slots), rows, depth), jnp.bfloat16),
            pltpu.VMEM((rows, len(slots) * depth), jnp.bfloat16),
            pltpu.VMEM((summed, depth, width), jnp.bfloat16),
            pltpu.VMEM((summed, 2 * rows, depth), jnp.bfloat16),
            pltpu.SemaphoreType.DMA((len(guests) + len(slots) + len(weights),)),
        ],
        cost_estimate=pl.CostEstimate(flops=flops, bytes_accessed=moved, transcendentals=0),
        compiler_params=pltpu.CompilerParams(vmem_limit_bytes=24 * 2**20),
        name="early_slots",
    )(*args)


def late_body(first, splits, before, last_rows, *refs):
    pieces, refs = (refs[:4], refs[4:])
    kept, sent = (refs[: len(splits)], refs[len(splits) : 2 * len(splits)])
    wide, sems = refs[2 * len(splits) :]
    rows, width = (kept[0].shape[0], wide.shape[1])
    pieces = [p if p.shape[1] == width else p.at[:, pl.ds(first, width)] for p in pieces]
    for flight in started(piece_copies(pieces, wide, lax.axis_index("ctx")), sems, 0):
        flight.wait()
    at = 0
    for own, other, columns in zip(kept, sent, splits):
        cols = slice(at, at + columns)
        product = jnp.dot(last_rows[...], wide[:, cols], preferred_element_type=jnp.float32)
        product = product + before[:, first + at : first + at + columns]
        own[...] = product[:rows]
        other[...] = product[rows:].astype(jnp.bfloat16)
        at += columns


def late_slot(first, splits, before, last_rows, pieces):
    rows, depth = (last_rows.shape[0] // 2, last_rows.shape[1])
    anywhere = pl.BlockSpec(memory_space=pl.ANY)
    inside = pl.BlockSpec(memory_space=pltpu.VMEM)
    width = sum(splits)
    outs = [jax.ShapeDtypeStruct((rows, w), jnp.float32) for w in splits]
    outs += [jax.ShapeDtypeStruct((rows, w), jnp.bfloat16) for w in splits]
    return pl.pallas_call(
        functools.partial(late_body, first, splits),
        out_shape=outs,
        in_specs=[inside] * 2 + [anywhere] * 4,
        out_specs=[inside] * len(outs),
        scratch_shapes=[
            pltpu.VMEM((depth, width), jnp.bfloat16),
            pltpu.SemaphoreType.DMA((4,)),
        ],
        cost_estimate=pl.CostEstimate(
            flops=4 * rows * depth * width, bytes_accessed=2 * depth * width, transcendentals=0
        ),
        compiler_params=pltpu.CompilerParams(vmem_limit_bytes=10 * 2**20),
        name="late_slot",
    )(before, last_rows, *pieces)


def turned(tensor, cosine, sine_table):
    half = tensor.shape[-1] // 2
    return tensor * cosine + pltpu.roll(tensor, half, 1) * sine_table


def key_value_body(sums, back, bias, cosine, sine_table, out):
    head = out.shape[1] // 2
    total = sums[:, : 2 * head] + back[:, : 2 * head].astype(jnp.float32) + bias[...]
    out[:, :head] = turned(total[:, :head], cosine[...], sine_table[...]).astype(jnp.bfloat16)
    out[:, head:] = total[:, head:].astype(jnp.bfloat16)


def attention_body(scale, first, skips, *refs):
    groups = len(skips)
    sums, refs = (refs[:groups], refs[groups:])
    backs, refs = (refs[:groups], refs[groups:])
    bias, cosine, sine_table, *refs = refs
    blocks, refs = (refs[:4], refs[4:])
    if first:
        done, *refs = refs
    out, keys, values, held, sems = refs
    spare = out.shape[1] // cosine.shape[1]
    rows = out.shape[0]
    head = cosine.shape[1]
    slab = lax.axis_index("ctx")
    odd = lax.rem(slab, 2)
    own_block, beside, across, corner = blocks
    for block, place in ((own_block, odd), (beside, 1 - odd)):
        row = pl.multiple_of(place * rows, rows)
        keys[pl.ds(row, rows), :] = block[:, :head]
        values[pl.ds(row, rows), :] = block[:, head:]
    near = (rows, keys.shape[0])
    row_ids = odd * rows + lax.broadcasted_iota(jnp.int32, near, 0)
    visible = lax.broadcasted_iota(jnp.int32, near, 1) <= row_ids
    power = scale * math.log2(math.e)

    def all_heads(far):
        at = first
        flights = []
        if first:
            flights += started([(done, out.at[:, pl.ds(0, first)])], sems, spare)
        for own, other, skip in zip(sums, backs, skips):
            for column in range(skip, own.shape[1], head):
                cols = slice(column, column + head)
                query = own[:, cols] + other[:, cols].astype(jnp.float32) + bias[:, at : at + head]
                query = turned(query, cosine[...], sine_table[...]).astype(jnp.bfloat16)
                pairs = [(keys[...], values[...])]
                pairs += [(block[:, :head], block[:, head:]) for block in far]
                scores = [
                    lax.dot_general(
                        query, key, (((1,), (1,)), ((), ())), preferred_element_type=jnp.float32
                    )
                    for key, _ in pairs
                ]
                scores[0] = jnp.where(visible, scores[0], masked_score)
                peak = jnp.max(scores[0], axis=1, keepdims=True)
                for block in scores[1:]:
                    peak = jnp.maximum(peak, jnp.max(block, axis=1, keepdims=True))
                length = jnp.zeros((rows, 1), jnp.float32)
                mixed = jnp.zeros((rows, head), jnp.float32)
                for block, (_, value) in zip(scores, pairs):
                    exps = jnp.exp2((block - peak) * power)
                    length = length + jnp.sum(exps, axis=1, keepdims=True)
                    mixed = mixed + jnp.dot(
                        exps.astype(jnp.bfloat16), value, preferred_element_type=jnp.float32
                    )
                result = (mixed / length).astype(jnp.bfloat16)
                if first:
                    part = held.at[:, pl.ds(at - first, head)]
                    part[...] = result
                    flights += started([(part, out.at[:, pl.ds(at, head)])], sems, at // head)
                else:
                    out[:, at : at + head] = result
                at += head
        for flight in flights:
            flight.wait()

    @pl.when(slab < 2)
    def _():
        all_heads(())

    @pl.when(slab >= 2)
    def _():
        all_heads((across, corner))


def attention(first, sums, backs, skips, bias, cosine, sine_table, blocks, done=None):
    rows = sums[0].shape[0]
    width = sum(own.shape[1] - skip for own, skip in zip(sums, skips))
    head = cosine.shape[1]
    inside = pl.BlockSpec(memory_space=pltpu.VMEM)
    args = [*sums, *backs, bias, cosine, sine_table, *blocks]
    in_specs = [inside] * len(args)
    if first:
        args.append(done)
        in_specs.append(inside)
    total = 4 * rows * rows * (width // head)
    return pl.pallas_call(
        functools.partial(attention_body, head ** (-0.5), first, skips),
        out_shape=jax.ShapeDtypeStruct((rows, first + width), jnp.bfloat16),
        in_specs=in_specs,
        out_specs=pl.BlockSpec(memory_space=pl.ANY) if first else inside,
        scratch_shapes=[
            pltpu.VMEM((2 * rows, head), jnp.bfloat16),
            pltpu.VMEM((2 * rows, head), jnp.bfloat16),
            pltpu.VMEM((rows, width), jnp.bfloat16),
            pltpu.SemaphoreType.DMA(((first + width) // head + 1,)),
        ],
        cost_estimate=pl.CostEstimate(
            flops=4 * total * head, bytes_accessed=8 * rows * width, transcendentals=total
        ),
        compiler_params=pltpu.CompilerParams(vmem_limit_bytes=12 * 2**20),
        name="attention",
    )(*args)


def planned(hidden, norm_gain, w_query, w_key, w_value, bias_query, bias_key, bias_value):
    tokens = hidden[0]
    rows = tokens.shape[0]
    depth = w_query.shape[0]
    head = w_key.shape[1]
    line, slab = (lax.axis_index("line"), lax.axis_index("ctx"))
    inner = (line == 1) | (line == 2)
    swap = [(0, 1), (1, 0)]
    ends = [(0, 1), (1, 0), (2, 3), (3, 2)]
    middle = [(1, 2), (2, 1)]
    outward = [(1, 0), (2, 3)]
    across = [(i, i ^ 2) for i in range(4)]
    beside = [(i, i ^ 1) for i in range(4)]
    held = lax.optimization_barrier
    cut = depth // 8
    parts_1 = ((0, 0, depth), (1, 0, 2 * cut))
    parts_2 = ((1, 2 * cut, 6 * cut), (2, 0, 6 * cut))
    parts_3 = ((2, 6 * cut, 2 * cut), (3, 0, depth))
    mine, sent_1 = pack(tokens, depth, (parts_1,), (w_key, w_value, w_query))
    kv_width = 2 * head
    half = kv_width + w_query.shape[1] // 2
    rest = mine.shape[1] - half
    second = lax.ppermute(mine, "line", ends)
    third_in = lax.ppermute(mine, "line", middle)
    came_1 = lax.ppermute(sent_1, "pair", swap)
    (sent_2,) = pack(tokens, depth, (parts_2,))
    gain = norm_gain.reshape(1, -1)
    bias_kv = jnp.concatenate([bias_key, bias_value]).reshape(1, -1).astype(jnp.float32)
    bias_q = bias_query.reshape(1, -1).astype(jnp.float32)
    positions = slab * rows + jnp.arange(rows, dtype=jnp.int32)
    cosine, sine_table = rotary_tables(positions, head)
    cosine = jnp.concatenate([cosine, cosine], axis=-1).reshape(rows, head)
    sine_table = jnp.concatenate([-sine_table, sine_table], axis=-1).reshape(rows, head)
    small = (gain, bias_kv, bias_q, cosine, sine_table)
    second, third_in, came_1, sent_2, small, later_tokens = held(
        (second, third_in, came_1, sent_2, small, tokens)
    )
    gain, bias_kv, bias_q, cosine, sine_table = small
    fourth_in = lax.ppermute(second, "line", middle)
    third_out = lax.ppermute(third_in, "line", outward)
    second_far = lax.ppermute(second, "ctx", across)
    came_2 = lax.ppermute(sent_2, "pair", swap)
    second_side = lax.ppermute(second, "ctx", beside)
    sent_3, scale, line_scale = prepare(later_tokens, depth, (parts_3,))
    came_scale = lax.ppermute(line_scale, "pair", swap)
    third = jnp.where(inner, third_in, third_out)
    fourth_in, came_scale, third, second_far, came_2, second_side, sent_3, scale = held(
        (fourth_in, came_scale, third, second_far, came_2, second_side, sent_3, scale)
    )
    fourth_out = lax.ppermute(fourth_in, "line", outward)
    third_far = lax.ppermute(third, "ctx", across)
    came_3 = lax.ppermute(sent_3, "pair", swap)
    second_corner = lax.ppermute(second_far, "ctx", beside)
    third_side = lax.ppermute(third, "ctx", beside)
    before = early_slots(
        (0, 1),
        ((0, 0, 10 * cut), (1, 0, 6 * cut)),
        True,
        False,
        tokens,
        (came_1, came_2),
        scale,
        came_scale,
        gain,
        [w_key, w_value, w_query, second, second_far, second_side, second_corner],
    )[0]
    fourth = jnp.where(inner, fourth_in, fourth_out)
    fourth, third_far, came_3, third_side, before = held(
        (fourth, third_far, came_3, third_side, before)
    )
    fourth_far_1 = lax.ppermute(fourth[:, :half], "ctx", across)
    third_corner = lax.ppermute(third_far, "ctx", beside)
    fourth_side = lax.ppermute(fourth, "ctx", beside)
    before, last_rows = early_slots(
        (2, 3),
        ((0, 6 * cut, 6 * cut), (1, 0, 10 * cut)),
        False,
        True,
        tokens,
        (came_2, came_3),
        scale,
        came_scale,
        gain,
        [third, third_far, third_side, third_corner],
        before,
    )
    fourth_far_1, fourth, before, last_rows, fourth_side = held(
        (fourth_far_1, fourth, before, last_rows, fourth_side)
    )
    fourth_far_2 = lax.ppermute(fourth[:, half:], "ctx", across)
    fourth_corner_1 = lax.ppermute(fourth_far_1, "ctx", beside)
    early_width = kv_width
    sums_0, sums_1, back_0, back_1 = late_slot(
        0,
        (early_width, half - early_width),
        before,
        last_rows,
        (fourth, fourth_far_1, fourth_side, fourth_corner_1),
    )
    back_0 = lax.ppermute(back_0, "pair", swap)
    back_1 = lax.ppermute(back_1, "pair", swap)
    back_0, fourth_far_2 = held((back_0, fourth_far_2))
    fourth_corner_2 = lax.ppermute(fourth_far_2, "ctx", beside)
    sums_2, back_2 = late_slot(
        half,
        (rest,),
        before,
        last_rows,
        (fourth, fourth_far_2, fourth_side, fourth_corner_2),
    )
    back_2 = lax.ppermute(back_2, "pair", swap)

    inside = pl.BlockSpec(memory_space=pltpu.VMEM)
    key_value = pl.pallas_call(
        key_value_body,
        out_shape=jax.ShapeDtypeStruct((rows, kv_width), jnp.bfloat16),
        in_specs=[inside] * 5,
        out_specs=inside,
        compiler_params=pltpu.CompilerParams(vmem_limit_bytes=4 * 2**20),
        name="key_value",
    )(sums_0, back_0, bias_kv, cosine, sine_table)
    kv_across = lax.ppermute(key_value, "ctx", [(0, 2), (1, 3)])
    kv_beside = lax.ppermute(key_value, "ctx", beside)
    kv_corner = lax.ppermute(kv_across, "ctx", [(2, 3), (3, 2)])
    blocks = (key_value, kv_beside, kv_across, kv_corner)
    tables = (bias_q, cosine, sine_table, blocks)
    attended = attention(0, (sums_0, sums_1), (back_0, back_1), (kv_width, 0), *tables)
    attended = attention(half - kv_width, (sums_2,), (back_2,), (0,), *tables, attended)
    return attended[None]


def shards(hidden, norm_gain, w_query, w_key, w_value, bias_query, bias_key, bias_value):
    if lax.axis_size("line") == 4 and lax.axis_size("ctx") == 4:
        return planned(
            hidden, norm_gain, w_query, w_key, w_value, bias_query, bias_key, bias_value
        )
    local_rows = hidden.shape[1]
    head_width = w_key.shape[1]
    query_width = w_query.shape[1]
    query_heads = query_width // head_width
    sums = project(hidden[0], norm_gain, w_query, w_key, w_value)
    query_sums = sums[:, :query_width]
    key_sums = sums[:, query_width : query_width + head_width]
    value_sums = sums[:, query_width + head_width :]
    slab_index = lax.axis_index("ctx")
    slab_count = lax.axis_size("ctx")
    positions = slab_index * local_rows + jnp.arange(local_rows, dtype=jnp.int32)
    cosine, sine_table = rotary_tables(positions, head_width)
    queries = rotate(
        (query_sums + bias_query.astype(jnp.float32)).reshape(local_rows, query_heads, head_width),
        cosine,
        sine_table,
    ).astype(jnp.bfloat16)
    keys = rotate((key_sums + bias_key.astype(jnp.float32))[:, None, :], cosine, sine_table)[
        :, 0, :
    ].astype(jnp.bfloat16)
    values = (value_sums + bias_value.astype(jnp.float32)).astype(jnp.bfloat16)
    score_scale = head_width ** (-0.5)
    start_state = (
        jnp.full((query_heads, local_rows), masked_score, jnp.float32),
        jnp.zeros((query_heads, local_rows), jnp.float32),
        jnp.zeros((query_heads, local_rows, head_width), jnp.float32),
    )
    key_value = jnp.stack([keys, values])
    column_ids = jnp.arange(local_rows, dtype=jnp.int32)
    causal = column_ids[None, :] <= column_ids[:, None]
    running = attend(queries, score_scale, start_state, key_value, causal[None])

    def forward_step(step_number, state):
        held_running, blocks = state
        blocks = shifted(blocks, "ctx", 1)
        visible = step_number <= slab_index
        held_running = attend(queries, score_scale, held_running, blocks, visible)
        return (held_running, blocks)

    running, key_value = lax.fori_loop(1, slab_count, forward_step, (running, key_value))
    row_peak, row_total, weighted = running
    attended = (
        (weighted / row_total[..., None])
        .transpose(1, 0, 2)
        .reshape(local_rows, query_width)
        .astype(jnp.bfloat16)
    )
    return attended[None]


def solution(mesh):
    groups, slabs = (mesh.shape["fsdp"], mesh.shape["ctx"])
    pairs = Mesh(mesh.devices.reshape(groups // 2, 2, slabs), ("line", "pair", "ctx"))
    both = ("line", "pair")
    in_specs = (
        P(both, "ctx", None),
        P(),
        P(both, None),
        P(both, None),
        P(both, None),
        P(),
        P(),
        P(),
    )
    out_specs = P(both, "ctx", None)
    return jax.shard_map(shards, mesh=pairs, in_specs=in_specs, out_specs=out_specs, check_vma=False)
```
